32 devices in a mesh: segment: 4 (over y, core), vol: 8 (over z, x).
Axes of the slice: x: 2, y: 2, z: 4, core: 2. Of those that a mesh axis runs over, the one named last changes fastest.
Arguments:
- cotangent: bfloat16 [64, 32, 256], P(None, 'vol'), may hold values from -6 to 6
- labels: int32 [32, 256], P('vol'), may hold values from 0 to 2
- class_weight: float32 [3], replicated, may hold values from 0.25 to 2
- inputs: bfloat16 [4, 64, 32, 256], P('segment', None, 'vol'), may hold values from -6 to 6
- fine_pre: bfloat16 [4, 64, 32, 256], P('segment', None, 'vol'), may hold values from -6 to 6
- pooled: bfloat16 [4, 64, 8, 128], P('segment', None, 'vol'), may hold values from -6 to 6
- coarse_pre: bfloat16 [4, 64, 8, 128], P('segment', None, 'vol'), may hold values from -6 to 6
- fine_filters: bfloat16 [4, 27, 64, 64], P('segment'), may hold values from -0.15625 to 0.15625
- coarse_filters: bfloat16 [4, 27, 64, 64], P('segment'), may hold values from -0.15625 to 0.15625
Outputs:
- input_grads: bfloat16 [4, 64, 32, 256], P('segment', None, 'vol')
- fine_filter_grads: float32 [4, 27, 64, 64], P('segment')
- coarse_filter_grads: float32 [4, 27, 64, 64], P('segment')
The draws below stay inside these ranges and needn't reach their ends.
Inputs may be any that keep to these rules, and one draw needn't show every extreme that they name: `labels`: 0 is background, 1 fault, 2 horizon.
All inputs are finite; a program needn't handle non-finite values.
Results may differ from the reference program's by a relative error of at most 0.02.
Values may be sent and summed in bfloat16 or wider, within the bound.
A program may use at most 64 MiB of HBM per device.

```python
import math
import jax
import jax.numpy as jnp
from jax import lax

C = 64
TAPS = 27
CLASSES = 3
XL = 16
SEGMENTS = 4
NDEP = 32
NI = 16
PLANE = 256
CROWS = 8
CPLANE = 128


def plant(entries, stream_key, least, largest):
    shape = entries.shape
    spot = [jax.random.randint(jax.random.fold_in(stream_key, axis), (), 0, shape[axis]) for axis in range(len(shape))]
    entries = entries.at[tuple(spot)].set(least)
    longest = shape.index(max(shape))
    spot[longest] = (spot[longest] + 1) % shape[longest]
    return entries.at[tuple(spot)].set(largest)


def steps_of(own_key, dims, cuts, least, top_value):
    factor_of, own = 1.0, jax.random.fold_in(own_key, 6)
    for axis_at, parts in cuts:
        draws = jnp.exp(jax.random.uniform(jax.random.fold_in(own, axis_at), (parts,), jnp.float32, least / len(cuts), top_value / len(cuts)))
        factor_of = factor_of * jnp.repeat(draws, dims[axis_at] // parts).reshape([-1 if axis == axis_at else 1 for axis in range(len(dims))])
    return factor_of


def noise(rng, dims, deviation, limit, cuts=(), kind=jnp.bfloat16):
    values = deviation * jax.random.normal(rng, dims, jnp.float32)
    if cuts:
        values = values * steps_of(rng, dims, cuts, -0.22, 0.18)
    return jnp.clip(values, -limit, limit).astype(kind)


def setup_inputs(seed: int = 0) -> dict:
    seeds = jax.random.split(jax.random.key(seed), 10)
    cotangent = noise(seeds[0], (C, NDEP, PLANE), 1.0, 6.0, ((1, 8),))
    labels = plant(jax.random.randint(seeds[1], (NDEP, PLANE), 0, 3), jax.random.fold_in(seeds[1], 1), 0, 2).astype(jnp.int32)
    class_weight = jnp.clip(jnp.exp(jax.random.uniform(seeds[2], (CLASSES,), jnp.float32, math.log(0.25), math.log(2.0))), 0.25, 2.0)
    inputs = noise(seeds[3], (SEGMENTS, C, NDEP, PLANE), 1.0, 6.0, ((0, 4), (2, 8)))
    fine_pre = noise(seeds[4], (SEGMENTS, C, NDEP, PLANE), 1.0, 6.0, ((0, 4), (2, 8)))
    pooled = noise(seeds[5], (SEGMENTS, C, CROWS, CPLANE), 1.0, 6.0, ((0, 4), (2, 8)))
    coarse_pre = noise(seeds[6], (SEGMENTS, C, CROWS, CPLANE), 1.0, 6.0, ((0, 4), (2, 8)))
    fine_filters = noise(seeds[7], (SEGMENTS, TAPS, C, C), (TAPS * C) ** -0.5, 0.15625, ((0, 4),))
    coarse_filters = noise(seeds[8], (SEGMENTS, TAPS, C, C), (TAPS * C) ** -0.5, 0.15625, ((0, 4),))
    return {"cotangent": cotangent, "labels": labels, "class_weight": class_weight, "inputs": inputs, "fine_pre": fine_pre, "pooled": pooled, "coarse_pre": coarse_pre, "fine_filters": fine_filters, "coarse_filters": coarse_filters}


def shift_volume(volume, depth_step, inline_step, cross_step):
    padded = jnp.pad(volume, ((0, 0), (1, 1), (1, 1), (1, 1)))
    depth_len, inline_len, cross_len = (volume.shape[1], volume.shape[2], volume.shape[3])
    return padded[:, 1 - depth_step:1 - depth_step + depth_len, 1 - inline_step:1 - inline_step + inline_len, 1 - cross_step:1 - cross_step + cross_len]

def conv_back(gradient, saved_input, weights):
    kernel = weights.astype(jnp.float32)
    grad_wide = gradient.astype(jnp.float32)
    saved_wide = saved_input.astype(jnp.float32)
    summed = jnp.zeros(grad_wide.shape, jnp.float32)
    filter_list = []
    for tap_index in range(27):
        shifted = shift_volume(grad_wide, tap_index // 9 - 1, tap_index // 3 % 3 - 1, tap_index % 3 - 1)
        summed = summed + jnp.einsum('io,oabc->iabc', kernel[tap_index], shifted, precision=lax.Precision.HIGHEST)
        filter_list.append(jnp.einsum('iabc,oabc->io', saved_wide, shifted, precision=lax.Precision.HIGHEST))
    return (summed, jnp.stack(filter_list))

def reference(cotangent, labels, class_weight, inputs, fine_pre, pooled, coarse_pre, fine_filters, coarse_filters):
    half_depth, half_inline, half_cross = (NDEP // 2, NI // 2, XL // 2)
    fine_scale = 1.0 / math.sqrt(NDEP * NI * XL)
    coarse_scale = 1.0 / math.sqrt(half_depth * half_inline * half_cross)
    cell_weight = class_weight[labels]
    gradient = (cotangent.astype(jnp.float32) * cell_weight[None]).astype(jnp.bfloat16).reshape(C, NDEP, NI, XL)
    grads_out = [None] * SEGMENTS
    fine_out = [None] * SEGMENTS
    coarse_out = [None] * SEGMENTS
    for segment_index in range(SEGMENTS - 1, -1, -1):
        saved_input = inputs[segment_index].reshape(C, NDEP, NI, XL)
        fine_gate = fine_pre[segment_index].reshape(C, NDEP, NI, XL)
        coarse_input = pooled[segment_index].reshape(C, half_inline, half_depth, half_cross).transpose(0, 2, 1, 3)
        coarse_gate = coarse_pre[segment_index].reshape(C, half_inline, half_depth, half_cross).transpose(0, 2, 1, 3)
        grad_wide = gradient.astype(jnp.float32)
        pooled_grad = grad_wide.reshape(C, half_depth, 2, half_inline, 2, half_cross, 2).sum(axis=(2, 4, 6)).astype(jnp.bfloat16)
        coarse_gz = jnp.where(coarse_gate > 0, pooled_grad, jnp.zeros_like(pooled_grad))
        coarse_back, coarse_filt = conv_back(coarse_gz, coarse_input, coarse_filters[segment_index])
        coarse_back = lax.optimization_barrier(coarse_back.astype(jnp.bfloat16)).astype(jnp.float32)
        spread = jnp.broadcast_to(coarse_back[:, :, None, :, None, :, None], (C, half_depth, 2, half_inline, 2, half_cross, 2)).reshape(C, NDEP, NI, XL)
        fine_grad = grad_wide + 0.125 * spread
        fine_gz = jnp.where(fine_gate > 0, fine_grad, jnp.zeros_like(fine_grad)).astype(jnp.bfloat16)
        fine_back, fine_filt = conv_back(fine_gz, saved_input, fine_filters[segment_index])
        gradient = (grad_wide + fine_back).astype(jnp.bfloat16)
        grads_out[segment_index] = gradient.reshape(C, NDEP, NI * XL)
        fine_out[segment_index] = fine_filt * fine_scale
        coarse_out[segment_index] = coarse_filt * coarse_scale
    return (jnp.stack(grads_out), jnp.stack(fine_out), jnp.stack(coarse_out))
```

```python
import functools
import math

import jax
import jax.numpy as jnp
from jax import lax
from jax.experimental import pallas as pl
from jax.experimental.pallas import tpu as pltpu
from jax.sharding import PartitionSpec as P

XL = 16
HX = XL // 2
TAPS = 27
OWNERS = 4
GROUP_LANES = 1024
MIB = 1024 * 1024
PICK_BYTES = 4 * MIB
BF = jnp.bfloat16
F32 = jnp.float32


def iota(shape, dim):
    return lax.broadcasted_iota(jnp.int32, shape, dim)


def matmul(a, b):
    return lax.dot_general(a, b, (((1,), (0,)), ((), ())), preferred_element_type=F32)


def matmul_nt(a, b):
    return lax.dot_general(a, b, (((1,), (1,)), ((), ())), preferred_element_type=F32)


def tap_mask(lanes, plane, columns, row_step, col_step):
    lane = iota((1, lanes), 1)
    column = lax.rem(lane, columns) - col_step
    row = lax.div(lax.rem(lane, plane), columns) - row_step
    rows = plane // columns
    inside = (column >= 0) & (column < columns) & (row >= 0) & (row < rows)
    return jnp.where(inside, 1.0, 0.0).astype(BF)


def rolled(value, shift):
    size = value.shape[1]
    shift = shift % size
    return value if shift == 0 else pltpu.roll(value, shift, 1)


STEPS = [(r, c) for r in (-1, 0, 1) for c in (-1, 0, 1)]


def kernel(
    sizes, scales,
    class_weight_h, cotangent_h, labels_h, saved_h, fine_pre_h, coarse_pre_h, pooled_h,
    fine_w_h, coarse_w_h,
    grad_out, fine_out, coarse_out,
    class_weight, cotangent, labels, saved, fine_pre, fine_w, coarse_w,
    out, seed, fine_cat, coarse_cat, pre_rows, pool_rows, pre_ext, x_ext, grad_ext, pool_ext,
    pool_out, coarse_gate, pick, pool_matrix, fine_x, pool_all, fine_cols, coarse_cols,
    full_cols, gz_all, parts, arrived, collected,
    load_sem, row_send, row_recv, halo_send, halo_recv, step_send, step_recv,
    sum_send, sum_recv, all_send, all_recv, gz_send, gz_recv, go,
):
    segments, n, channels, depth, plane = sizes
    cw = plane // 4
    cdepth = depth // 2
    own = depth * plane
    slab = cdepth * cw
    row_len = coarse_pre_h.shape[1]
    groups = pool_all.shape[0]
    group = pool_all.shape[2]
    s = lax.axis_index("segment")
    v = lax.axis_index("vol")
    has_left, has_right = v > 0, v < n - 1
    last = s == segments - 1
    late = s >= segments - 2
    first_owner = n // 2 - OWNERS // 2
    mine = v - first_owner
    owner = (mine >= 0) & (mine < OWNERS)
    share = 3 * channels // OWNERS

    def put(src, dst, send, recv, segment, vol):
        return pltpu.make_async_remote_copy(
            src_ref=src, dst_ref=dst, send_sem=send, recv_sem=recv,
            device_id=(segment, vol), device_id_type=pl.DeviceIdType.MESH,
        )

    def credit(segment):
        pl.semaphore_signal(
            go, inc=1, device_id=(segment, v), device_id_type=pl.DeviceIdType.MESH
        )

    barrier = pltpu.get_barrier_semaphore()

    def greet(off, carry):
        pl.semaphore_signal(
            barrier, inc=1, device_id=(s, lax.rem(v + off, n)),
            device_id_type=pl.DeviceIdType.MESH,
        )
        return carry

    lax.fori_loop(1, n, greet, 0)
    for up in (-1, 1):
        for side in (-1, 0, 1):
            there = (s + up >= 0) & (s + up < segments) & (v + side >= 0) & (v + side < n)

            @pl.when(there)
            def _(up=up, side=side):
                pl.semaphore_signal(
                    barrier, inc=1, device_id=(s + up, v + side),
                    device_id_type=pl.DeviceIdType.MESH,
                )

    def load(src, dst, index):
        return pltpu.make_async_copy(src, dst, load_sem.at[index])

    rows_load = load(coarse_pre_h, pre_rows.at[v], 0)
    pre_load = load(fine_pre_h, fine_pre, 1)
    seed_loads = (
        load(class_weight_h, class_weight, 2),
        load(cotangent_h, cotangent, 3),
        load(labels_h, labels, 4),
    )
    coarse_w_load = load(coarse_w_h, coarse_w, 5)
    fine_w_load = load(fine_w_h, fine_w, 6)
    saved_load = load(saved_h, saved, 7)
    pooled_load = load(pooled_h, pool_rows.at[v], 8)

    rows_load.start()

    @pl.when(last)
    def _():
        for copy in seed_loads:
            copy.start()

    for copy in (pre_load, coarse_w_load, fine_w_load, saved_load, pooled_load):
        copy.start()

    fine_lane = iota((1, own), 1)
    pool_target = (
        lax.div(fine_lane, 2 * plane) * cw
        + lax.div(lax.rem(fine_lane, plane), 2 * XL) * HX
        + lax.div(lax.rem(fine_lane, XL), 2)
    )
    pool_matrix[...] = jnp.where(iota((slab, own), 0) == pool_target, 1.0, 0.0).astype(BF)

    up_lane = iota((1, plane), 1)
    up_target = lax.div(up_lane, 2 * XL) * HX + lax.div(lax.rem(up_lane, XL), 2)
    up_matrix = jnp.where(iota((cw, plane), 0) == up_target, 0.125, 0.0).astype(BF)

    reach = cdepth + 4
    reach_lane = iota((1, reach * cw), 1)
    reach_depth = v * cdepth - 2 + lax.div(reach_lane, cw)
    reach_cell = reach_depth * HX + lax.rem(reach_lane, HX)
    reach_cell = jnp.where(
        (reach_depth >= 0) & (reach_depth < n * cdepth), reach_cell, -1
    )
    reach_inline = lax.div(lax.rem(reach_lane, cw), HX)
    whole_pick = pick.shape[0] > 1

    def picked(rows, u, cell, inline, lanes):
        chosen = iota((row_len, lanes), 0) == jnp.where(inline == u, cell, -1)
        return matmul(rows[u], jnp.where(chosen, 1.0, 0.0).astype(BF))

    if whole_pick:
        for u in range(n):
            chosen = iota((row_len, reach * cw), 0) == jnp.where(reach_inline == u, reach_cell, -1)
            pick[u * row_len:(u + 1) * row_len, :] = jnp.where(chosen, 1.0, 0.0).astype(BF)

    def step_copies(src, turn, segment):
        def step(which, a, b, vol):
            return put(a, b, step_send.at[turn, which], step_recv.at[which], segment, vol)

        block = pool_out.at[turn]
        planes = [step(5 + p, src.at[p], grad_ext.at[p + 1], v) for p in range(depth)]
        return (
            step(0, block, pool_ext.at[1], v),
            step(1, block, pool_ext.at[2], v - 1),
            step(2, block, pool_ext.at[0], v + 1),
            step(3, src.at[0], grad_ext.at[depth + 1], v - 1),
            step(4, src.at[depth - 1], grad_ext.at[0], v + 1),
            *planes,
        )

    def on_left(act, *copies):
        @pl.when(has_left)
        def _():
            for copy in copies:
                act(copy)

    def on_right(act, *copies):
        @pl.when(has_right)
        def _():
            for copy in copies:
                act(copy)

    def start(copy):
        copy.start()

    def wait_send(copy):
        copy.wait_send()

    def wait_recv(copy):
        copy.wait_recv()

    def pool_of(ref):
        flat = jnp.concatenate([ref[p] for p in range(depth)], axis=1)
        return matmul_nt(flat, pool_matrix[...]).astype(BF)

    @pl.when(last)
    def _():
        for copy in seed_loads:
            copy.wait()
        planes = jnp.swapaxes(cotangent[...], 0, 1)
        for p in range(depth):
            label = labels[p:p + 1, :]
            weight = jnp.zeros(label.shape, F32)
            for index in range(class_weight.shape[0]):
                weight = weight + jnp.where(label == index, class_weight[index], 0.0)
            block = (planes[p].astype(F32) * weight).astype(BF)
            seed[p] = block
            grad_ext[p + 1] = block
        pool_out[0] = pool_of(seed)
        pool_ext[1] = pool_out[0]

    pre_load.wait()
    pre_ext[1:depth + 1] = jnp.swapaxes(fine_pre[...], 0, 1)
    coarse_w_load.wait()
    fine_w_load.wait()
    for k in range(TAPS):
        rows = slice(k // 9 * channels, (k // 9 + 1) * channels)
        lanes = slice(k % 9 * channels, (k % 9 + 1) * channels)
        coarse_cat[rows, lanes] = coarse_w[k]
        fine_cat[rows, lanes] = fine_w[k]
    saved_load.wait()
    x_ext[1:depth + 1] = jnp.swapaxes(saved[...], 0, 1)

    @pl.when(v == 0)
    def _():
        pre_ext[0] = jnp.zeros((channels, plane), BF)
        x_ext[0] = jnp.zeros((channels, plane), BF)
        grad_ext[0] = jnp.zeros((channels, plane), BF)
        pool_ext[0] = jnp.zeros(pool_ext.shape[1:], BF)

    @pl.when(v == n - 1)
    def _():
        pre_ext[depth + 1] = jnp.zeros((channels, plane), BF)
        x_ext[depth + 1] = jnp.zeros((channels, plane), BF)
        grad_ext[depth + 1] = jnp.zeros((channels, plane), BF)
        pool_ext[2] = jnp.zeros(pool_ext.shape[1:], BF)

    rows_load.wait()
    pooled_load.wait()

    ups = jnp.where(s > 0, 1, 0) + jnp.where(last, 0, 1)
    sides = 1 + jnp.where(has_left, 1, 0) + jnp.where(has_right, 1, 0)
    pl.semaphore_wait(barrier, n - 1 + ups * sides)

    def halo(ref, index):
        return (
            put(ref.at[1], ref.at[depth + 1], halo_send.at[index], halo_recv.at[index], s, v - 1),
            put(
                ref.at[depth], ref.at[0],
                halo_send.at[index + 1], halo_recv.at[index + 1], s, v + 1,
            ),
        )

    pre_left, pre_right = halo(pre_ext, 0)
    x_left, x_right = halo(x_ext, 2)

    def row_copy(which, off):
        ref = (pre_rows, pool_rows, gz_all)[which]
        return put(
            ref.at[v], ref.at[v], row_send.at[which, off], row_recv.at[which, v],
            s, lax.rem(v + off, n),
        )

    def send_rows(which):
        def body(off, carry):
            row_copy(which, off).start()
            return carry

        lax.fori_loop(1, n, body, 0)

    def wait_rows(which):
        ref = (pre_rows, pool_rows, gz_all)[which]

        def body(off, carry):
            u = lax.rem(v + off, n)
            put(
                ref.at[u], ref.at[u], row_send.at[which, off], row_recv.at[which, u], s, u
            ).wait_recv()
            return carry

        lax.fori_loop(1, n, body, 0)

    @pl.when(last)
    def _():
        send_rows(0)
        copies = step_copies(seed, 0, s)
        on_left(start, copies[1], copies[3], pre_left)
        on_right(start, copies[2], copies[4], pre_right)

    @pl.when(jnp.logical_not(last))
    def _():
        @pl.when(s == segments - 2)
        def _():
            pl.semaphore_wait(go, 1)

        send_rows(0)
        on_left(start, pre_left, x_left)
        on_right(start, pre_right, x_right)

    wait_rows(0)

    @pl.when(last)
    def _():
        credit(s - 1)

    if whole_pick:
        flat_rows = jnp.concatenate([pre_rows[u] for u in range(n)], axis=1)
        coarse_gate[...] = matmul(flat_rows, pick[...]).astype(BF)
    else:
        coarse_gate[...] = lax.fori_loop(
            0, n,
            lambda u, total: total + picked(
                pre_rows, u, reach_cell, reach_inline, reach * cw
            ),
            jnp.zeros((channels, reach * cw), F32),
        ).astype(BF)

    def take_pooled():
        wait_rows(1)
        lane = iota((1, group), 1)
        inline = lax.div(lax.rem(lane, cw), HX)

        def body(g, carry):
            cell = (g * (group // cw) + lax.div(lane, cw)) * HX + lax.rem(lane, HX)
            pool_all[g] = lax.fori_loop(
                0, n,
                lambda u, total: total + picked(pool_rows, u, cell, inline, group),
                jnp.zeros((channels, group), F32),
            ).astype(BF)
            return carry

        lax.fori_loop(0, groups, body, 0)

    def take_fine_x():
        for outer in range(3):
            for p in range(depth):
                fine_x[outer * channels:(outer + 1) * channels, p * plane:(p + 1) * plane] = (
                    x_ext[p + outer]
                )

    @pl.when(jnp.logical_not(late))
    def _():
        send_rows(1)
        take_pooled()

    @pl.when(jnp.logical_not(last))
    def _():
        on_left(wait_recv, pre_right, x_right)
        on_right(wait_recv, pre_left, x_left)
        take_fine_x()

    incoming = step_copies(out, 1, s)

    @pl.when(jnp.logical_not(last))
    def _():
        incoming[0].wait_recv()

    on_left(wait_recv, incoming[2])
    on_right(wait_recv, incoming[1])

    side = pool_ext.shape[2]
    near = jnp.concatenate(
        [pool_ext[0][:, side - 2 * cw:], pool_ext[1], pool_ext[2][:, :2 * cw]], axis=1
    )
    coarse_gz = jnp.where(coarse_gate[...] > 0, near, jnp.zeros_like(near))
    gz_all[v] = coarse_gz[:, 2 * cw:2 * cw + slab]
    for r, (row_step, col_step) in enumerate(STEPS):
        mask = tap_mask(reach * cw, cw, HX, row_step, col_step)
        coarse_cols[r * channels:(r + 1) * channels, :] = (
            rolled(coarse_gz, row_step * HX + col_step) * mask
        )

    @pl.when(s == 0)
    def _():
        send_rows(2)

    terms = matmul(coarse_cat[...], coarse_cols[...])
    width = (cdepth + 2) * cw
    coarse_back = sum(
        terms[outer * channels:(outer + 1) * channels, (2 - outer) * cw:(2 - outer) * cw + width]
        for outer in range(3)
    ).astype(BF)

    pieces = []
    for p in range(depth + 2):
        j = (p + 1) // 2
        if p and j == p // 2:
            spread = pieces[-1]
        else:
            spread = matmul(coarse_back[:, j * cw:(j + 1) * cw], up_matrix)
        pieces.append(spread)

    @pl.when(last)
    def _():
        on_left(wait_recv, pre_right)
        on_right(wait_recv, pre_left)

    masks = [tap_mask(plane, plane, XL, *step) for step in STEPS]
    for p in (1, 0, depth + 1, *range(2, depth + 1)):
        if p == 0:
            on_left(wait_recv, incoming[4])
        elif p == depth + 1:
            on_right(wait_recv, incoming[3])
        else:
            @pl.when(jnp.logical_not(last))
            def _(p=p):
                incoming[4 + p].wait_recv()

        grad = grad_ext[p].astype(F32) + pieces[p]
        gz = jnp.where(pre_ext[p].astype(F32) > 0, grad, 0.0).astype(BF)
        for r, (row_step, col_step) in enumerate(STEPS):
            fine_cols[r * channels:(r + 1) * channels, p * plane:(p + 1) * plane] = (
                rolled(gz, row_step * XL + col_step) * masks[r]
            )

    @pl.when(s == segments - 2)
    def _():
        credit(s + 1)

    def sum_copy(j, vol_from, vol_to):
        return put(
            parts.at[j], arrived.at[vol_from],
            sum_send.at[j], sum_recv.at[vol_from], s, vol_to,
        )

    def fine_sums():
        grads = matmul_nt(fine_x[...], fine_cols[:, plane:plane + own]).astype(BF)
        for j in range(OWNERS):
            parts[j] = grads[j * share:(j + 1) * share, :]
        for j in range(OWNERS):
            @pl.when(v != first_owner + j)
            def _(j=j):
                sum_copy(j, v, first_owner + j).start()

            @pl.when(v == first_owner + j)
            def _(j=j):
                arrived[v] = parts[j]

    @pl.when(s == 0)
    def _():
        fine_sums()

    outgoing = step_copies(out, 1, s - 1)
    terms = matmul(fine_cat[...], fine_cols[...])
    for p in range(depth):
        total = grad_ext[p + 1].astype(F32)
        for outer in range(3):
            total = total + terms[
                outer * channels:(outer + 1) * channels,
                (p + 2 - outer) * plane:(p + 3 - outer) * plane,
            ]
        out[p] = total.astype(BF)

    @pl.when(s > 0)
    def _():
        outgoing[5].start()
        pool_out[1] = pool_of(out)
        on_left(start, outgoing[1])
        on_right(start, outgoing[2])
        outgoing[0].start()
        on_left(start, outgoing[3])
        on_right(start, outgoing[4])
        for p in range(1, depth):
            outgoing[5 + p].start()

    @pl.when(last)
    def _():
        pl.semaphore_wait(go, 1)
        on_left(start, x_left)
        on_right(start, x_right)

    @pl.when(late)
    def _():
        send_rows(1)
        take_pooled()

    @pl.when(last)
    def _():
        on_left(wait_recv, x_right)
        on_right(wait_recv, x_left)
        take_fine_x()

    @pl.when(s > 0)
    def _():
        fine_sums()
        send_rows(2)

    grad_out[...] = jnp.swapaxes(out[...], 0, 1)

    def coarse_sums():
        total = jnp.zeros((3 * channels, 9 * channels), F32)
        edge = jnp.zeros((channels, cw), BF)
        for g in range(groups):
            xs = jnp.concatenate(
                [
                    pool_all[g - 1][:, group - cw:] if g else edge,
                    pool_all[g],
                    pool_all[g + 1][:, :cw] if g < groups - 1 else edge,
                ],
                axis=1,
            )
            tall = jnp.concatenate([xs[:, o * cw:o * cw + group] for o in range(3)], axis=0)
            slabs = group // slab
            flat = jnp.concatenate([gz_all[g * slabs + u] for u in range(slabs)], axis=1)
            for r, (row_step, col_step) in enumerate(STEPS):
                mask = tap_mask(group, cw, HX, row_step, col_step)
                full_cols[r * channels:(r + 1) * channels, :] = (
                    rolled(flat, row_step * HX + col_step) * mask
                )
            total = total + matmul_nt(tall, full_cols[...])
        return total * scales[1]

    def place(ref, first_row, value):
        rows = value.shape[0]
        at = first_row
        while at < first_row + rows:
            outer, inner = divmod(at, channels)
            count = min(channels - inner, first_row + rows - at)
            for r in range(9):
                ref[outer * 9 + r, inner:inner + count, :] = value[
                    at - first_row:at - first_row + count, r * channels:(r + 1) * channels
                ]
            at += count

    def all_copy(j, off, vol_to):
        return put(
            collected.at[j], collected.at[j], all_send.at[off], all_recv.at[j], s, vol_to
        )

    @pl.when(owner)
    def _():
        def arrive(off, carry):
            u = lax.rem(v + off, n)
            sum_copy(0, u, u).wait_recv()
            return carry

        lax.fori_loop(1, n, arrive, 0)
        whole = arrived[0].astype(F32)
        for u in range(1, n):
            whole = whole + arrived[u].astype(F32)
        collected[mine] = whole.astype(BF)

        def hand(off, carry):
            all_copy(mine, off, lax.rem(v + off, n)).start()
            return carry

        lax.fori_loop(1, n, hand, 0)

    wait_rows(2)
    place(coarse_out, 0, coarse_sums())

    for j in range(OWNERS):
        @pl.when(v != first_owner + j)
        def _(j=j):
            all_copy(j, 0, v).wait_recv()

        place(fine_out, j * share, collected[j].astype(F32) * scales[0])

    def rest(off, carry):
        for which in range(3):
            row_copy(which, off).wait_send()

        @pl.when(owner)
        def _():
            all_copy(mine, off, lax.rem(v + off, n)).wait_send()

        return carry

    lax.fori_loop(1, n, rest, 0)
    for j in range(OWNERS):
        @pl.when(v != first_owner + j)
        def _(j=j):
            sum_copy(j, v, first_owner + j).wait_send()

    on_left(wait_send, pre_left, x_left)
    on_right(wait_send, pre_right, x_right)

    @pl.when(last)
    def _():
        copies = step_copies(seed, 0, s)
        on_left(wait_send, copies[1], copies[3])
        on_right(wait_send, copies[2], copies[4])

    @pl.when(s > 0)
    def _():
        on_left(wait_send, outgoing[1], outgoing[3])
        on_right(wait_send, outgoing[2], outgoing[4])
        wait_send(outgoing[0])
        for p in range(depth):
            wait_send(outgoing[5 + p])


def finish(grad, fine, coarse, grad_out, fine_out, coarse_out, sem):
    copies = [
        pltpu.make_async_copy(src, dst, sem.at[index])
        for index, (src, dst) in enumerate(
            ((fine, fine_out), (coarse, coarse_out), (grad, grad_out))
        )
    ]
    for copy in copies:
        copy.start()
    for copy in copies:
        copy.wait()


def on_device(
    cotangent, labels, class_weight, inputs, fine_pre, pooled, coarse_pre,
    fine_filters, coarse_filters,
):
    segments = lax.axis_size("segment")
    n = lax.axis_size("vol")
    channels, depth, plane = inputs.shape[1:]
    own = depth * plane
    cw = plane // 4
    cdepth = depth // 2
    slab = cdepth * cw
    reach = cdepth + 4
    row_len = pooled.shape[2] * pooled.shape[3]
    cells = own * n
    scales = (1.0 / math.sqrt(cells), 1.0 / math.sqrt(cells // 8))
    sizes = (segments, n, channels, depth, plane)
    group = min(GROUP_LANES, n * slab)
    groups = n * slab // group
    share = 3 * channels // OWNERS
    pick_shape = (n * row_len, reach * cw)
    if math.prod(pick_shape) * 2 > PICK_BYTES:
        pick_shape = (1, 128)
    vmem = pl.BlockSpec(memory_space=pltpu.VMEM)
    limit = min(60 * MIB, 16 * MIB + 6 * 2 * 9 * channels * (own + 2 * plane))
    hbm = pl.BlockSpec(memory_space=pltpu.HBM)
    dma = pltpu.SemaphoreType.DMA
    tap_shape = jax.ShapeDtypeStruct((TAPS, channels, channels), F32)
    grad_shape = jax.ShapeDtypeStruct((channels, depth, plane), BF)
    outs = pl.pallas_call(
        functools.partial(kernel, sizes, scales),
        out_shape=(grad_shape, tap_shape, tap_shape),
        in_specs=[hbm] * 9,
        out_specs=(vmem, vmem, vmem),
        scratch_shapes=[
            pltpu.SMEM(class_weight.shape, F32),
            pltpu.VMEM(cotangent.shape, BF),
            pltpu.VMEM(labels.shape, jnp.int32),
            pltpu.VMEM((channels, depth, plane), BF),
            pltpu.VMEM((channels, depth, plane), BF),
            pltpu.VMEM((TAPS, channels, channels), BF),
            pltpu.VMEM((TAPS, channels, channels), BF),
            pltpu.VMEM((depth, channels, plane), BF),
            pltpu.VMEM((depth, channels, plane), BF),
            pltpu.VMEM((3 * channels, 9 * channels), BF),
            pltpu.VMEM((3 * channels, 9 * channels), BF),
            pltpu.VMEM((n, channels, row_len), BF),
            pltpu.VMEM((n, channels, row_len), BF),
            pltpu.VMEM((depth + 2, channels, plane), BF),
            pltpu.VMEM((depth + 2, channels, plane), BF),
            pltpu.VMEM((depth + 2, channels, plane), BF),
            pltpu.VMEM((3, channels, slab), BF),
            pltpu.VMEM((2, channels, slab), BF),
            pltpu.VMEM((channels, reach * cw), BF),
            pltpu.VMEM(pick_shape, BF),
            pltpu.VMEM((slab, own), BF),
            pltpu.VMEM((3 * channels, own), BF),
            pltpu.VMEM((groups, channels, group), BF),
            pltpu.VMEM((9 * channels, own + 2 * plane), BF),
            pltpu.VMEM((9 * channels, reach * cw), BF),
            pltpu.VMEM((9 * channels, group), BF),
            pltpu.VMEM((n, channels, slab), BF),
            pltpu.VMEM((OWNERS, share, 9 * channels), BF),
            pltpu.VMEM((n, share, 9 * channels), BF),
            pltpu.VMEM((OWNERS, share, 9 * channels), BF),
            dma((9,)), dma((3, n)), dma((3, n)), dma((4,)), dma((4,)),
            dma((2, 5 + depth)), dma((5 + depth,)),
            dma((OWNERS,)), dma((n,)), dma((n,)), dma((OWNERS,)), dma((1,)), dma((1,)),
            pltpu.SemaphoreType.REGULAR,
        ],
        compiler_params=pltpu.CompilerParams(
            collective_id=0, has_side_effects=True, vmem_limit_bytes=limit
        ),
    )(
        *(
            pltpu.with_memory_space_constraint(array, pltpu.HBM)
            for array in (
                class_weight,
                cotangent,
                labels,
                inputs[0],
                fine_pre[0],
                coarse_pre[0].reshape(channels, row_len),
                pooled[0].reshape(channels, row_len),
                fine_filters[0],
                coarse_filters[0],
            )
        )
    )

    spaces = pl.BlockSpec(memory_space=pl.ANY)
    grad, fine_grads, coarse_grads = pl.pallas_call(
        finish,
        out_shape=(grad_shape, tap_shape, tap_shape),
        in_specs=[spaces] * 3,
        out_specs=[hbm] * 3,
        scratch_shapes=[dma((3,))],
        compiler_params=pltpu.CompilerParams(vmem_limit_bytes=1024 * 1024),
    )(*outs)
    return (grad[None], fine_grads[None], coarse_grads[None])


def solution(mesh):
    return jax.shard_map(
        on_device,
        mesh=mesh,
        in_specs=(
            P(None, "vol", None),
            P("vol", None),
            P(),
            P("segment", None, "vol", None),
            P("segment", None, "vol", None),
            P("segment", None, "vol", None),
            P("segment", None, "vol", None),
            P("segment", None, None, None),
            P("segment", None, None, None),
        ),
        out_specs=(
            P("segment", None, "vol", None),
            P("segment", None, None, None),
            P("segment", None, None, None),
        ),
        check_vma=False,
    )
```

```python
import functools
import math

import jax
import jax.numpy as jnp
from jax import lax
from jax.experimental import pallas as pl
from jax.experimental.pallas import tpu as pltpu
from jax.sharding import PartitionSpec as P

XL = 16
HX = XL // 2
TAPS = 27
KEEPERS = 4
PARTS = 3
GROUP_LANES = 1024
MIB = 1024 * 1024
PICK_BYTES = 4 * MIB
BF = jnp.bfloat16
F32 = jnp.float32


def iota(shape, dim):
    return lax.broadcasted_iota(jnp.int32, shape, dim)


def matmul(a, b):
    return lax.dot_general(a, b, (((1,), (0,)), ((), ())), preferred_element_type=F32)


def matmul_nt(a, b):
    return lax.dot_general(a, b, (((1,), (1,)), ((), ())), preferred_element_type=F32)


def tap_mask(lanes, plane, columns, row_step, col_step):
    lane = iota((1, lanes), 1)
    column = lax.rem(lane, columns) - col_step
    row = lax.div(lax.rem(lane, plane), columns) - row_step
    rows = plane // columns
    inside = (column >= 0) & (column < columns) & (row >= 0) & (row < rows)
    return jnp.where(inside, 1.0, 0.0).astype(BF)


def rolled(value, shift):
    size = value.shape[1]
    shift = shift % size
    return value if shift == 0 else pltpu.roll(value, shift, 1)


STEPS = [(r, c) for r in (-1, 0, 1) for c in (-1, 0, 1)]


def kernel(
    sizes, scales,
    class_weight_h, cotangent_h, labels_h, saved_h, fine_pre_h, coarse_pre_h, pooled_h,
    fine_w_h, coarse_w_h,
    grad_o, fine_o, coarse_o,
    grad_out, fine_out, coarse_out, class_weight, cotangent, labels, saved, fine_pre, weights,
    out, seed, fine_cat, coarse_cat, pre_rows, pool_rows, pre_ext, x_ext, grad_ext, pool_ext,
    pool_out, coarse_gate, pick, pool_matrix, fine_x, pool_all, fine_cols, coarse_cols,
    full_cols, gz_all, parts, landed, paired, middle, arrived, collected,
    load_sem, row_send, row_recv, halo_send, halo_recv, step_send, step_recv,
    pair_send, pair_recv, sum_send, sum_recv, hand_send, pass_send, all_recv,
    straight_send, straight_recv, spread_send, store_sem, go,
):
    segments, n, channels, depth, plane = sizes
    cw = plane // 4
    cdepth = depth // 2
    own = depth * plane
    slab = cdepth * cw
    row_len = coarse_pre_h.shape[1]
    groups = pool_all.shape[0]
    group = pool_all.shape[2]
    s = lax.axis_index("segment")
    v = lax.axis_index("vol")
    has_left, has_right = v > 0, v < n - 1
    last = s == segments - 1
    late = s >= segments - 2
    paced = lax.rem(s, 2) == 1
    direct = jnp.logical_not(paced)
    half = lax.rem(v, 2)
    other = 1 - half
    partner = v + 1 - 2 * half
    row = lax.div(v, 2)
    columns = n // 2
    first_owner = columns // 2 - 1
    share = 3 * channels // KEEPERS
    rows_each = share // PARTS
    first_keeper = n // 2 - KEEPERS // 2
    mine = v - first_keeper
    keeper = (mine >= 0) & (mine < KEEPERS)

    def put(src, dst, send, recv, segment, vol):
        return pltpu.make_async_remote_copy(
            src_ref=src, dst_ref=dst, send_sem=send, recv_sem=recv,
            device_id=(segment, vol), device_id_type=pl.DeviceIdType.MESH,
        )

    def credit(segment):
        pl.semaphore_signal(
            go, inc=1, device_id=(segment, v), device_id_type=pl.DeviceIdType.MESH
        )

    barrier = pltpu.get_barrier_semaphore()

    def greet(off, carry):
        pl.semaphore_signal(
            barrier, inc=1, device_id=(s, lax.rem(v + off, n)),
            device_id_type=pl.DeviceIdType.MESH,
        )
        return carry

    lax.fori_loop(1, n, greet, 0)
    for up in (-1, 1):
        for side in (-1, 0, 1):
            there = (s + up >= 0) & (s + up < segments) & (v + side >= 0) & (v + side < n)

            @pl.when(there)
            def _(up=up, side=side):
                pl.semaphore_signal(
                    barrier, inc=1, device_id=(s + up, v + side),
                    device_id_type=pl.DeviceIdType.MESH,
                )

    def load(src, dst, index):
        return pltpu.make_async_copy(src, dst, load_sem.at[index])

    rows_load = load(coarse_pre_h, pre_rows.at[v], 0)
    pre_load = load(fine_pre_h, fine_pre, 1)
    seed_loads = (
        load(class_weight_h, class_weight, 2),
        load(cotangent_h, cotangent, 3),
        load(labels_h, labels, 4),
    )
    coarse_w_load = load(coarse_w_h, weights.at[0], 5)
    fine_w_load = load(fine_w_h, weights.at[1], 5)
    both_w_load = load(weights, weights, 5)
    saved_load = load(saved_h, saved, 6)
    pooled_load = load(pooled_h, pool_rows.at[v], 7)

    rows_load.start()

    @pl.when(last)
    def _():
        for copy in seed_loads:
            copy.start()

    for copy in (pre_load, coarse_w_load, fine_w_load, saved_load, pooled_load):
        copy.start()

    fine_lane = iota((own, 1), 0)
    pool_target = (
        lax.div(fine_lane, 2 * plane) * cw
        + lax.div(lax.rem(fine_lane, plane), 2 * XL) * HX
        + lax.div(lax.rem(fine_lane, XL), 2)
    )
    pool_matrix[...] = jnp.where(iota((own, slab), 1) == pool_target, 1.0, 0.0).astype(BF)

    up_lane = iota((1, plane), 1)
    up_target = lax.div(up_lane, 2 * XL) * HX + lax.div(lax.rem(up_lane, XL), 2)
    up_matrix = jnp.where(iota((cw, plane), 0) == up_target, 0.125, 0.0).astype(BF)

    reach = cdepth + 4
    reach_lane = iota((1, reach * cw), 1)
    reach_depth = v * cdepth - 2 + lax.div(reach_lane, cw)
    reach_cell = reach_depth * HX + lax.rem(reach_lane, HX)
    reach_cell = jnp.where(
        (reach_depth >= 0) & (reach_depth < n * cdepth), reach_cell, -1
    )
    reach_inline = lax.div(lax.rem(reach_lane, cw), HX)
    whole_pick = pick.shape[0] > 1

    def picked(rows, u, cell, inline, lanes):
        chosen = iota((row_len, lanes), 0) == jnp.where(inline == u, cell, -1)
        return matmul(rows[u], jnp.where(chosen, 1.0, 0.0).astype(BF))

    if whole_pick:
        for u in range(n):
            chosen = iota((row_len, reach * cw), 0) == jnp.where(reach_inline == u, reach_cell, -1)
            pick[u * row_len:(u + 1) * row_len, :] = jnp.where(chosen, 1.0, 0.0).astype(BF)

    def step_copies(src, turn, segment):
        def step(which, a, b, vol):
            return put(a, b, step_send.at[which], step_recv.at[which], segment, vol)

        block = pool_out.at[turn]
        return (
            step(0, block, pool_ext.at[1], v),
            step(1, block, pool_ext.at[2], v - 1),
            step(2, block, pool_ext.at[0], v + 1),
            step(3, src.at[0], grad_ext.at[depth + 1], v - 1),
            step(4, src.at[depth - 1], grad_ext.at[0], v + 1),
            step(5, src, grad_ext.at[1:depth + 1], v),
            step(5, src.at[0], grad_ext.at[1], v),
            step(5, src.at[1:depth], grad_ext.at[2:depth + 1], v),
        )

    def on_left(act, *copies):
        @pl.when(has_left)
        def _():
            for copy in copies:
                act(copy)

    def on_right(act, *copies):
        @pl.when(has_right)
        def _():
            for copy in copies:
                act(copy)

    def start(copy):
        copy.start()

    def wait_send(copy):
        copy.wait_send()

    def wait_recv(copy):
        copy.wait_recv()

    def pool_of(ref):
        flat = jnp.concatenate([ref[p] for p in range(depth)], axis=1)
        return matmul(flat, pool_matrix[...]).astype(BF)

    @pl.when(last)
    def _():
        for copy in seed_loads:
            copy.wait()
        planes = jnp.swapaxes(cotangent[...], 0, 1)
        for p in range(depth):
            label = labels[p:p + 1, :]
            weight = jnp.zeros(label.shape, F32)
            for index in range(class_weight.shape[0]):
                weight = weight + jnp.where(label == index, class_weight[index], 0.0)
            block = (planes[p].astype(F32) * weight).astype(BF)
            seed[p] = block
            grad_ext[p + 1] = block
        pool_out[0] = pool_of(seed)
        pool_ext[1] = pool_out[0]

    pre_load.wait()
    pre_ext[1:depth + 1] = jnp.swapaxes(fine_pre[...], 0, 1)
    both_w_load.wait()
    for k in range(TAPS):
        rows = slice(k // 9 * channels, (k // 9 + 1) * channels)
        lanes = slice(k % 9 * channels, (k % 9 + 1) * channels)
        coarse_cat[rows, lanes] = weights[0, k]
        fine_cat[rows, lanes] = weights[1, k]
    saved_load.wait()
    x_ext[1:depth + 1] = jnp.swapaxes(saved[...], 0, 1)

    @pl.when(v == 0)
    def _():
        pre_ext[0] = jnp.zeros((channels, plane), BF)
        x_ext[0] = jnp.zeros((channels, plane), BF)
        grad_ext[0] = jnp.zeros((channels, plane), BF)
        pool_ext[0] = jnp.zeros(pool_ext.shape[1:], BF)

    @pl.when(v == n - 1)
    def _():
        pre_ext[depth + 1] = jnp.zeros((channels, plane), BF)
        x_ext[depth + 1] = jnp.zeros((channels, plane), BF)
        grad_ext[depth + 1] = jnp.zeros((channels, plane), BF)
        pool_ext[2] = jnp.zeros(pool_ext.shape[1:], BF)

    rows_load.wait()
    pooled_load.wait()

    ups = jnp.where(s > 0, 1, 0) + jnp.where(last, 0, 1)
    sides = 1 + jnp.where(has_left, 1, 0) + jnp.where(has_right, 1, 0)
    pl.semaphore_wait(barrier, n - 1 + ups * sides)

    def halo(ref, index):
        return (
            put(ref.at[1], ref.at[depth + 1], halo_send.at[index], halo_recv.at[index], s, v - 1),
            put(
                ref.at[depth], ref.at[0],
                halo_send.at[index + 1], halo_recv.at[index + 1], s, v + 1,
            ),
        )

    pre_left, pre_right = halo(pre_ext, 0)
    x_left, x_right = halo(x_ext, 2)

    def far_first(act):
        def body(step, carry):
            for u in (v + n - step, v - n + step):
                @pl.when((u >= 0) & (u < n))
                def _(u=u):
                    act(u)

            return carry

        lax.fori_loop(1, n, body, 0)

    def others(act):
        def body(off, carry):
            act(lax.rem(v + off, n))
            return carry

        lax.fori_loop(1, n, body, 0)

    def row_copy(which, source, target):
        ref = (pre_rows, pool_rows, gz_all)[which]
        return put(
            ref.at[source], ref.at[source], row_send.at[which], row_recv.at[which], s, target
        )

    def all_rows(which):
        ref = (pre_rows, pool_rows, gz_all)[which].at[pl.ds(0, n - 1)]
        return put(ref, ref, row_send.at[which], row_recv.at[which], s, partner)

    def send_rows(which):
        far_first(lambda u: row_copy(which, v, u).start())

    def send_gz():
        for off in range(1, n):
            row_copy(2, v, lax.rem(v + off, n)).start()

    def wait_rows(which):
        all_rows(which).wait_recv()

    @pl.when(last)
    def _():
        copies = step_copies(seed, 0, s)
        on_left(start, copies[1])
        on_right(start, copies[2])
        send_rows(0)
        on_left(start, copies[3], pre_left)
        on_right(start, copies[4], pre_right)

    @pl.when(jnp.logical_not(last))
    def _():
        @pl.when(s == segments - 2)
        def _():
            pl.semaphore_wait(go, 1)

        send_rows(0)
        on_left(start, pre_left)
        on_right(start, pre_right)

    @pl.when(jnp.logical_not(late))
    def _():
        on_left(start, x_left)
        on_right(start, x_right)

    wait_rows(0)

    @pl.when(last)
    def _():
        credit(s - 1)

    if whole_pick:
        flat_rows = jnp.concatenate([pre_rows[u] for u in range(n)], axis=1)
        coarse_gate[...] = matmul(flat_rows, pick[...]).astype(BF)
    else:
        coarse_gate[...] = lax.fori_loop(
            0, n,
            lambda u, total: total + picked(
                pre_rows, u, reach_cell, reach_inline, reach * cw
            ),
            jnp.zeros((channels, reach * cw), F32),
        ).astype(BF)

    def take_pooled():
        wait_rows(1)
        lane = iota((1, group), 1)
        inline = lax.div(lax.rem(lane, cw), HX)

        def body(g, carry):
            cell = (g * (group // cw) + lax.div(lane, cw)) * HX + lax.rem(lane, HX)
            pool_all[g] = lax.fori_loop(
                0, n,
                lambda u, total: total + picked(pool_rows, u, cell, inline, group),
                jnp.zeros((channels, group), F32),
            ).astype(BF)
            return carry

        lax.fori_loop(0, groups, body, 0)

    def take_fine_x():
        for outer in range(3):
            for p in range(depth):
                fine_x[outer * channels:(outer + 1) * channels, p * plane:(p + 1) * plane] = (
                    x_ext[p + outer]
                )

    @pl.when(jnp.logical_not(late))
    def _():
        send_rows(1)
        take_pooled()

    @pl.when(jnp.logical_not(late))
    def _():
        on_left(wait_recv, x_right)
        on_right(wait_recv, x_left)
        take_fine_x()

    incoming = step_copies(out, 1, s)

    on_left(wait_recv, incoming[2])
    on_right(wait_recv, incoming[1])

    @pl.when(jnp.logical_not(last))
    def _():
        incoming[0].wait_recv()

    side = pool_ext.shape[2]
    near = jnp.concatenate(
        [pool_ext[0][:, side - 2 * cw:], pool_ext[1], pool_ext[2][:, :2 * cw]], axis=1
    )
    coarse_gz = jnp.where(coarse_gate[...] > 0, near, jnp.zeros_like(near))
    gz_all[v] = coarse_gz[:, 2 * cw:2 * cw + slab]
    for r, (row_step, col_step) in enumerate(STEPS):
        mask = tap_mask(reach * cw, cw, HX, row_step, col_step)
        coarse_cols[r * channels:(r + 1) * channels, :] = (
            rolled(coarse_gz, row_step * HX + col_step) * mask
        )

    terms = matmul(coarse_cat[...], coarse_cols[...])
    width = (cdepth + 2) * cw
    coarse_back = sum(
        terms[outer * channels:(outer + 1) * channels, (2 - outer) * cw:(2 - outer) * cw + width]
        for outer in range(3)
    ).astype(BF)

    pieces = []
    for p in range(depth + 2):
        j = (p + 1) // 2
        if p and j == p // 2:
            spread = pieces[-1]
        else:
            spread = matmul(coarse_back[:, j * cw:(j + 1) * cw], up_matrix)
        pieces.append(spread)

    on_left(wait_recv, pre_right, incoming[4])
    on_right(wait_recv, pre_left, incoming[3])

    @pl.when(jnp.logical_not(last))
    def _():
        incoming[5].wait_recv()

    @pl.when(jnp.logical_not(late) & (s > 0))
    def _():
        send_gz()

    gz = []
    for p in range(depth + 2):
        grad = grad_ext[p].astype(F32) + pieces[p]
        gz.append(jnp.where(pre_ext[p].astype(F32) > 0, grad, 0.0).astype(BF))
    for r, (row_step, col_step) in enumerate(STEPS):
        mask = tap_mask(plane, plane, XL, row_step, col_step)
        for p in range(depth + 2):
            fine_cols[r * channels:(r + 1) * channels, p * plane:(p + 1) * plane] = (
                rolled(gz[p], row_step * XL + col_step) * mask
            )

    def pair_copy(k):
        return put(
            parts.at[2 * other + k], paired.at[k], pair_send.at[k], pair_recv.at[k], s, partner
        )

    def sum_copy(k, row_from, row_to):
        return put(
            middle.at[k], arrived.at[row_from],
            sum_send.at[k], sum_recv.at[0], s, 2 * row_to + half,
        )

    def fine_sums():
        grads = matmul_nt(fine_x[...], fine_cols[:, plane:plane + own]).astype(BF)
        for j in range(KEEPERS):
            parts[j] = grads[j * share:(j + 1) * share, :]

    def pair_sends():
        for k in range(2):
            pair_copy(k).start()

    def part_rows(part):
        return pl.ds(part * rows_each, rows_each)

    def straight_copy(j, part, vol_to):
        return put(
            parts.at[j, part_rows(part)], landed.at[part, v],
            straight_send.at[0], straight_recv.at[part], s, vol_to,
        )

    def straight_landed(part):
        block = landed.at[part, pl.ds(0, n - 1)]
        return put(block, block, straight_send.at[0], straight_recv.at[part], s, partner)

    def straight_sends():
        def send(order):
            for part in range(PARTS):
                for j in order:
                    @pl.when(v != first_keeper + j)
                    def _(j=j, part=part):
                        straight_copy(j, part, first_keeper + j).start()

        @pl.when(v < n // 2)
        def _():
            send(range(KEEPERS - 1, -1, -1))

        @pl.when(v >= n // 2)
        def _():
            send(range(KEEPERS))

        @pl.when(keeper)
        def _():
            for part in range(PARTS):
                landed[part, v] = parts[mine, part_rows(part)]

    def column_sums():
        for k in range(2):
            pair_copy(k).wait_recv()
            both = parts[2 * half + k].astype(F32) + paired[k].astype(F32)
            middle[k] = both.astype(BF)

            @pl.when(row != first_owner + k)
            def _(k=k):
                sum_copy(k, row, first_owner + k).start()

            @pl.when(row == first_owner + k)
            def _(k=k):
                arrived[row] = middle[k]

    @pl.when(s == 0)
    def _():
        fine_sums()
        straight_sends()
        send_gz()

    @pl.when(last)
    def _():
        copies = step_copies(seed, 0, s)
        on_left(wait_send, copies[1], copies[3])
        on_right(wait_send, copies[2], copies[4])

    outgoing = step_copies(out, 1, s - 1)
    terms = matmul(fine_cat[...], fine_cols[...])
    for p in range(depth):
        total = grad_ext[p + 1].astype(F32)
        for outer in range(3):
            total = total + terms[
                outer * channels:(outer + 1) * channels,
                (p + 2 - outer) * plane:(p + 3 - outer) * plane,
            ]
        out[p] = total.astype(BF)

    @pl.when(s > 0)
    def _():
        outgoing[6].start()
        pool_out[1] = pool_of(out)
        on_left(start, outgoing[1])
        on_right(start, outgoing[2])
        outgoing[0].start()
        on_left(start, outgoing[3])
        on_right(start, outgoing[4])
        outgoing[7].start()

    @pl.when(s == segments - 2)
    def _():
        credit(s + 1)

    @pl.when(last)
    def _():
        pl.semaphore_wait(go, 1)

    @pl.when(late)
    def _():
        on_left(start, x_left)
        on_right(start, x_right)
        send_rows(1)
        take_pooled()
        on_left(wait_recv, x_right)
        on_right(wait_recv, x_left)
        take_fine_x()

    @pl.when(late)
    def _():
        send_gz()

    @pl.when(s > 0)
    def _():
        fine_sums()

        @pl.when(paced)
        def _():
            pair_sends()

        @pl.when(direct)
        def _():
            straight_sends()

    grad_store = pltpu.make_async_copy(grad_out, grad_o, store_sem.at[0])
    coarse_store = pltpu.make_async_copy(coarse_out, coarse_o, store_sem.at[1])

    def fine_store(outer, first, stop):
        at = (slice(outer * 9, (outer + 1) * 9), slice(first, stop))
        return pltpu.make_async_copy(fine_out.at[at], fine_o.at[at], store_sem.at[2])

    grad_out[...] = jnp.swapaxes(out[...], 0, 1)
    grad_store.start()

    def coarse_sums():
        total = jnp.zeros((3 * channels, 9 * channels), F32)
        edge = jnp.zeros((channels, cw), BF)
        for g in range(groups):
            xs = jnp.concatenate(
                [
                    pool_all[g - 1][:, group - cw:] if g else edge,
                    pool_all[g],
                    pool_all[g + 1][:, :cw] if g < groups - 1 else edge,
                ],
                axis=1,
            )
            tall = jnp.concatenate([xs[:, o * cw:o * cw + group] for o in range(3)], axis=0)
            slabs = group // slab
            flat = jnp.concatenate([gz_all[g * slabs + u] for u in range(slabs)], axis=1)
            for r, (row_step, col_step) in enumerate(STEPS):
                mask = tap_mask(group, cw, HX, row_step, col_step)
                full_cols[r * channels:(r + 1) * channels, :] = (
                    rolled(flat, row_step * HX + col_step) * mask
                )
            total = total + matmul_nt(tall, full_cols[...])
        return total * scales[1]

    def place(ref, first_row, value):
        rows = value.shape[0]
        at = first_row
        while at < first_row + rows:
            outer, inner = divmod(at, channels)
            count = min(channels - inner, first_row + rows - at)
            for r in range(9):
                ref[outer * 9 + r, inner:inner + count, :] = value[
                    at - first_row:at - first_row + count, r * channels:(r + 1) * channels
                ]
            at += count

    @pl.when(paced)
    def _():
        column_sums()

    def hand_copy(piece, row_to):
        return put(
            collected.at[piece], collected.at[piece],
            hand_send.at[0], all_recv.at[piece], s, 2 * row_to + half,
        )

    def pass_copy(k, piece):
        return put(
            collected.at[piece], collected.at[piece],
            pass_send.at[k], all_recv.at[piece], s, partner,
        )

    def other_rows(act):
        def body(off, carry):
            act(lax.rem(row + off, columns))
            return carry

        lax.fori_loop(1, columns, body, 0)

    sums_arrived = put(
        arrived.at[pl.ds(0, columns - 1)], arrived.at[pl.ds(0, columns - 1)],
        sum_send.at[0], sum_recv.at[0], s, partner,
    )

    for k in range(2):
        @pl.when((row == first_owner + k) & paced)
        def _(k=k):
            piece = 2 * half + k
            sums_arrived.wait_recv()
            whole = arrived[0].astype(F32)
            for u in range(1, columns):
                whole = whole + arrived[u].astype(F32)
            collected[piece] = whole.astype(BF)
            other_rows(lambda u: hand_copy(piece, u).start())
            pass_copy(k, piece).start()

    def spread_copy(j, part, vol_to):
        block = collected.at[j, part_rows(part)]
        return put(block, block, spread_send.at[0], all_recv.at[j], s, vol_to)

    def whole_share(j):
        return put(
            collected.at[j], collected.at[j], spread_send.at[0], all_recv.at[j], s, partner
        )

    @pl.when(keeper & direct)
    def _():
        for part in range(PARTS):
            straight_landed(part).wait_recv()
            whole = landed[part, 0].astype(F32)
            for u in range(1, n):
                whole = whole + landed[part, u].astype(F32)
            collected[mine, part_rows(part)] = whole.astype(BF)
            far_first(lambda u, part=part: spread_copy(mine, part, u).start())

    wait_rows(2)
    place(coarse_out, 0, coarse_sums())
    coarse_store.start()

    for which in range(3):
        all_rows(which).wait_send()

    @pl.when(paced)
    def _():
        for k in range(2):
            pair_copy(k).wait_send()

            @pl.when(row != first_owner + k)
            def _(k=k):
                sum_copy(k, row, first_owner + k).wait_send()

    @pl.when(direct)
    def _():
        @pl.when(keeper)
        def _():
            block = parts.at[pl.ds(0, KEEPERS - 1)]
            put(block, block, straight_send.at[0], straight_recv.at[0], s, partner).wait_send()

        @pl.when(jnp.logical_not(keeper))
        def _():
            put(parts, parts, straight_send.at[0], straight_recv.at[0], s, partner).wait_send()

    on_left(wait_send, pre_left, x_left)
    on_right(wait_send, pre_right, x_right)

    @pl.when(s > 0)
    def _():
        on_left(wait_send, outgoing[1], outgoing[3])
        on_right(wait_send, outgoing[2], outgoing[4])
        wait_send(outgoing[0])
        wait_send(outgoing[5])

    @pl.when(paced)
    def _():
        for k in range(2):
            @pl.when(row != first_owner + k)
            def _(k=k):
                hand_copy(2 * half + k, row).wait_recv()
                pass_copy(k, 2 * half + k).start()

        for k in range(2):
            pass_copy(k, 2 * other + k).wait_recv()

    for j in range(KEEPERS):
        @pl.when(direct & (v != first_keeper + j))
        def _(j=j):
            whole_share(j).wait_recv()

        place(fine_out, j * share, collected[j].astype(F32) * scales[0])
        for outer in range(j * share // channels, ((j + 1) * share - 1) // channels + 1):
            first = max(j * share, outer * channels) - outer * channels
            stop = min((j + 1) * share, (outer + 1) * channels) - outer * channels
            fine_store(outer, first, stop).start()

    @pl.when(paced)
    def _():
        for k in range(2):
            pass_copy(k, 2 * half + k).wait_send()

            @pl.when(row == first_owner + k)
            def _(k=k):
                other_rows(lambda u: hand_copy(2 * half + k, u).wait_send())

    @pl.when(keeper & direct)
    def _():
        others(lambda u: whole_share(mine).wait_send())

    grad_store.wait()
    coarse_store.wait()
    pltpu.make_async_copy(fine_out, fine_o, store_sem.at[2]).wait()


def finish(grad, fine, coarse, grad_out, fine_out, coarse_out, sem):
    copies = [
        pltpu.make_async_copy(src, dst, sem.at[index])
        for index, (src, dst) in enumerate(
            ((fine, fine_out), (coarse, coarse_out), (grad, grad_out))
        )
    ]
    for copy in copies:
        copy.start()
    for copy in copies:
        copy.wait()


def on_device(
    cotangent, labels, class_weight, inputs, fine_pre, pooled, coarse_pre,
    fine_filters, coarse_filters,
):
    segments = lax.axis_size("segment")
    n = lax.axis_size("vol")
    channels, depth, plane = inputs.shape[1:]
    own = depth * plane
    cw = plane // 4
    cdepth = depth // 2
    slab = cdepth * cw
    reach = cdepth + 4
    row_len = pooled.shape[2] * pooled.shape[3]
    cells = own * n
    scales = (1.0 / math.sqrt(cells), 1.0 / math.sqrt(cells // 8))
    sizes = (segments, n, channels, depth, plane)
    group = min(GROUP_LANES, n * slab)
    groups = n * slab // group
    share = (3 * channels // KEEPERS, 9 * channels)
    pick_shape = (n * row_len, reach * cw)
    if math.prod(pick_shape) * 2 > PICK_BYTES:
        pick_shape = (1, 128)
    spaces = pl.BlockSpec(memory_space=pl.ANY)
    limit = min(60 * MIB, 16 * MIB + 6 * 2 * 9 * channels * (own + 2 * plane))
    hbm = pl.BlockSpec(memory_space=pltpu.HBM)
    dma = pltpu.SemaphoreType.DMA
    tap_shape = jax.ShapeDtypeStruct((TAPS, channels, channels), F32)
    grad_shape = jax.ShapeDtypeStruct((channels, depth, plane), BF)
    outs = pl.pallas_call(
        functools.partial(kernel, sizes, scales),
        out_shape=(grad_shape, tap_shape, tap_shape),
        in_specs=[hbm] * 9,
        out_specs=(spaces, spaces, spaces),
        scratch_shapes=[
            pltpu.VMEM((channels, depth, plane), BF),
            pltpu.VMEM((TAPS, channels, channels), F32),
            pltpu.VMEM((TAPS, channels, channels), F32),
            pltpu.SMEM(class_weight.shape, F32),
            pltpu.VMEM(cotangent.shape, BF),
            pltpu.VMEM(labels.shape, jnp.int32),
            pltpu.VMEM((channels, depth, plane), BF),
            pltpu.VMEM((channels, depth, plane), BF),
            pltpu.VMEM((2, TAPS, channels, channels), BF),
            pltpu.VMEM((depth, channels, plane), BF),
            pltpu.VMEM((depth, channels, plane), BF),
            pltpu.VMEM((3 * channels, 9 * channels), BF),
            pltpu.VMEM((3 * channels, 9 * channels), BF),
            pltpu.VMEM((n, channels, row_len), BF),
            pltpu.VMEM((n, channels, row_len), BF),
            pltpu.VMEM((depth + 2, channels, plane), BF),
            pltpu.VMEM((depth + 2, channels, plane), BF),
            pltpu.VMEM((depth + 2, channels, plane), BF),
            pltpu.VMEM((3, channels, slab), BF),
            pltpu.VMEM((2, channels, slab), BF),
            pltpu.VMEM((channels, reach * cw), BF),
            pltpu.VMEM(pick_shape, BF),
            pltpu.VMEM((own, slab), BF),
            pltpu.VMEM((3 * channels, own), BF),
            pltpu.VMEM((groups, channels, group), BF),
            pltpu.VMEM((9 * channels, own + 2 * plane), BF),
            pltpu.VMEM((9 * channels, reach * cw), BF),
            pltpu.VMEM((9 * channels, group), BF),
            pltpu.VMEM((n, channels, slab), BF),
            pltpu.VMEM((KEEPERS, *share), BF),
            pltpu.VMEM((PARTS, n, share[0] // PARTS, share[1]), BF),
            pltpu.VMEM((2, *share), BF),
            pltpu.VMEM((2, *share), BF),
            pltpu.VMEM((n // 2, *share), BF),
            pltpu.VMEM((KEEPERS, *share), BF),
            dma((8,)), dma((3,)), dma((3,)), dma((4,)), dma((4,)), dma((6,)), dma((6,)),
            dma((2,)), dma((2,)), dma((2,)), dma((1,)), dma((1,)), dma((2,)), dma((KEEPERS,)),
            dma((1,)), dma((PARTS,)), dma((1,)), dma((3,)),
            pltpu.SemaphoreType.REGULAR,
        ],
        compiler_params=pltpu.CompilerParams(
            collective_id=0, has_side_effects=True, vmem_limit_bytes=limit
        ),
    )(
        *(
            pltpu.with_memory_space_constraint(array, pltpu.HBM)
            for array in (
                class_weight,
                cotangent,
                labels,
                inputs[0],
                fine_pre[0],
                coarse_pre[0].reshape(channels, row_len),
                pooled[0].reshape(channels, row_len),
                fine_filters[0],
                coarse_filters[0],
            )
        )
    )

    grad, fine_grads, coarse_grads = pl.pallas_call(
        finish,
        out_shape=(grad_shape, tap_shape, tap_shape),
        in_specs=[spaces] * 3,
        out_specs=[hbm] * 3,
        scratch_shapes=[dma((3,))],
        compiler_params=pltpu.CompilerParams(vmem_limit_bytes=1024 * 1024),
    )(*outs)
    return (grad[None], fine_grads[None], coarse_grads[None])


def solution(mesh):
    return jax.shard_map(
        on_device,
        mesh=mesh,
        in_specs=(
            P(None, "vol", None),
            P("vol", None),
            P(),
            P("segment", None, "vol", None),
            P("segment", None, "vol", None),
            P("segment", None, "vol", None),
            P("segment", None, "vol", None),
            P("segment", None, None, None),
            P("segment", None, None, None),
        ),
        out_specs=(
            P("segment", None, "vol", None),
            P("segment", None, None, None),
            P("segment", None, None, None),
        ),
        check_vma=False,
    )
```

```python
import functools
import math

import jax
import jax.numpy as jnp
from jax import lax
from jax.experimental import pallas as pl
from jax.experimental.pallas import tpu as pltpu
from jax.sharding import PartitionSpec as P

XL = 16
HX = XL // 2
TAPS = 27
KEEPERS = 4
PARTS = 3
GROUP_LANES = 1024
MIB = 1024 * 1024
PICK_BYTES = 4 * MIB
BF = jnp.bfloat16
F32 = jnp.float32


def iota(shape, dim):
    return lax.broadcasted_iota(jnp.int32, shape, dim)


def matmul(a, b):
    return lax.dot_general(a, b, (((1,), (0,)), ((), ())), preferred_element_type=F32)


def matmul_nt(a, b):
    return lax.dot_general(a, b, (((1,), (1,)), ((), ())), preferred_element_type=F32)


def tap_mask(lanes, plane, columns, row_step, col_step):
    lane = iota((1, lanes), 1)
    column = lax.rem(lane, columns) - col_step
    row = lax.div(lax.rem(lane, plane), columns) - row_step
    rows = plane // columns
    inside = (column >= 0) & (column < columns) & (row >= 0) & (row < rows)
    return jnp.where(inside, 1.0, 0.0).astype(BF)


def rolled(value, shift):
    size = value.shape[1]
    shift = shift % size
    return value if shift == 0 else pltpu.roll(value, shift, 1)


STEPS = [(r, c) for r in (-1, 0, 1) for c in (-1, 0, 1)]


def kernel(
    sizes, scales,
    class_weight_h, cotangent_h, labels_h, saved_h, fine_pre_h, coarse_pre_h, pooled_h,
    fine_w_h, coarse_w_h,
    grad_o, fine_o, coarse_o,
    grad_out, fine_out, coarse_out, class_weight, cotangent, labels, saved, fine_pre, weights,
    out, seed, fine_cat, coarse_cat, pre_rows, pool_rows, pre_ext, x_ext, grad_ext, pool_ext,
    pool_out, coarse_gate, pick, pool_matrix, up_matrix, fine_x, pool_all, fine_cols, coarse_cols,
    full_cols, gz_all, parts, landed, paired, middle, arrived, collected,
    load_sem, row_send, row_recv, halo_send, halo_recv, step_send, step_recv,
    pair_send, pair_recv, sum_send, sum_recv, hand_send, pass_send, all_recv,
    straight_send, straight_recv, spread_send, store_sem, go,
):
    segments, n, channels, depth, plane = sizes
    cw = plane // 4
    cdepth = depth // 2
    own = depth * plane
    slab = cdepth * cw
    row_len = coarse_pre_h.shape[1]
    groups = pool_all.shape[0]
    group = pool_all.shape[2]
    s = lax.axis_index("segment")
    v = lax.axis_index("vol")
    has_left, has_right = v > 0, v < n - 1
    last = s == segments - 1
    late = s >= segments - 2
    paced = lax.rem(s, 2) == 1
    direct = jnp.logical_not(paced)
    half = lax.rem(v, 2)
    other = 1 - half
    partner = v + 1 - 2 * half
    row = lax.div(v, 2)
    columns = n // 2
    first_owner = columns // 2 - 1
    share = 3 * channels // KEEPERS
    rows_each = share // PARTS
    first_keeper = n // 2 - KEEPERS // 2
    mine = v - first_keeper
    keeper = (mine >= 0) & (mine < KEEPERS)

    def put(src, dst, send, recv, segment, vol):
        return pltpu.make_async_remote_copy(
            src_ref=src, dst_ref=dst, send_sem=send, recv_sem=recv,
            device_id=(segment, vol), device_id_type=pl.DeviceIdType.MESH,
        )

    def credit(segment):
        pl.semaphore_signal(
            go, inc=1, device_id=(segment, v), device_id_type=pl.DeviceIdType.MESH
        )

    barrier = pltpu.get_barrier_semaphore()

    def greet(off, carry):
        pl.semaphore_signal(
            barrier, inc=1, device_id=(s, lax.rem(v + off, n)),
            device_id_type=pl.DeviceIdType.MESH,
        )
        return carry

    lax.fori_loop(1, n, greet, 0)
    for up in (-1, 1):
        for side in (-1, 0, 1):
            there = (s + up >= 0) & (s + up < segments) & (v + side >= 0) & (v + side < n)

            @pl.when(there)
            def _(up=up, side=side):
                pl.semaphore_signal(
                    barrier, inc=1, device_id=(s + up, v + side),
                    device_id_type=pl.DeviceIdType.MESH,
                )

    def load(src, dst, index):
        return pltpu.make_async_copy(src, dst, load_sem.at[index])

    rows_load = load(coarse_pre_h, pre_rows.at[v], 0)
    pre_load = load(fine_pre_h, fine_pre, 1)
    seed_loads = (
        load(class_weight_h, class_weight, 2),
        load(cotangent_h, cotangent, 3),
        load(labels_h, labels, 4),
    )
    coarse_w_load = load(coarse_w_h, weights.at[0], 5)
    fine_w_load = load(fine_w_h, weights.at[1], 5)
    both_w_load = load(weights, weights, 5)
    saved_load = load(saved_h, saved, 6)
    pooled_load = load(pooled_h, pool_rows.at[v], 7)

    rows_load.start()

    @pl.when(last)
    def _():
        for copy in seed_loads:
            copy.start()

    for copy in (pre_load, coarse_w_load, fine_w_load, saved_load, pooled_load):
        copy.start()

    fine_lane = iota((own, 1), 0)
    pool_target = (
        lax.div(fine_lane, 2 * plane) * cw
        + lax.div(lax.rem(fine_lane, plane), 2 * XL) * HX
        + lax.div(lax.rem(fine_lane, XL), 2)
    )
    pool_matrix[...] = jnp.where(iota((own, slab), 1) == pool_target, 1.0, 0.0).astype(BF)

    up_wide = (cdepth + 2) * plane
    up_lane = iota((1, up_wide), 1)
    up_target = (
        lax.div(up_lane, plane) * cw
        + lax.div(lax.rem(up_lane, plane), 2 * XL) * HX
        + lax.div(lax.rem(up_lane, XL), 2)
    )
    up_matrix[...] = jnp.where(
        iota(((cdepth + 2) * cw, up_wide), 0) == up_target, 0.125, 0.0
    ).astype(BF)

    reach = cdepth + 4
    reach_lane = iota((1, reach * cw), 1)
    reach_depth = v * cdepth - 2 + lax.div(reach_lane, cw)
    reach_cell = reach_depth * HX + lax.rem(reach_lane, HX)
    reach_cell = jnp.where(
        (reach_depth >= 0) & (reach_depth < n * cdepth), reach_cell, -1
    )
    reach_inline = lax.div(lax.rem(reach_lane, cw), HX)
    whole_pick = pick.shape[0] > 1

    def picked(rows, u, cell, inline, lanes):
        chosen = iota((row_len, lanes), 0) == jnp.where(inline == u, cell, -1)
        return matmul(rows[u], jnp.where(chosen, 1.0, 0.0).astype(BF))

    if whole_pick:
        for u in range(n):
            chosen = iota((row_len, reach * cw), 0) == jnp.where(reach_inline == u, reach_cell, -1)
            pick[u * row_len:(u + 1) * row_len, :] = jnp.where(chosen, 1.0, 0.0).astype(BF)

    def step_copies(src, turn, segment):
        def step(which, a, b, vol):
            return put(a, b, step_send.at[which], step_recv.at[which], segment, vol)

        block = pool_out.at[turn]
        return (
            step(0, block, pool_ext.at[1], v),
            step(1, block, pool_ext.at[2], v - 1),
            step(2, block, pool_ext.at[0], v + 1),
            step(3, src.at[0], grad_ext.at[depth + 1], v - 1),
            step(4, src.at[depth - 1], grad_ext.at[0], v + 1),
            step(5, src, grad_ext.at[1:depth + 1], v),
            step(5, src.at[0], grad_ext.at[1], v),
            step(5, src.at[1:depth], grad_ext.at[2:depth + 1], v),
        )

    def on_left(act, *copies):
        @pl.when(has_left)
        def _():
            for copy in copies:
                act(copy)

    def on_right(act, *copies):
        @pl.when(has_right)
        def _():
            for copy in copies:
                act(copy)

    def start(copy):
        copy.start()

    def wait_send(copy):
        copy.wait_send()

    def wait_recv(copy):
        copy.wait_recv()

    def pool_of(ref):
        flat = jnp.concatenate([ref[p] for p in range(depth)], axis=1)
        return matmul(flat, pool_matrix[...]).astype(BF)

    @pl.when(last)
    def _():
        for copy in seed_loads:
            copy.wait()
        planes = jnp.swapaxes(cotangent[...], 0, 1)
        for p in range(depth):
            label = labels[p:p + 1, :]
            weight = jnp.zeros(label.shape, F32)
            for index in range(class_weight.shape[0]):
                weight = weight + jnp.where(label == index, class_weight[index], 0.0)
            block = (planes[p].astype(F32) * weight).astype(BF)
            seed[p] = block
            grad_ext[p + 1] = block
        pool_out[0] = pool_of(seed)
        pool_ext[1] = pool_out[0]

    pre_load.wait()
    pre_ext[1:depth + 1] = jnp.swapaxes(fine_pre[...], 0, 1)
    both_w_load.wait()
    for k in range(TAPS):
        rows = slice(k // 9 * channels, (k // 9 + 1) * channels)
        lanes = slice(k % 9 * channels, (k % 9 + 1) * channels)
        coarse_cat[rows, lanes] = weights[0, k]
        fine_cat[rows, lanes] = weights[1, k]
    saved_load.wait()
    x_ext[1:depth + 1] = jnp.swapaxes(saved[...], 0, 1)

    @pl.when(v == 0)
    def _():
        pre_ext[0] = jnp.zeros((channels, plane), BF)
        x_ext[0] = jnp.zeros((channels, plane), BF)
        grad_ext[0] = jnp.zeros((channels, plane), BF)
        pool_ext[0] = jnp.zeros(pool_ext.shape[1:], BF)

    @pl.when(v == n - 1)
    def _():
        pre_ext[depth + 1] = jnp.zeros((channels, plane), BF)
        x_ext[depth + 1] = jnp.zeros((channels, plane), BF)
        grad_ext[depth + 1] = jnp.zeros((channels, plane), BF)
        pool_ext[2] = jnp.zeros(pool_ext.shape[1:], BF)

    rows_load.wait()
    pooled_load.wait()

    ups = jnp.where(s > 0, 1, 0) + jnp.where(last, 0, 1)
    sides = 1 + jnp.where(has_left, 1, 0) + jnp.where(has_right, 1, 0)
    pl.semaphore_wait(barrier, n - 1 + ups * sides)

    def halo(ref, index):
        return (
            put(ref.at[1], ref.at[depth + 1], halo_send.at[index], halo_recv.at[index], s, v - 1),
            put(
                ref.at[depth], ref.at[0],
                halo_send.at[index + 1], halo_recv.at[index + 1], s, v + 1,
            ),
        )

    pre_left, pre_right = halo(pre_ext, 0)
    x_left, x_right = halo(x_ext, 2)

    def far_first(act):
        def body(step, carry):
            for u in (v + n - step, v - n + step):
                @pl.when((u >= 0) & (u < n))
                def _(u=u):
                    act(u)

            return carry

        lax.fori_loop(1, n, body, 0)

    def in_order(act):
        def body(u, carry):
            @pl.when(u != v)
            def _():
                act(u)

            return carry

        lax.fori_loop(0, n, body, 0)

    def others(act):
        def body(off, carry):
            act(lax.rem(v + off, n))
            return carry

        lax.fori_loop(1, n, body, 0)

    def row_copy(which, source, target):
        ref = (pre_rows, pool_rows, gz_all)[which]
        return put(
            ref.at[source], ref.at[source], row_send.at[which], row_recv.at[which], s, target
        )

    def all_rows(which):
        ref = (pre_rows, pool_rows, gz_all)[which].at[pl.ds(0, n - 1)]
        return put(ref, ref, row_send.at[which], row_recv.at[which], s, partner)

    def send_rows(which):
        far_first(lambda u: row_copy(which, v, u).start())

    def send_gz():
        for off in range(1, n):
            row_copy(2, v, lax.rem(v + off, n)).start()

    def wait_rows(which):
        all_rows(which).wait_recv()

    @pl.when(last)
    def _():
        copies = step_copies(seed, 0, s)
        on_left(start, copies[1])
        on_right(start, copies[2])
        send_rows(0)
        on_left(start, copies[3], pre_left)
        on_right(start, copies[4], pre_right)

    @pl.when(jnp.logical_not(last))
    def _():
        @pl.when(s == segments - 2)
        def _():
            pl.semaphore_wait(go, 1)

        send_rows(0)
        on_left(start, pre_left)
        on_right(start, pre_right)

    @pl.when(jnp.logical_not(late))
    def _():
        on_left(start, x_left)
        on_right(start, x_right)

    wait_rows(0)

    @pl.when(last)
    def _():
        credit(s - 1)

    if whole_pick:
        flat_rows = jnp.concatenate([pre_rows[u] for u in range(n)], axis=1)
        coarse_gate[...] = matmul(flat_rows, pick[...]).astype(BF)
    else:
        coarse_gate[...] = lax.fori_loop(
            0, n,
            lambda u, total: total + picked(
                pre_rows, u, reach_cell, reach_inline, reach * cw
            ),
            jnp.zeros((channels, reach * cw), F32),
        ).astype(BF)

    def take_pooled():
        wait_rows(1)
        lane = iota((1, group), 1)
        inline = lax.div(lax.rem(lane, cw), HX)

        def body(g, carry):
            cell = (g * (group // cw) + lax.div(lane, cw)) * HX + lax.rem(lane, HX)
            pool_all[g] = lax.fori_loop(
                0, n,
                lambda u, total: total + picked(pool_rows, u, cell, inline, group),
                jnp.zeros((channels, group), F32),
            ).astype(BF)
            return carry

        lax.fori_loop(0, groups, body, 0)

    def take_fine_x():
        for outer in range(3):
            for p in range(depth):
                fine_x[outer * channels:(outer + 1) * channels, p * plane:(p + 1) * plane] = (
                    x_ext[p + outer]
                )

    @pl.when(jnp.logical_not(late))
    def _():
        send_rows(1)
        take_pooled()

    @pl.when(jnp.logical_not(late))
    def _():
        on_left(wait_recv, x_right)
        on_right(wait_recv, x_left)
        take_fine_x()

    incoming = step_copies(out, 1, s)

    on_left(wait_recv, incoming[2])
    on_right(wait_recv, incoming[1])

    @pl.when(jnp.logical_not(last))
    def _():
        incoming[0].wait_recv()

    @pl.when(s == segments - 2)
    def _():
        credit(s + 1)

    side = pool_ext.shape[2]
    near = jnp.concatenate(
        [pool_ext[0][:, side - 2 * cw:], pool_ext[1], pool_ext[2][:, :2 * cw]], axis=1
    )
    coarse_gz = jnp.where(coarse_gate[...] > 0, near, jnp.zeros_like(near))
    gz_all[v] = coarse_gz[:, 2 * cw:2 * cw + slab]
    for r, (row_step, col_step) in enumerate(STEPS):
        mask = tap_mask(reach * cw, cw, HX, row_step, col_step)
        coarse_cols[r * channels:(r + 1) * channels, :] = (
            rolled(coarse_gz, row_step * HX + col_step) * mask
        )

    terms = matmul(coarse_cat[...], coarse_cols[...])
    width = (cdepth + 2) * cw
    coarse_back = sum(
        terms[outer * channels:(outer + 1) * channels, (2 - outer) * cw:(2 - outer) * cw + width]
        for outer in range(3)
    ).astype(BF)

    spread = matmul(coarse_back, up_matrix[...])
    pieces = [
        spread[:, (p + 1) // 2 * plane:((p + 1) // 2 + 1) * plane] for p in range(depth + 2)
    ]

    on_left(wait_recv, pre_right, incoming[4])
    on_right(wait_recv, pre_left, incoming[3])

    @pl.when(jnp.logical_not(last))
    def _():
        incoming[5].wait_recv()

    @pl.when(jnp.logical_not(late) & (s > 0))
    def _():
        send_gz()

    def take_cols():
        masks = [tap_mask(plane, plane, XL, *step) for step in STEPS]
        for p in range(depth + 2):
            grad = grad_ext[p].astype(F32) + pieces[p]
            gz = jnp.where(pre_ext[p].astype(F32) > 0, grad, 0.0).astype(BF)
            for r, (row_step, col_step) in enumerate(STEPS):
                fine_cols[r * channels:(r + 1) * channels, p * plane:(p + 1) * plane] = (
                    rolled(gz, row_step * XL + col_step) * masks[r]
                )

    def take_out():
        terms = matmul(fine_cat[...], fine_cols[...])
        for p in range(depth):
            total = grad_ext[p + 1].astype(F32)
            for outer in range(3):
                total = total + terms[
                    outer * channels:(outer + 1) * channels,
                    (p + 2 - outer) * plane:(p + 3 - outer) * plane,
                ]
            out[p] = total.astype(BF)

    def pair_copy(k):
        return put(
            parts.at[2 * other + k], paired.at[k], pair_send.at[k], pair_recv.at[k], s, partner
        )

    def sum_copy(k, row_from, row_to):
        return put(
            middle.at[k], arrived.at[row_from],
            sum_send.at[k], sum_recv.at[0], s, 2 * row_to + half,
        )

    def fine_sums(first, count):
        rows = slice(first * share, (first + count) * share)
        grads = matmul_nt(fine_x[rows, :], fine_cols[:, plane:plane + own]).astype(BF)
        for j in range(count):
            parts[first + j] = grads[j * share:(j + 1) * share, :]

    def pair_sends():
        for k in range(2):
            pair_copy(k).start()

    def part_rows(part):
        return pl.ds(part * rows_each, rows_each)

    def straight_copy(j, part, vol_to):
        return put(
            parts.at[j, part_rows(part)], landed.at[part, v],
            straight_send.at[0], straight_recv.at[part], s, vol_to,
        )

    def straight_landed(part):
        block = landed.at[part, pl.ds(0, n - 1)]
        return put(block, block, straight_send.at[0], straight_recv.at[part], s, partner)

    def straight_sums():
        fine_sums(0, KEEPERS)

        def send(order):
            for part in range(PARTS):
                for j in order:
                    @pl.when(v != first_keeper + j)
                    def _(j=j, part=part):
                        straight_copy(j, part, first_keeper + j).start()

        @pl.when(v < n // 2)
        def _():
            send(range(KEEPERS - 1, -1, -1))

        @pl.when(v >= n // 2)
        def _():
            send(range(KEEPERS))

        @pl.when((mine >= 0) & (mine < KEEPERS))
        def _():
            for part in range(PARTS):
                landed[part, v] = parts[mine, part_rows(part)]

    def column_sums():
        for k in range(2):
            pair_copy(k).wait_recv()
            both = parts[2 * half + k].astype(F32) + paired[k].astype(F32)
            middle[k] = both.astype(BF)

            @pl.when(row != first_owner + k)
            def _(k=k):
                sum_copy(k, row, first_owner + k).start()

            @pl.when(row == first_owner + k)
            def _(k=k):
                arrived[row] = middle[k]

    @pl.when(s == 0)
    def _():
        take_cols()
        straight_sums()
        send_gz()
        take_out()

    outgoing = step_copies(out, 1, s - 1)

    @pl.when(last)
    def _():
        copies = step_copies(seed, 0, s)
        on_left(wait_send, copies[1], copies[3])
        on_right(wait_send, copies[2], copies[4])

    @pl.when(s > 0)
    def _():
        take_cols()
        take_out()
        outgoing[6].start()
        pool_out[1] = pool_of(out)
        on_left(start, outgoing[1])
        on_right(start, outgoing[2])
        outgoing[0].start()
        on_left(start, outgoing[3])
        on_right(start, outgoing[4])
        outgoing[7].start()

    @pl.when(last)
    def _():
        pl.semaphore_wait(go, 1)

    @pl.when(late)
    def _():
        on_left(start, x_left)
        on_right(start, x_right)
        send_rows(1)

    @pl.when(late)
    def _():
        take_pooled()
        on_left(wait_recv, x_right)
        on_right(wait_recv, x_left)
        take_fine_x()

    @pl.when(late)
    def _():
        send_gz()

    @pl.when(s > 0)
    def _():
        @pl.when(paced)
        def _():
            fine_sums(0, KEEPERS)
            pair_sends()

        @pl.when(direct)
        def _():
            straight_sums()

    grad_store = pltpu.make_async_copy(grad_out, grad_o, store_sem.at[0])
    coarse_store = pltpu.make_async_copy(coarse_out, coarse_o, store_sem.at[1])

    def fine_store(outer, first, stop):
        at = (slice(outer * 9, (outer + 1) * 9), slice(first, stop))
        return pltpu.make_async_copy(fine_out.at[at], fine_o.at[at], store_sem.at[2])

    grad_out[...] = jnp.swapaxes(out[...], 0, 1)
    grad_store.start()

    def coarse_sums():
        total = jnp.zeros((3 * channels, 9 * channels), F32)
        edge = jnp.zeros((channels, cw), BF)
        for g in range(groups):
            xs = jnp.concatenate(
                [
                    pool_all[g - 1][:, group - cw:] if g else edge,
                    pool_all[g],
                    pool_all[g + 1][:, :cw] if g < groups - 1 else edge,
                ],
                axis=1,
            )
            tall = jnp.concatenate([xs[:, o * cw:o * cw + group] for o in range(3)], axis=0)
            slabs = group // slab
            flat = jnp.concatenate([gz_all[g * slabs + u] for u in range(slabs)], axis=1)
            for r, (row_step, col_step) in enumerate(STEPS):
                mask = tap_mask(group, cw, HX, row_step, col_step)
                full_cols[r * channels:(r + 1) * channels, :] = (
                    rolled(flat, row_step * HX + col_step) * mask
                )
            total = total + matmul_nt(tall, full_cols[...])
        return total * scales[1]

    def place(ref, first_row, value):
        rows = value.shape[0]
        at = first_row
        while at < first_row + rows:
            outer, inner = divmod(at, channels)
            count = min(channels - inner, first_row + rows - at)
            for r in range(9):
                ref[outer * 9 + r, inner:inner + count, :] = value[
                    at - first_row:at - first_row + count, r * channels:(r + 1) * channels
                ]
            at += count

    @pl.when(paced)
    def _():
        column_sums()

    def hand_copy(piece, row_to):
        return put(
            collected.at[piece], collected.at[piece],
            hand_send.at[0], all_recv.at[piece], s, 2 * row_to + half,
        )

    def pass_copy(k, piece):
        return put(
            collected.at[piece], collected.at[piece],
            pass_send.at[k], all_recv.at[piece], s, partner,
        )

    def other_rows(act):
        def body(off, carry):
            act(lax.rem(row + off, columns))
            return carry

        lax.fori_loop(1, columns, body, 0)

    sums_arrived = put(
        arrived.at[pl.ds(0, columns - 1)], arrived.at[pl.ds(0, columns - 1)],
        sum_send.at[0], sum_recv.at[0], s, partner,
    )

    for k in range(2):
        @pl.when((row == first_owner + k) & paced)
        def _(k=k):
            piece = 2 * half + k
            sums_arrived.wait_recv()
            whole = arrived[0].astype(F32)
            for u in range(1, columns):
                whole = whole + arrived[u].astype(F32)
            collected[piece] = whole.astype(BF)
            other_rows(lambda u: hand_copy(piece, u).start())
            pass_copy(k, piece).start()

    def spread_copy(j, part, vol_to):
        block = collected.at[j, part_rows(part)]
        return put(block, block, spread_send.at[0], all_recv.at[j], s, vol_to)

    def whole_share(j):
        return put(
            collected.at[j], collected.at[j], spread_send.at[0], all_recv.at[j], s, partner
        )

    @pl.when(keeper & direct)
    def _():
        for part in range(PARTS):
            straight_landed(part).wait_recv()
            whole = landed[part, 0].astype(F32)
            for u in range(1, n):
                whole = whole + landed[part, u].astype(F32)
            collected[mine, part_rows(part)] = whole.astype(BF)
            in_order(lambda u, part=part: spread_copy(mine, part, u).start())

    wait_rows(2)
    place(coarse_out, 0, coarse_sums())
    coarse_store.start()

    for which in range(3):
        all_rows(which).wait_send()

    @pl.when(paced)
    def _():
        for k in range(2):
            pair_copy(k).wait_send()

            @pl.when(row != first_owner + k)
            def _(k=k):
                sum_copy(k, row, first_owner + k).wait_send()

    @pl.when(direct)
    def _():
        @pl.when(keeper)
        def _():
            block = parts.at[pl.ds(0, KEEPERS - 1)]
            put(block, block, straight_send.at[0], straight_recv.at[0], s, partner).wait_send()

        @pl.when(jnp.logical_not(keeper))
        def _():
            put(parts, parts, straight_send.at[0], straight_recv.at[0], s, partner).wait_send()

    on_left(wait_send, pre_left, x_left)
    on_right(wait_send, pre_right, x_right)

    @pl.when(s > 0)
    def _():
        on_left(wait_send, outgoing[1], outgoing[3])
        on_right(wait_send, outgoing[2], outgoing[4])
        wait_send(outgoing[0])
        wait_send(outgoing[5])

    @pl.when(paced)
    def _():
        for k in range(2):
            @pl.when(row != first_owner + k)
            def _(k=k):
                hand_copy(2 * half + k, row).wait_recv()
                pass_copy(k, 2 * half + k).start()

        for k in range(2):
            pass_copy(k, 2 * other + k).wait_recv()

    for j in range(KEEPERS):
        @pl.when(direct & (v != first_keeper + j))
        def _(j=j):
            whole_share(j).wait_recv()

        place(fine_out, j * share, collected[j].astype(F32) * scales[0])
        for outer in range(j * share // channels, ((j + 1) * share - 1) // channels + 1):
            first = max(j * share, outer * channels) - outer * channels
            stop = min((j + 1) * share, (outer + 1) * channels) - outer * channels
            fine_store(outer, first, stop).start()

    @pl.when(paced)
    def _():
        for k in range(2):
            pass_copy(k, 2 * half + k).wait_send()

            @pl.when(row == first_owner + k)
            def _(k=k):
                other_rows(lambda u: hand_copy(2 * half + k, u).wait_send())

    @pl.when(keeper & direct)
    def _():
        others(lambda u: whole_share(mine).wait_send())

    grad_store.wait()
    coarse_store.wait()
    pltpu.make_async_copy(fine_out, fine_o, store_sem.at[2]).wait()


def finish(grad, fine, coarse, grad_out, fine_out, coarse_out, sem):
    copies = [
        pltpu.make_async_copy(src, dst, sem.at[index])
        for index, (src, dst) in enumerate(
            ((fine, fine_out), (coarse, coarse_out), (grad, grad_out))
        )
    ]
    for copy in copies:
        copy.start()
    for copy in copies:
        copy.wait()


def on_device(
    cotangent, labels, class_weight, inputs, fine_pre, pooled, coarse_pre,
    fine_filters, coarse_filters,
):
    segments = lax.axis_size("segment")
    n = lax.axis_size("vol")
    channels, depth, plane = inputs.shape[1:]
    own = depth * plane
    cw = plane // 4
    cdepth = depth // 2
    slab = cdepth * cw
    reach = cdepth + 4
    row_len = pooled.shape[2] * pooled.shape[3]
    cells = own * n
    scales = (1.0 / math.sqrt(cells), 1.0 / math.sqrt(cells // 8))
    sizes = (segments, n, channels, depth, plane)
    group = min(GROUP_LANES, n * slab)
    groups = n * slab // group
    share = (3 * channels // KEEPERS, 9 * channels)
    pick_shape = (n * row_len, reach * cw)
    if math.prod(pick_shape) * 2 > PICK_BYTES:
        pick_shape = (1, 128)
    spaces = pl.BlockSpec(memory_space=pl.ANY)
    limit = min(60 * MIB, 16 * MIB + 6 * 2 * 9 * channels * (own + 2 * plane))
    hbm = pl.BlockSpec(memory_space=pltpu.HBM)
    dma = pltpu.SemaphoreType.DMA
    tap_shape = jax.ShapeDtypeStruct((TAPS, channels, channels), F32)
    grad_shape = jax.ShapeDtypeStruct((channels, depth, plane), BF)
    outs = pl.pallas_call(
        functools.partial(kernel, sizes, scales),
        out_shape=(grad_shape, tap_shape, tap_shape),
        in_specs=[hbm] * 9,
        out_specs=(spaces, spaces, spaces),
        scratch_shapes=[
            pltpu.VMEM((channels, depth, plane), BF),
            pltpu.VMEM((TAPS, channels, channels), F32),
            pltpu.VMEM((TAPS, channels, channels), F32),
            pltpu.SMEM(class_weight.shape, F32),
            pltpu.VMEM(cotangent.shape, BF),
            pltpu.VMEM(labels.shape, jnp.int32),
            pltpu.VMEM((channels, depth, plane), BF),
            pltpu.VMEM((channels, depth, plane), BF),
            pltpu.VMEM((2, TAPS, channels, channels), BF),
            pltpu.VMEM((depth, channels, plane), BF),
            pltpu.VMEM((depth, channels, plane), BF),
            pltpu.VMEM((3 * channels, 9 * channels), BF),
            pltpu.VMEM((3 * channels, 9 * channels), BF),
            pltpu.VMEM((n, channels, row_len), BF),
            pltpu.VMEM((n, channels, row_len), BF),
            pltpu.VMEM((depth + 2, channels, plane), BF),
            pltpu.VMEM((depth + 2, channels, plane), BF),
            pltpu.VMEM((depth + 2, channels, plane), BF),
            pltpu.VMEM((3, channels, slab), BF),
            pltpu.VMEM((2, channels, slab), BF),
            pltpu.VMEM((channels, reach * cw), BF),
            pltpu.VMEM(pick_shape, BF),
            pltpu.VMEM((own, slab), BF),
            pltpu.VMEM(((cdepth + 2) * cw, (cdepth + 2) * plane), BF),
            pltpu.VMEM((3 * channels, own), BF),
            pltpu.VMEM((groups, channels, group), BF),
            pltpu.VMEM((9 * channels, own + 2 * plane), BF),
            pltpu.VMEM((9 * channels, reach * cw), BF),
            pltpu.VMEM((9 * channels, group), BF),
            pltpu.VMEM((n, channels, slab), BF),
            pltpu.VMEM((KEEPERS, *share), BF),
            pltpu.VMEM((PARTS, n, share[0] // PARTS, share[1]), BF),
            pltpu.VMEM((2, *share), BF),
            pltpu.VMEM((2, *share), BF),
            pltpu.VMEM((n // 2, *share), BF),
            pltpu.VMEM((KEEPERS, *share), BF),
            dma((8,)), dma((3,)), dma((3,)), dma((4,)), dma((4,)), dma((6,)), dma((6,)),
            dma((2,)), dma((2,)), dma((2,)), dma((1,)), dma((1,)), dma((2,)), dma((KEEPERS,)),
            dma((1,)), dma((PARTS,)), dma((1,)), dma((3,)),
            pltpu.SemaphoreType.REGULAR,
        ],
        compiler_params=pltpu.CompilerParams(
            collective_id=0, has_side_effects=True, vmem_limit_bytes=limit
        ),
    )(
        *(
            pltpu.with_memory_space_constraint(array, pltpu.HBM)
            for array in (
                class_weight,
                cotangent,
                labels,
                inputs[0],
                fine_pre[0],
                coarse_pre[0].reshape(channels, row_len),
                pooled[0].reshape(channels, row_len),
                fine_filters[0],
                coarse_filters[0],
            )
        )
    )

    grad, fine_grads, coarse_grads = pl.pallas_call(
        finish,
        out_shape=(grad_shape, tap_shape, tap_shape),
        in_specs=[spaces] * 3,
        out_specs=[hbm] * 3,
        scratch_shapes=[dma((3,))],
        compiler_params=pltpu.CompilerParams(vmem_limit_bytes=1024 * 1024),
    )(*outs)
    return (grad[None], fine_grads[None], coarse_grads[None])


def solution(mesh):
    return jax.shard_map(
        on_device,
        mesh=mesh,
        in_specs=(
            P(None, "vol", None),
            P("vol", None),
            P(),
            P("segment", None, "vol", None),
            P("segment", None, "vol", None),
            P("segment", None, "vol", None),
            P("segment", None, "vol", None),
            P("segment", None, None, None),
            P("segment", None, None, None),
        ),
        out_specs=(
            P("segment", None, "vol", None),
            P("segment", None, None, None),
            P("segment", None, None, None),
        ),
        check_vma=False,
    )
```

```python
import functools
import math

import jax
import jax.numpy as jnp
from jax import lax
from jax.experimental import pallas as pl
from jax.experimental.pallas import tpu as pltpu
from jax.sharding import PartitionSpec as P

XL = 16
HX = XL // 2
TAPS = 27
KEEPERS = 4
PARTS = 3
GROUP_LANES = 1024
MIB = 1024 * 1024
PICK_BYTES = 4 * MIB
BF = jnp.bfloat16
F32 = jnp.float32


def iota(shape, dim):
    return lax.broadcasted_iota(jnp.int32, shape, dim)


def matmul(a, b):
    return lax.dot_general(a, b, (((1,), (0,)), ((), ())), preferred_element_type=F32)


def matmul_nt(a, b):
    return lax.dot_general(a, b, (((1,), (1,)), ((), ())), preferred_element_type=F32)


def tap_mask(lanes, plane, columns, row_step, col_step):
    lane = iota((1, lanes), 1)
    column = lax.rem(lane, columns) - col_step
    row = lax.div(lax.rem(lane, plane), columns) - row_step
    rows = plane // columns
    inside = (column >= 0) & (column < columns) & (row >= 0) & (row < rows)
    return jnp.where(inside, 1.0, 0.0).astype(BF)


def rolled(value, shift):
    size = value.shape[1]
    shift = shift % size
    return value if shift == 0 else pltpu.roll(value, shift, 1)


STEPS = [(r, c) for r in (-1, 0, 1) for c in (-1, 0, 1)]


def kernel(
    sizes, scales,
    class_weight_h, cotangent_h, labels_h, saved_h, fine_pre_h, coarse_pre_h, pooled_h,
    fine_w_h, coarse_w_h,
    grad_o, fine_o, coarse_o,
    grad_out, fine_out, coarse_out, class_weight, cotangent, labels, saved, fine_pre, weights,
    out, seed, fine_cat, coarse_cat, own_rows, to_send, pre_rows, pool_rows, pre_ext, x_ext, grad_ext, pool_ext,
    pool_out, coarse_gate, pick, pool_matrix, up_matrix, fine_x, pool_all, fine_cols, coarse_cols,
    full_cols, gz_all, parts, landed, paired, middle, arrived, collected,
    load_sem, row_send, row_recv, halo_send, halo_recv, step_send, step_recv,
    pair_send, pair_recv, sum_send, sum_recv, hand_send, pass_send, all_recv,
    straight_send, straight_recv, spread_send, store_sem, go,
):
    segments, n, channels, depth, plane = sizes
    cw = plane // 4
    cdepth = depth // 2
    own = depth * plane
    slab = cdepth * cw
    row_len = coarse_pre_h.shape[1]
    groups = pool_all.shape[0]
    group = pool_all.shape[2]
    s = lax.axis_index("segment")
    v = lax.axis_index("vol")
    has_left, has_right = v > 0, v < n - 1
    last = s == segments - 1
    late = s >= segments - 2
    paced = lax.rem(s, 2) == 1
    direct = jnp.logical_not(paced)
    half = lax.rem(v, 2)
    other = 1 - half
    partner = v + 1 - 2 * half
    row = lax.div(v, 2)
    columns = n // 2
    first_owner = columns // 2 - 1
    share = channels // KEEPERS
    tiles = parts.shape[2] // 128
    cuts = [128 * (tiles * part // PARTS) for part in range(PARTS + 1)]
    first_keeper = n // 2 - KEEPERS // 2
    mine = v - first_keeper
    keeper = (mine >= 0) & (mine < KEEPERS)

    def put(src, dst, send, recv, segment, vol):
        return pltpu.make_async_remote_copy(
            src_ref=src, dst_ref=dst, send_sem=send, recv_sem=recv,
            device_id=(segment, vol), device_id_type=pl.DeviceIdType.MESH,
        )

    def credit(segment):
        pl.semaphore_signal(
            go, inc=1, device_id=(segment, v), device_id_type=pl.DeviceIdType.MESH
        )

    barrier = pltpu.get_barrier_semaphore()

    def greet(off, carry):
        pl.semaphore_signal(
            barrier, inc=1, device_id=(s, lax.rem(v + off, n)),
            device_id_type=pl.DeviceIdType.MESH,
        )
        return carry

    lax.fori_loop(1, n, greet, 0)
    for up in (-1, 1):
        for side in (-1, 0, 1):
            there = (s + up >= 0) & (s + up < segments) & (v + side >= 0) & (v + side < n)

            @pl.when(there)
            def _(up=up, side=side):
                pl.semaphore_signal(
                    barrier, inc=1, device_id=(s + up, v + side),
                    device_id_type=pl.DeviceIdType.MESH,
                )

    def load(src, dst, index):
        return pltpu.make_async_copy(src, dst, load_sem.at[index])

    compact = pick.shape[0] > 1
    rows_load = load(coarse_pre_h, own_rows if compact else pre_rows.at[v], 0)
    pre_load = load(fine_pre_h, fine_pre, 1)
    seed_loads = (
        load(class_weight_h, class_weight, 2),
        load(cotangent_h, cotangent, 3),
        load(labels_h, labels, 4),
    )
    coarse_w_load = load(coarse_w_h, weights.at[0], 5)
    fine_w_load = load(fine_w_h, weights.at[1], 5)
    both_w_load = load(weights, weights, 5)
    saved_load = load(saved_h, saved, 6)
    pooled_load = load(pooled_h, pool_rows.at[v], 7)

    rows_load.start()

    @pl.when(last)
    def _():
        for copy in seed_loads:
            copy.start()

    for copy in (pre_load, coarse_w_load, fine_w_load, saved_load, pooled_load):
        copy.start()

    fine_lane = iota((own, 1), 0)
    pool_target = (
        lax.div(fine_lane, 2 * plane) * cw
        + lax.div(lax.rem(fine_lane, plane), 2 * XL) * HX
        + lax.div(lax.rem(fine_lane, XL), 2)
    )
    pool_matrix[...] = jnp.where(iota((own, slab), 1) == pool_target, 1.0, 0.0).astype(BF)

    reach = cdepth + 4
    reach_lane = iota((1, reach * cw), 1)
    reach_depth = v * cdepth - 2 + lax.div(reach_lane, cw)
    reach_cell = reach_depth * HX + lax.rem(reach_lane, HX)
    reach_cell = jnp.where(
        (reach_depth >= 0) & (reach_depth < n * cdepth), reach_cell, -1
    )
    reach_inline = lax.div(lax.rem(reach_lane, cw), HX)

    def picked(rows, u, cell, inline, lanes):
        chosen = iota((row_len, lanes), 0) == jnp.where(inline == u, cell, -1)
        return matmul(rows[u], jnp.where(chosen, 1.0, 0.0).astype(BF))

    small = channels // 2
    if compact:
        to_lane = iota((1, n * 128), 1)
        to_cell = lax.rem(to_lane, 128 // 2)
        to_depth = lax.div(to_lane, 128) * cdepth - 2 + lax.div(to_cell, HX)
        to_row = (
            lax.div(lax.rem(to_lane, 128), 128 // 2) * row_len
            + to_depth * HX + lax.rem(to_cell, HX)
        )
        inside = (to_depth >= 0) & (to_depth < n * cdepth) & (to_cell < reach * HX)
        to_row = jnp.where(inside, to_row, -1)
        split = jnp.where(iota((2 * row_len, n * 128), 0) == to_row, 1.0, 0.0).astype(BF)

    def step_copies(src, turn, segment):
        def step(which, a, b, vol):
            return put(a, b, step_send.at[which], step_recv.at[which], segment, vol)

        block = pool_out.at[turn]
        return (
            step(0, block, pool_ext.at[1], v),
            step(1, block, pool_ext.at[2], v - 1),
            step(2, block, pool_ext.at[0], v + 1),
            step(3, src.at[0], grad_ext.at[depth + 1], v - 1),
            step(4, src.at[depth - 1], grad_ext.at[0], v + 1),
            step(5, src, grad_ext.at[1:depth + 1], v),
            step(5, src.at[0], grad_ext.at[1], v),
            step(5, src.at[1:depth], grad_ext.at[2:depth + 1], v),
        )

    def on_left(act, *copies):
        @pl.when(has_left)
        def _():
            for copy in copies:
                act(copy)

    def on_right(act, *copies):
        @pl.when(has_right)
        def _():
            for copy in copies:
                act(copy)

    def start(copy):
        copy.start()

    def wait_send(copy):
        copy.wait_send()

    def wait_recv(copy):
        copy.wait_recv()

    def pool_of(ref):
        flat = jnp.concatenate([ref[p] for p in range(depth)], axis=1)
        return matmul(flat, pool_matrix[...]).astype(BF)

    @pl.when(last)
    def _():
        for copy in seed_loads:
            copy.wait()
        planes = jnp.swapaxes(cotangent[...], 0, 1)
        for p in range(depth):
            label = labels[p:p + 1, :]
            weight = jnp.zeros(label.shape, F32)
            for index in range(class_weight.shape[0]):
                weight = weight + jnp.where(label == index, class_weight[index], 0.0)
            block = (planes[p].astype(F32) * weight).astype(BF)
            seed[p] = block
            grad_ext[p + 1] = block
        pool_out[0] = pool_of(seed)
        pool_ext[1] = pool_out[0]

    pre_load.wait()
    pre_ext[1:depth + 1] = jnp.swapaxes(fine_pre[...], 0, 1)
    both_w_load.wait()
    for k in range(TAPS):
        rows = slice(k // 9 * channels, (k // 9 + 1) * channels)
        lanes = slice(k % 9 * channels, (k % 9 + 1) * channels)
        coarse_cat[rows, lanes] = weights[0, k]
        fine_cat[rows, lanes] = weights[1, k]
    saved_load.wait()
    x_ext[1:depth + 1] = jnp.swapaxes(saved[...], 0, 1)

    @pl.when(v == 0)
    def _():
        pre_ext[0] = jnp.zeros((channels, plane), BF)
        x_ext[0] = jnp.zeros((channels, plane), BF)
        grad_ext[0] = jnp.zeros((channels, plane), BF)
        pool_ext[0] = jnp.zeros(pool_ext.shape[1:], BF)

    @pl.when(v == n - 1)
    def _():
        pre_ext[depth + 1] = jnp.zeros((channels, plane), BF)
        x_ext[depth + 1] = jnp.zeros((channels, plane), BF)
        grad_ext[depth + 1] = jnp.zeros((channels, plane), BF)
        pool_ext[2] = jnp.zeros(pool_ext.shape[1:], BF)

    rows_load.wait()
    pooled_load.wait()
    if compact:
        halves = jnp.concatenate([own_rows[:small, :], own_rows[small:, :]], axis=1)
        blocks = matmul(halves, split).astype(BF)
        for u in range(n):
            to_send[u] = blocks[:, u * 128:(u + 1) * 128]
        pre_rows[v] = to_send[v]

    ups = jnp.where(s > 0, 1, 0) + jnp.where(last, 0, 1)
    sides = 1 + jnp.where(has_left, 1, 0) + jnp.where(has_right, 1, 0)
    pl.semaphore_wait(barrier, n - 1 + ups * sides)

    def halo(ref, index):
        return (
            put(ref.at[1], ref.at[depth + 1], halo_send.at[index], halo_recv.at[index], s, v - 1),
            put(
                ref.at[depth], ref.at[0],
                halo_send.at[index + 1], halo_recv.at[index + 1], s, v + 1,
            ),
        )

    pre_left, pre_right = halo(pre_ext, 0)
    x_left, x_right = halo(x_ext, 2)

    def far_first(act):
        def body(step, carry):
            for u in (v + n - step, v - n + step):
                @pl.when((u >= 0) & (u < n))
                def _(u=u):
                    act(u)

            return carry

        lax.fori_loop(1, n, body, 0)

    def in_order(act):
        def body(u, carry):
            @pl.when(u != v)
            def _():
                act(u)

            return carry

        lax.fori_loop(0, n, body, 0)

    def others(act):
        def body(off, carry):
            act(lax.rem(v + off, n))
            return carry

        lax.fori_loop(1, n, body, 0)

    def row_copy(which, source, target):
        ref = (pre_rows, pool_rows, gz_all)[which]
        compacted = compact and which == 0
        return put(
            to_send.at[target] if compacted else ref.at[source], ref.at[source],
            row_send.at[which], row_recv.at[which], s, target,
        )

    def all_rows(which):
        ref = (pre_rows, pool_rows, gz_all)[which].at[pl.ds(0, n - 1)]
        return put(ref, ref, row_send.at[which], row_recv.at[which], s, partner)

    def send_rows(which):
        far_first(lambda u: row_copy(which, v, u).start())

    def send_gz():
        for off in range(1, n):
            row_copy(2, v, lax.rem(v + off, n)).start()

    def wait_rows(which):
        all_rows(which).wait_recv()

    @pl.when(last)
    def _():
        copies = step_copies(seed, 0, s)
        on_left(start, copies[1])
        on_right(start, copies[2])
        send_rows(0)
        on_left(start, copies[3], pre_left)
        on_right(start, copies[4], pre_right)

    @pl.when(jnp.logical_not(last))
    def _():
        @pl.when(s == segments - 2)
        def _():
            pl.semaphore_wait(go, 1)

        send_rows(0)
        on_left(start, pre_left)
        on_right(start, pre_right)

    @pl.when(jnp.logical_not(late))
    def _():
        on_left(start, x_left)
        on_right(start, x_right)

    up_wide = (cdepth + 2) * plane
    up_lane = iota((1, up_wide), 1)
    up_target = (
        lax.div(up_lane, plane) * cw
        + lax.div(lax.rem(up_lane, plane), 2 * XL) * HX
        + lax.div(lax.rem(up_lane, XL), 2)
    )
    up_matrix[...] = jnp.where(
        iota(((cdepth + 2) * cw, up_wide), 0) == up_target, 0.125, 0.0
    ).astype(BF)

    if compact:
        for u in range(n):
            from_row = iota((128, 2 * reach * cw), 0)
            to_lane = lax.rem(iota((1, 2 * reach * cw), 1), reach * cw)
            second = lax.div(iota((1, 2 * reach * cw), 1), reach * cw)
            wanted = second * (128 // 2) + lax.div(to_lane, cw) * HX + lax.rem(to_lane, HX)
            wanted = jnp.where(lax.div(lax.rem(to_lane, cw), HX) == u, wanted, -1)
            pick[u * 128:(u + 1) * 128, :] = jnp.where(from_row == wanted, 1.0, 0.0).astype(BF)

    wait_rows(0)

    @pl.when(last)
    def _():
        credit(s - 1)

    if compact:
        flat_rows = jnp.concatenate([pre_rows[u] for u in range(n)], axis=1)
        gates = matmul(flat_rows, pick[...]).astype(BF)
        coarse_gate[:small, :] = gates[:, :reach * cw]
        coarse_gate[small:, :] = gates[:, reach * cw:]
    else:
        coarse_gate[...] = lax.fori_loop(
            0, n,
            lambda u, total: total + picked(
                pre_rows, u, reach_cell, reach_inline, reach * cw
            ),
            jnp.zeros((channels, reach * cw), F32),
        ).astype(BF)

    def take_pooled():
        wait_rows(1)
        lane = iota((1, group), 1)
        inline = lax.div(lax.rem(lane, cw), HX)

        def body(g, carry):
            cell = (g * (group // cw) + lax.div(lane, cw)) * HX + lax.rem(lane, HX)
            pool_all[g] = lax.fori_loop(
                0, n,
                lambda u, total: total + picked(pool_rows, u, cell, inline, group),
                jnp.zeros((channels, group), F32),
            ).astype(BF)
            return carry

        lax.fori_loop(0, groups, body, 0)

    def take_fine_x():
        for block in range(9):
            outer, row_step = block // 3, 1 - block % 3
            mask = tap_mask(plane, plane, XL, row_step, 0)
            for p in range(depth):
                fine_x[block * channels:(block + 1) * channels, p * plane:(p + 1) * plane] = (
                    rolled(x_ext[p + outer], row_step * XL) * mask
                )

    @pl.when(jnp.logical_not(late))
    def _():
        send_rows(1)
        take_pooled()

    @pl.when(jnp.logical_not(late))
    def _():
        on_left(wait_recv, x_right)
        on_right(wait_recv, x_left)
        take_fine_x()

    incoming = step_copies(out, 1, s)

    on_left(wait_recv, incoming[2])
    on_right(wait_recv, incoming[1])

    @pl.when(jnp.logical_not(last))
    def _():
        incoming[0].wait_recv()

    @pl.when(s == segments - 2)
    def _():
        credit(s + 1)

    side = pool_ext.shape[2]
    near = jnp.concatenate(
        [pool_ext[0][:, side - 2 * cw:], pool_ext[1], pool_ext[2][:, :2 * cw]], axis=1
    )
    coarse_gz = jnp.where(coarse_gate[...] > 0, near, jnp.zeros_like(near))
    gz_all[v] = coarse_gz[:, 2 * cw:2 * cw + slab]
    for r, (row_step, col_step) in enumerate(STEPS):
        mask = tap_mask(reach * cw, cw, HX, row_step, col_step)
        coarse_cols[r * channels:(r + 1) * channels, :] = (
            rolled(coarse_gz, row_step * HX + col_step) * mask
        )

    terms = matmul(coarse_cat[...], coarse_cols[...])
    width = (cdepth + 2) * cw
    coarse_back = sum(
        terms[outer * channels:(outer + 1) * channels, (2 - outer) * cw:(2 - outer) * cw + width]
        for outer in range(3)
    ).astype(BF)

    spread = matmul(coarse_back, up_matrix[...])
    pieces = [
        spread[:, (p + 1) // 2 * plane:((p + 1) // 2 + 1) * plane] for p in range(depth + 2)
    ]

    on_left(wait_recv, pre_right, incoming[4])
    on_right(wait_recv, pre_left, incoming[3])

    @pl.when(jnp.logical_not(last))
    def _():
        incoming[5].wait_recv()

    @pl.when(jnp.logical_not(late) & (s > 0))
    def _():
        send_gz()

    def take_cols(planes, first, count):
        for p in planes:
            grad = grad_ext[p].astype(F32) + pieces[p]
            gz = jnp.where(pre_ext[p].astype(F32) > 0, grad, 0.0).astype(BF)
            for r in range(first, first + count):
                row_step, col_step = STEPS[r]
                mask = tap_mask(plane, plane, XL, row_step, col_step)
                fine_cols[r * channels:(r + 1) * channels, p * plane:(p + 1) * plane] = (
                    rolled(gz, row_step * XL + col_step) * mask
                )

    def take_out():
        terms = matmul(fine_cat[...], fine_cols[...])
        for p in range(depth):
            total = grad_ext[p + 1].astype(F32)
            for outer in range(3):
                total = total + terms[
                    outer * channels:(outer + 1) * channels,
                    (p + 2 - outer) * plane:(p + 3 - outer) * plane,
                ]
            out[p] = total.astype(BF)

    def pair_copy(k):
        return put(
            parts.at[2 * other + k], paired.at[k], pair_send.at[k], pair_recv.at[k], s, partner
        )

    def sum_copy(k, row_from, row_to):
        return put(
            middle.at[k], arrived.at[row_from],
            sum_send.at[k], sum_recv.at[0], s, 2 * row_to + half,
        )

    def fine_sums():
        gz = fine_cols[3 * channels:6 * channels, plane:plane + own]
        grads = matmul_nt(fine_x[...], gz)
        blocks = [grads[block * channels:(block + 1) * channels, :] for block in range(9)]
        rest = parts.shape[2] - TAPS * channels
        if rest:
            blocks.append(jnp.zeros((channels, rest), F32))
        flat = jnp.concatenate(blocks, axis=1).astype(BF)
        for j in range(KEEPERS):
            parts[j] = flat[j * share:(j + 1) * share, :]

    def pair_sends():
        for k in range(2):
            pair_copy(k).start()

    def lanes_of(part):
        return slice(cuts[part], cuts[part + 1])

    def straight_copy(j, part, vol_to):
        return put(
            parts.at[j, :, lanes_of(part)], landed.at[v, :, lanes_of(part)],
            straight_send.at[0], straight_recv.at[part], s, vol_to,
        )

    def straight_landed(part):
        block = landed.at[pl.ds(0, n - 1), :, lanes_of(part)]
        return put(block, block, straight_send.at[0], straight_recv.at[part], s, partner)

    def straight_sums():
        fine_sums()

        def send(order):
            for part in range(PARTS):
                for j in order:
                    @pl.when(v != first_keeper + j)
                    def _(j=j, part=part):
                        straight_copy(j, part, first_keeper + j).start()

        @pl.when(v < n // 2)
        def _():
            send(range(KEEPERS - 1, -1, -1))

        @pl.when(v >= n // 2)
        def _():
            send(range(KEEPERS))

        @pl.when((mine >= 0) & (mine < KEEPERS))
        def _():
            landed[v] = parts[mine]

    def column_sums():
        for k in range(2):
            pair_copy(k).wait_recv()
            both = parts[2 * half + k].astype(F32) + paired[k].astype(F32)
            middle[k] = both.astype(BF)

            @pl.when(row != first_owner + k)
            def _(k=k):
                sum_copy(k, row, first_owner + k).start()

            @pl.when(row == first_owner + k)
            def _(k=k):
                arrived[row] = middle[k]

    @pl.when(s == 0)
    def _():
        inner = range(1, depth + 1)
        take_cols(inner, 3, 3)
        straight_sums()
        send_gz()
        take_cols(inner, 0, 3)
        take_cols(inner, 6, 3)
        take_cols((0, depth + 1), 0, 9)
        take_out()

    outgoing = step_copies(out, 1, s - 1)

    @pl.when(last)
    def _():
        copies = step_copies(seed, 0, s)
        on_left(wait_send, copies[1], copies[3])
        on_right(wait_send, copies[2], copies[4])

    @pl.when(s > 0)
    def _():
        take_cols(range(depth + 2), 0, 9)
        take_out()
        outgoing[6].start()
        pool_out[1] = pool_of(out)
        on_left(start, outgoing[1])
        on_right(start, outgoing[2])
        outgoing[0].start()
        on_left(start, outgoing[3])
        on_right(start, outgoing[4])
        outgoing[7].start()

    @pl.when(last)
    def _():
        pl.semaphore_wait(go, 1)

    @pl.when(late)
    def _():
        on_left(start, x_left)
        on_right(start, x_right)
        send_rows(1)

    @pl.when(late)
    def _():
        take_pooled()
        on_left(wait_recv, x_right)
        on_right(wait_recv, x_left)
        take_fine_x()

    @pl.when(late)
    def _():
        send_gz()

    @pl.when(s > 0)
    def _():
        @pl.when(paced)
        def _():
            fine_sums()
            pair_sends()

        @pl.when(direct)
        def _():
            straight_sums()

    grad_store = pltpu.make_async_copy(grad_out, grad_o, store_sem.at[0])
    coarse_store = pltpu.make_async_copy(coarse_out, coarse_o, store_sem.at[1])

    def fine_store(rows):
        return pltpu.make_async_copy(
            fine_out.at[:, rows], fine_o.at[:, rows], store_sem.at[2]
        )

    grad_out[...] = jnp.swapaxes(out[...], 0, 1)
    grad_store.start()

    def coarse_sums():
        total = jnp.zeros((3 * channels, 9 * channels), F32)
        edge = jnp.zeros((channels, cw), BF)
        for g in range(groups):
            xs = jnp.concatenate(
                [
                    pool_all[g - 1][:, group - cw:] if g else edge,
                    pool_all[g],
                    pool_all[g + 1][:, :cw] if g < groups - 1 else edge,
                ],
                axis=1,
            )
            tall = jnp.concatenate([xs[:, o * cw:o * cw + group] for o in range(3)], axis=0)
            slabs = group // slab
            flat = jnp.concatenate([gz_all[g * slabs + u] for u in range(slabs)], axis=1)
            for r, (row_step, col_step) in enumerate(STEPS):
                mask = tap_mask(group, cw, HX, row_step, col_step)
                full_cols[r * channels:(r + 1) * channels, :] = (
                    rolled(flat, row_step * HX + col_step) * mask
                )
            total = total + matmul_nt(tall, full_cols[...])
        return total * scales[1]

    def place(ref, first_row, value):
        rows = value.shape[0]
        at = first_row
        while at < first_row + rows:
            outer, inner = divmod(at, channels)
            count = min(channels - inner, first_row + rows - at)
            for r in range(9):
                ref[outer * 9 + r, inner:inner + count, :] = value[
                    at - first_row:at - first_row + count, r * channels:(r + 1) * channels
                ]
            at += count

    @pl.when(paced)
    def _():
        column_sums()

    def hand_copy(piece, row_to):
        return put(
            collected.at[piece], collected.at[piece],
            hand_send.at[0], all_recv.at[piece], s, 2 * row_to + half,
        )

    def pass_copy(k, piece):
        return put(
            collected.at[piece], collected.at[piece],
            pass_send.at[k], all_recv.at[piece], s, partner,
        )

    def other_rows(act):
        def body(off, carry):
            act(lax.rem(row + off, columns))
            return carry

        lax.fori_loop(1, columns, body, 0)

    sums_arrived = put(
        arrived.at[pl.ds(0, columns - 1)], arrived.at[pl.ds(0, columns - 1)],
        sum_send.at[0], sum_recv.at[0], s, partner,
    )

    for k in range(2):
        @pl.when((row == first_owner + k) & paced)
        def _(k=k):
            piece = 2 * half + k
            sums_arrived.wait_recv()
            whole = arrived[0].astype(F32)
            for u in range(1, columns):
                whole = whole + arrived[u].astype(F32)
            collected[piece] = whole.astype(BF)
            other_rows(lambda u: hand_copy(piece, u).start())
            pass_copy(k, piece).start()

    def spread_copy(j, part, vol_to):
        block = collected.at[j, :, lanes_of(part)]
        return put(block, block, spread_send.at[0], all_recv.at[j], s, vol_to)

    def whole_share(j):
        return put(
            collected.at[j], collected.at[j], spread_send.at[0], all_recv.at[j], s, partner
        )

    @pl.when(keeper & direct)
    def _():
        for part in range(PARTS):
            straight_landed(part).wait_recv()
            at = lanes_of(part)
            whole = landed[0, :, at].astype(F32)
            for u in range(1, n):
                whole = whole + landed[u, :, at].astype(F32)
            collected[mine, :, at] = whole.astype(BF)
            in_order(lambda u, part=part: spread_copy(mine, part, u).start())

    wait_rows(2)
    place(coarse_out, 0, coarse_sums())
    coarse_store.start()

    for which in range(3):
        all_rows(which).wait_send()

    @pl.when(paced)
    def _():
        for k in range(2):
            pair_copy(k).wait_send()

            @pl.when(row != first_owner + k)
            def _(k=k):
                sum_copy(k, row, first_owner + k).wait_send()

    @pl.when(direct)
    def _():
        @pl.when(keeper)
        def _():
            block = parts.at[pl.ds(0, KEEPERS - 1)]
            put(block, block, straight_send.at[0], straight_recv.at[0], s, partner).wait_send()

        @pl.when(jnp.logical_not(keeper))
        def _():
            put(parts, parts, straight_send.at[0], straight_recv.at[0], s, partner).wait_send()

    on_left(wait_send, pre_left, x_left)
    on_right(wait_send, pre_right, x_right)

    @pl.when(s > 0)
    def _():
        on_left(wait_send, outgoing[1], outgoing[3])
        on_right(wait_send, outgoing[2], outgoing[4])
        wait_send(outgoing[0])
        wait_send(outgoing[5])

    @pl.when(paced)
    def _():
        for k in range(2):
            @pl.when(row != first_owner + k)
            def _(k=k):
                hand_copy(2 * half + k, row).wait_recv()
                pass_copy(k, 2 * half + k).start()

        for k in range(2):
            pass_copy(k, 2 * other + k).wait_recv()

    for j in range(KEEPERS):
        @pl.when(direct & (v != first_keeper + j))
        def _(j=j):
            whole_share(j).wait_recv()

        value = collected[j].astype(F32) * scales[0]
        rows = slice(j * share, (j + 1) * share)
        for k in range(TAPS):
            fine_out[k, rows, :] = value[:, k * channels:(k + 1) * channels]
        fine_store(rows).start()

    @pl.when(paced)
    def _():
        for k in range(2):
            pass_copy(k, 2 * half + k).wait_send()

            @pl.when(row == first_owner + k)
            def _(k=k):
                other_rows(lambda u: hand_copy(2 * half + k, u).wait_send())

    @pl.when(keeper & direct)
    def _():
        others(lambda u: whole_share(mine).wait_send())

    grad_store.wait()
    coarse_store.wait()
    pltpu.make_async_copy(fine_out, fine_o, store_sem.at[2]).wait()


def finish(grad, fine, coarse, grad_out, fine_out, coarse_out, sem):
    copies = [
        pltpu.make_async_copy(src, dst, sem.at[index])
        for index, (src, dst) in enumerate(
            ((fine, fine_out), (coarse, coarse_out), (grad, grad_out))
        )
    ]
    for copy in copies:
        copy.start()
    for copy in copies:
        copy.wait()


def on_device(
    cotangent, labels, class_weight, inputs, fine_pre, pooled, coarse_pre,
    fine_filters, coarse_filters,
):
    segments = lax.axis_size("segment")
    n = lax.axis_size("vol")
    channels, depth, plane = inputs.shape[1:]
    own = depth * plane
    cw = plane // 4
    cdepth = depth // 2
    slab = cdepth * cw
    reach = cdepth + 4
    row_len = pooled.shape[2] * pooled.shape[3]
    cells = own * n
    scales = (1.0 / math.sqrt(cells), 1.0 / math.sqrt(cells // 8))
    sizes = (segments, n, channels, depth, plane)
    group = min(GROUP_LANES, n * slab)
    groups = n * slab // group
    share = (channels // KEEPERS, -(-TAPS * channels // 128) * 128)
    pick_shape = (n * 128, 2 * reach * cw)
    compact_shape = (channels // 2, 128)
    if math.prod(pick_shape) * 2 > PICK_BYTES or reach * HX > 64:
        pick_shape = (1, 128)
        compact_shape = (channels, row_len)
    spaces = pl.BlockSpec(memory_space=pl.ANY)
    limit = min(60 * MIB, 16 * MIB + 6 * 2 * 9 * channels * (own + 2 * plane))
    hbm = pl.BlockSpec(memory_space=pltpu.HBM)
    dma = pltpu.SemaphoreType.DMA
    tap_shape = jax.ShapeDtypeStruct((TAPS, channels, channels), F32)
    grad_shape = jax.ShapeDtypeStruct((channels, depth, plane), BF)
    outs = pl.pallas_call(
        functools.partial(kernel, sizes, scales),
        out_shape=(grad_shape, tap_shape, tap_shape),
        in_specs=[hbm] * 9,
        out_specs=(spaces, spaces, spaces),
        scratch_shapes=[
            pltpu.VMEM((channels, depth, plane), BF),
            pltpu.VMEM((TAPS, channels, channels), F32),
            pltpu.VMEM((TAPS, channels, channels), F32),
            pltpu.SMEM(class_weight.shape, F32),
            pltpu.VMEM(cotangent.shape, BF),
            pltpu.VMEM(labels.shape, jnp.int32),
            pltpu.VMEM((channels, depth, plane), BF),
            pltpu.VMEM((channels, depth, plane), BF),
            pltpu.VMEM((2, TAPS, channels, channels), BF),
            pltpu.VMEM((depth, channels, plane), BF),
            pltpu.VMEM((depth, channels, plane), BF),
            pltpu.VMEM((3 * channels, 9 * channels), BF),
            pltpu.VMEM((3 * channels, 9 * channels), BF),
            pltpu.VMEM((channels, row_len), BF),
            pltpu.VMEM((n, channels // 2, 128), BF),
            pltpu.VMEM((n, *compact_shape), BF),
            pltpu.VMEM((n, channels, row_len), BF),
            pltpu.VMEM((depth + 2, channels, plane), BF),
            pltpu.VMEM((depth + 2, channels, plane), BF),
            pltpu.VMEM((depth + 2, channels, plane), BF),
            pltpu.VMEM((3, channels, slab), BF),
            pltpu.VMEM((2, channels, slab), BF),
            pltpu.VMEM((channels, reach * cw), BF),
            pltpu.VMEM(pick_shape, BF),
            pltpu.VMEM((own, slab), BF),
            pltpu.VMEM(((cdepth + 2) * cw, (cdepth + 2) * plane), BF),
            pltpu.VMEM((9 * channels, own), BF),
            pltpu.VMEM((groups, channels, group), BF),
            pltpu.VMEM((9 * channels, own + 2 * plane), BF),
            pltpu.VMEM((9 * channels, reach * cw), BF),
            pltpu.VMEM((9 * channels, group), BF),
            pltpu.VMEM((n, channels, slab), BF),
            pltpu.VMEM((KEEPERS, *share), BF),
            pltpu.VMEM((n, *share), BF),
            pltpu.VMEM((2, *share), BF),
            pltpu.VMEM((2, *share), BF),
            pltpu.VMEM((n // 2, *share), BF),
            pltpu.VMEM((KEEPERS, *share), BF),
            dma((8,)), dma((3,)), dma((3,)), dma((4,)), dma((4,)), dma((6,)), dma((6,)),
            dma((2,)), dma((2,)), dma((2,)), dma((1,)), dma((1,)), dma((2,)), dma((KEEPERS,)),
            dma((1,)), dma((PARTS,)), dma((1,)), dma((3,)),
            pltpu.SemaphoreType.REGULAR,
        ],
        compiler_params=pltpu.CompilerParams(
            collective_id=0, has_side_effects=True, vmem_limit_bytes=limit
        ),
    )(
        *(
            pltpu.with_memory_space_constraint(array, pltpu.HBM)
            for array in (
                class_weight,
                cotangent,
                labels,
                inputs[0],
                fine_pre[0],
                coarse_pre[0].reshape(channels, row_len),
                pooled[0].reshape(channels, row_len),
                fine_filters[0],
                coarse_filters[0],
            )
        )
    )

    grad, fine_grads, coarse_grads = pl.pallas_call(
        finish,
        out_shape=(grad_shape, tap_shape, tap_shape),
        in_specs=[spaces] * 3,
        out_specs=[hbm] * 3,
        scratch_shapes=[dma((3,))],
        compiler_params=pltpu.CompilerParams(vmem_limit_bytes=1024 * 1024),
    )(*outs)
    return (grad[None], fine_grads[None], coarse_grads[None])


def solution(mesh):
    return jax.shard_map(
        on_device,
        mesh=mesh,
        in_specs=(
            P(None, "vol", None),
            P("vol", None),
            P(),
            P("segment", None, "vol", None),
            P("segment", None, "vol", None),
            P("segment", None, "vol", None),
            P("segment", None, "vol", None),
            P("segment", None, None, None),
            P("segment", None, None, None),
        ),
        out_specs=(
            P("segment", None, "vol", None),
            P("segment", None, None, None),
            P("segment", None, None, None),
        ),
        check_vma=False,
    )
```

```python
import functools
import math

import jax
import jax.numpy as jnp
from jax import lax
from jax.experimental import pallas as pl
from jax.experimental.pallas import tpu as pltpu
from jax.sharding import PartitionSpec as P

XL = 16
HX = XL // 2
TAPS = 27
KEEPERS = 4
PARTS = 3
GROUP_LANES = 1024
MIB = 1024 * 1024
PICK_BYTES = 4 * MIB
BF = jnp.bfloat16
F32 = jnp.float32


def iota(shape, dim):
    return lax.broadcasted_iota(jnp.int32, shape, dim)


def matmul(a, b):
    return lax.dot_general(a, b, (((1,), (0,)), ((), ())), preferred_element_type=F32)


def matmul_nt(a, b):
    return lax.dot_general(a, b, (((1,), (1,)), ((), ())), preferred_element_type=F32)


def tap_mask(lanes, plane, columns, row_step, col_step):
    lane = iota((1, lanes), 1)
    column = lax.rem(lane, columns) - col_step
    row = lax.div(lax.rem(lane, plane), columns) - row_step
    rows = plane // columns
    inside = (column >= 0) & (column < columns) & (row >= 0) & (row < rows)
    return jnp.where(inside, 1.0, 0.0).astype(BF)


def rolled(value, shift):
    size = value.shape[1]
    shift = shift % size
    return value if shift == 0 else pltpu.roll(value, shift, 1)


STEPS = [(r, c) for r in (-1, 0, 1) for c in (-1, 0, 1)]


def kernel(
    sizes, scales,
    class_weight_h, cotangent_h, labels_h, saved_h, fine_pre_h, coarse_pre_h, pooled_h,
    fine_w_h, coarse_w_h,
    grad_o, fine_o, coarse_o,
    grad_out, fine_out, coarse_out, class_weight, cotangent, labels, saved, fine_pre, weights,
    out, seed, fine_cat, coarse_cat, own_rows, to_send, pre_rows, pool_rows, pre_ext, x_ext, grad_ext, pool_ext,
    pool_out, coarse_gate, pick, pool_matrix, up_matrix, fine_x, pool_all, fine_cols, coarse_cols,
    full_cols, gz_all, parts, landed, paired, middle, arrived, collected,
    load_sem, row_send, row_recv, halo_send, halo_recv, step_send, step_recv,
    pair_recv, sum_send, sum_recv, all_recv,
    straight_recv, go,
):
    segments, n, channels, depth, plane = sizes
    cw = plane // 4
    cdepth = depth // 2
    own = depth * plane
    slab = cdepth * cw
    row_len = coarse_pre_h.shape[1]
    groups = pool_all.shape[0]
    group = pool_all.shape[2]
    s = lax.axis_index("segment")
    v = lax.axis_index("vol")
    has_left, has_right = v > 0, v < n - 1
    last = s == segments - 1
    late = s >= segments - 2
    paced = (lax.rem(s, 2) == 1) & (s < segments - 1)
    direct = jnp.logical_not(paced)
    half = lax.rem(v, 2)
    other = 1 - half
    partner = v + 1 - 2 * half
    row = lax.div(v, 2)
    columns = n // 2
    first_owner = columns // 2 - 1
    share = channels // KEEPERS
    tiles = parts.shape[2] // 128
    cuts = [128 * (tiles * part // PARTS) for part in range(PARTS + 1)]
    first_keeper = n // 2 - KEEPERS // 2
    mine = v - first_keeper
    keeper = (mine >= 0) & (mine < KEEPERS)

    def put(src, dst, send, recv, segment, vol):
        return pltpu.make_async_remote_copy(
            src_ref=src, dst_ref=dst, send_sem=send, recv_sem=recv,
            device_id=(segment, vol), device_id_type=pl.DeviceIdType.MESH,
        )

    def credit(segment):
        pl.semaphore_signal(
            go, inc=1, device_id=(segment, v), device_id_type=pl.DeviceIdType.MESH
        )

    barrier = pltpu.get_barrier_semaphore()

    def greet(off, carry):
        pl.semaphore_signal(
            barrier, inc=1, device_id=(s, lax.rem(v + off, n)),
            device_id_type=pl.DeviceIdType.MESH,
        )
        return carry

    lax.fori_loop(1, n, greet, 0)
    for up in (-1, 1):
        for side in (-1, 0, 1):
            there = (s + up >= 0) & (s + up < segments) & (v + side >= 0) & (v + side < n)

            @pl.when(there)
            def _(up=up, side=side):
                pl.semaphore_signal(
                    barrier, inc=1, device_id=(s + up, v + side),
                    device_id_type=pl.DeviceIdType.MESH,
                )

    def load(src, dst, index):
        return pltpu.make_async_copy(src, dst, load_sem.at[index])

    compact = pick.shape[0] > 1
    rows_load = load(coarse_pre_h, own_rows if compact else pre_rows.at[v], 0)
    pre_load = load(fine_pre_h, fine_pre, 1)
    seed_loads = (
        load(class_weight_h, class_weight, 2),
        load(cotangent_h, cotangent, 3),
        load(labels_h, labels, 4),
    )
    coarse_w_load = load(coarse_w_h, weights.at[0], 5)
    fine_w_load = load(fine_w_h, weights.at[1], 5)
    both_w_load = load(weights, weights, 5)
    saved_load = load(saved_h, saved, 6)
    pooled_load = load(pooled_h, pool_rows.at[v], 7)

    rows_load.start()

    @pl.when(last)
    def _():
        for copy in seed_loads:
            copy.start()

    for copy in (pre_load, coarse_w_load, fine_w_load, saved_load, pooled_load):
        copy.start()

    reach = cdepth + 4
    reach_lane = iota((1, reach * cw), 1)
    reach_depth = v * cdepth - 2 + lax.div(reach_lane, cw)
    reach_cell = reach_depth * HX + lax.rem(reach_lane, HX)
    reach_cell = jnp.where(
        (reach_depth >= 0) & (reach_depth < n * cdepth), reach_cell, -1
    )
    reach_inline = lax.div(lax.rem(reach_lane, cw), HX)

    def picked(rows, u, cell, inline, lanes):
        chosen = iota((row_len, lanes), 0) == jnp.where(inline == u, cell, -1)
        return matmul(rows[u], jnp.where(chosen, 1.0, 0.0).astype(BF))

    small = channels // 2
    if compact:
        to_lane = iota((1, n * 128), 1)
        to_cell = lax.rem(to_lane, 128 // 2)
        to_depth = lax.div(to_lane, 128) * cdepth - 2 + lax.div(to_cell, HX)
        to_row = (
            lax.div(lax.rem(to_lane, 128), 128 // 2) * row_len
            + to_depth * HX + lax.rem(to_cell, HX)
        )
        inside = (to_depth >= 0) & (to_depth < n * cdepth) & (to_cell < reach * HX)
        to_row = jnp.where(inside, to_row, -1)
        split = jnp.where(iota((2 * row_len, n * 128), 0) == to_row, 1.0, 0.0).astype(BF)

    def step_copies(src, turn, segment):
        def step(which, a, b, vol):
            return put(a, b, step_send.at[which], step_recv.at[which], segment, vol)

        block = pool_out.at[turn]
        return (
            step(0, block, pool_ext.at[1], v),
            step(1, block, pool_ext.at[2], v - 1),
            step(2, block, pool_ext.at[0], v + 1),
            step(3, src.at[0], grad_ext.at[depth + 1], v - 1),
            step(4, src.at[depth - 1], grad_ext.at[0], v + 1),
            step(5, src, grad_ext.at[1:depth + 1], v),
            step(5, src.at[0], grad_ext.at[1], v),
            step(5, src.at[1:depth], grad_ext.at[2:depth + 1], v),
        )

    def on_left(act, *copies):
        @pl.when(has_left)
        def _():
            for copy in copies:
                act(copy)

    def on_right(act, *copies):
        @pl.when(has_right)
        def _():
            for copy in copies:
                act(copy)

    def start(copy):
        copy.start()

    def wait_send(copy):
        copy.wait_send()

    def wait_recv(copy):
        copy.wait_recv()

    def pool_of(ref):
        flat = jnp.concatenate([ref[p] for p in range(depth)], axis=1)
        return matmul(flat, pool_matrix[...]).astype(BF)

    def prepare():
        fine_lane = iota((own, 1), 0)
        pool_target = (
            lax.div(fine_lane, 2 * plane) * cw
            + lax.div(lax.rem(fine_lane, plane), 2 * XL) * HX
            + lax.div(lax.rem(fine_lane, XL), 2)
        )
        pool_matrix[...] = jnp.where(iota((own, slab), 1) == pool_target, 1.0, 0.0).astype(BF)

        @pl.when(last)
        def _():
            for copy in seed_loads:
                copy.wait()
            planes = jnp.swapaxes(cotangent[...], 0, 1)
            for p in range(depth):
                label = labels[p:p + 1, :]
                weight = jnp.zeros(label.shape, F32)
                for index in range(class_weight.shape[0]):
                    weight = weight + jnp.where(label == index, class_weight[index], 0.0)
                block = (planes[p].astype(F32) * weight).astype(BF)
                seed[p] = block
                grad_ext[p + 1] = block
            pool_out[0] = pool_of(seed)
            pool_ext[1] = pool_out[0]

        pre_load.wait()
        pre_ext[1:depth + 1] = jnp.swapaxes(fine_pre[...], 0, 1)
        both_w_load.wait()
        for k in range(TAPS):
            rows = slice(k // 9 * channels, (k // 9 + 1) * channels)
            lanes = slice(k % 9 * channels, (k % 9 + 1) * channels)
            coarse_cat[rows, lanes] = weights[0, k]
            fine_cat[rows, lanes] = weights[1, k]
        saved_load.wait()
        x_ext[1:depth + 1] = jnp.swapaxes(saved[...], 0, 1)

        @pl.when(v == 0)
        def _():
            pre_ext[0] = jnp.zeros((channels, plane), BF)
            x_ext[0] = jnp.zeros((channels, plane), BF)
            grad_ext[0] = jnp.zeros((channels, plane), BF)
            pool_ext[0] = jnp.zeros(pool_ext.shape[1:], BF)

        @pl.when(v == n - 1)
        def _():
            pre_ext[depth + 1] = jnp.zeros((channels, plane), BF)
            x_ext[depth + 1] = jnp.zeros((channels, plane), BF)
            grad_ext[depth + 1] = jnp.zeros((channels, plane), BF)
            pool_ext[2] = jnp.zeros(pool_ext.shape[1:], BF)

        pooled_load.wait()

    pl.when(v < n // 2)(prepare)

    rows_load.wait()
    if compact:
        halves = jnp.concatenate([own_rows[:small, :], own_rows[small:, :]], axis=1)
        blocks = matmul(halves, split).astype(BF)
        for u in range(n):
            to_send[u] = blocks[:, u * 128:(u + 1) * 128]
        pre_rows[v] = to_send[v]

    ups = jnp.where(s > 0, 1, 0) + jnp.where(last, 0, 1)
    sides = 1 + jnp.where(has_left, 1, 0) + jnp.where(has_right, 1, 0)
    pl.semaphore_wait(barrier, n - 1 + ups * sides)

    def halo(ref, index):
        return (
            put(ref.at[1], ref.at[depth + 1], halo_send.at[index], halo_recv.at[index], s, v - 1),
            put(
                ref.at[depth], ref.at[0],
                halo_send.at[index + 1], halo_recv.at[index + 1], s, v + 1,
            ),
        )

    pre_left, pre_right = halo(pre_ext, 0)
    x_left, x_right = halo(x_ext, 2)

    def far_first(act):
        def body(step, carry):
            for u in (v + n - step, v - n + step):
                @pl.when((u >= 0) & (u < n))
                def _(u=u):
                    act(u)

            return carry

        lax.fori_loop(1, n, body, 0)

    def in_order(act):
        def body(u, carry):
            @pl.when(u != v)
            def _():
                act(u)

            return carry

        lax.fori_loop(0, n, body, 0)

    def others(act):
        def body(off, carry):
            act(lax.rem(v + off, n))
            return carry

        lax.fori_loop(1, n, body, 0)

    def row_copy(which, source, target):
        ref = (pre_rows, pool_rows, gz_all)[which]
        compacted = compact and which == 0
        return put(
            to_send.at[target] if compacted else ref.at[source], ref.at[source],
            row_send.at[which], row_recv.at[which], s, target,
        )

    def all_rows(which):
        ref = (pre_rows, pool_rows, gz_all)[which].at[pl.ds(0, n - 1)]
        return put(ref, ref, row_send.at[which], row_recv.at[which], s, partner)

    def send_rows(which):
        far_first(lambda u: row_copy(which, v, u).start())

    def send_gz():
        for off in range(1, n):
            row_copy(2, v, lax.rem(v + off, n)).start()

    def wait_rows(which):
        all_rows(which).wait_recv()

    @pl.when(last)
    def _():
        send_rows(0)

    pl.when(v >= n // 2)(prepare)

    @pl.when(last)
    def _():
        copies = step_copies(seed, 0, s)
        on_left(start, copies[1])
        on_right(start, copies[2])
        on_left(start, copies[3], pre_left)
        on_right(start, copies[4], pre_right)

    @pl.when(jnp.logical_not(last))
    def _():
        @pl.when(s == segments - 2)
        def _():
            pl.semaphore_wait(go, 1)

        send_rows(0)
        on_left(start, pre_left)
        on_right(start, pre_right)

    @pl.when(jnp.logical_not(late))
    def _():
        on_left(start, x_left)
        on_right(start, x_right)

    up_wide = (cdepth + 2) * plane
    up_lane = iota((1, up_wide), 1)
    up_target = (
        lax.div(up_lane, plane) * cw
        + lax.div(lax.rem(up_lane, plane), 2 * XL) * HX
        + lax.div(lax.rem(up_lane, XL), 2)
    )
    up_matrix[...] = jnp.where(
        iota(((cdepth + 2) * cw, up_wide), 0) == up_target, 0.125, 0.0
    ).astype(BF)

    if compact:
        from_row = iota((128 // 2, reach * cw), 0)
        to_lane = iota((1, reach * cw), 1)
        wanted = lax.div(to_lane, cw) * HX + lax.rem(to_lane, HX)
        to_inline = lax.div(lax.rem(to_lane, cw), HX)
        for u in range(n):
            chosen = from_row == jnp.where(to_inline == u, wanted, -1)
            pick[u * 64:(u + 1) * 64, :] = jnp.where(chosen, 1.0, 0.0).astype(BF)

    wait_rows(0)

    @pl.when(last)
    def _():
        credit(s - 1)

    if compact:
        arrivals = [pre_rows[u] for u in range(n)]
        flat_rows = jnp.concatenate(
            [
                jnp.concatenate([rows[:, 64 * h:64 * (h + 1)] for rows in arrivals], axis=1)
                for h in range(2)
            ],
            axis=0,
        )
        coarse_gate[...] = matmul(flat_rows, pick[...]).astype(BF)
    else:
        coarse_gate[...] = lax.fori_loop(
            0, n,
            lambda u, total: total + picked(
                pre_rows, u, reach_cell, reach_inline, reach * cw
            ),
            jnp.zeros((channels, reach * cw), F32),
        ).astype(BF)

    def take_pooled():
        wait_rows(1)
        lane = iota((1, group), 1)
        inline = lax.div(lax.rem(lane, cw), HX)

        def body(g, carry):
            cell = (g * (group // cw) + lax.div(lane, cw)) * HX + lax.rem(lane, HX)
            pool_all[g] = lax.fori_loop(
                0, n,
                lambda u, total: total + picked(pool_rows, u, cell, inline, group),
                jnp.zeros((channels, group), F32),
            ).astype(BF)
            return carry

        lax.fori_loop(0, groups, body, 0)

    def take_fine_x():
        for block in range(9):
            outer, row_step = block // 3, 1 - block % 3
            mask = tap_mask(plane, plane, XL, row_step, 0)
            for p in range(depth):
                fine_x[block * channels:(block + 1) * channels, p * plane:(p + 1) * plane] = (
                    rolled(x_ext[p + outer], row_step * XL) * mask
                )

    @pl.when(jnp.logical_not(late))
    def _():
        send_rows(1)
        take_pooled()

    @pl.when(jnp.logical_not(late))
    def _():
        on_left(wait_recv, x_right)
        on_right(wait_recv, x_left)
        take_fine_x()

    incoming = step_copies(out, 1, s)

    on_left(wait_recv, incoming[2])
    on_right(wait_recv, incoming[1])

    @pl.when(jnp.logical_not(last))
    def _():
        incoming[0].wait_recv()

    @pl.when(s == segments - 2)
    def _():
        credit(s + 1)

    side = pool_ext.shape[2]
    near = jnp.concatenate(
        [pool_ext[0][:, side - 2 * cw:], pool_ext[1], pool_ext[2][:, :2 * cw]], axis=1
    )
    coarse_gz = jnp.where(coarse_gate[...] > 0, near, jnp.zeros_like(near))
    gz_all[v] = coarse_gz[:, 2 * cw:2 * cw + slab]
    for r, (row_step, col_step) in enumerate(STEPS):
        mask = tap_mask(reach * cw, cw, HX, row_step, col_step)
        coarse_cols[r * channels:(r + 1) * channels, :] = (
            rolled(coarse_gz, row_step * HX + col_step) * mask
        )

    terms = matmul(coarse_cat[...], coarse_cols[...])
    width = (cdepth + 2) * cw
    coarse_back = sum(
        terms[outer * channels:(outer + 1) * channels, (2 - outer) * cw:(2 - outer) * cw + width]
        for outer in range(3)
    ).astype(BF)

    spread = matmul(coarse_back, up_matrix[...])
    pieces = [
        spread[:, (p + 1) // 2 * plane:((p + 1) // 2 + 1) * plane] for p in range(depth + 2)
    ]

    on_left(wait_recv, pre_right, incoming[4])
    on_right(wait_recv, pre_left, incoming[3])

    @pl.when(jnp.logical_not(last))
    def _():
        incoming[5].wait_recv()

    @pl.when(jnp.logical_not(late) & (s > 0))
    def _():
        send_gz()

    def take_cols(planes, first, count):
        for p in planes:
            grad = grad_ext[p].astype(F32) + pieces[p]
            gz = jnp.where(pre_ext[p].astype(F32) > 0, grad, 0.0).astype(BF)
            for r in range(first, first + count):
                row_step, col_step = STEPS[r]
                mask = tap_mask(plane, plane, XL, row_step, col_step)
                fine_cols[r * channels:(r + 1) * channels, p * plane:(p + 1) * plane] = (
                    rolled(gz, row_step * XL + col_step) * mask
                )

    def take_out():
        terms = matmul(fine_cat[...], fine_cols[...])
        for p in range(depth):
            total = grad_ext[p + 1].astype(F32)
            for outer in range(3):
                total = total + terms[
                    outer * channels:(outer + 1) * channels,
                    (p + 2 - outer) * plane:(p + 3 - outer) * plane,
                ]
            out[p] = total.astype(BF)

    def pair_copy(k):
        return put(
            parts.at[2 * other + k], paired.at[k], load_sem.at[3 + k], pair_recv.at[k], s, partner
        )

    def sum_copy(k, row_from, row_to):
        return put(
            middle.at[k], arrived.at[row_from],
            sum_send.at[k], sum_recv.at[0], s, 2 * row_to + half,
        )

    def fine_sums():
        gz = fine_cols[3 * channels:6 * channels, plane:plane + own]
        grads = matmul_nt(fine_x[...], gz)
        blocks = [grads[block * channels:(block + 1) * channels, :] for block in range(9)]
        rest = parts.shape[2] - TAPS * channels
        if rest:
            blocks.append(jnp.zeros((channels, rest), F32))
        flat = jnp.concatenate(blocks, axis=1).astype(BF)
        for j in range(KEEPERS):
            parts[j] = flat[j * share:(j + 1) * share, :]

    def pair_sends():
        for k in range(2):
            pair_copy(k).start()

    def lanes_of(part):
        return slice(cuts[part], cuts[part + 1])

    def straight_copy(j, part, vol_to):
        return put(
            parts.at[j, :, lanes_of(part)], landed.at[v, :, lanes_of(part)],
            load_sem.at[3], straight_recv.at[part], s, vol_to,
        )

    def straight_landed(part):
        block = landed.at[pl.ds(0, n - 1), :, lanes_of(part)]
        return put(block, block, load_sem.at[3], straight_recv.at[part], s, partner)

    def straight_sums():
        fine_sums()

        def send(order):
            for part in range(PARTS):
                for j in order:
                    @pl.when(v != first_keeper + j)
                    def _(j=j, part=part):
                        straight_copy(j, part, first_keeper + j).start()

        @pl.when(v < n // 2)
        def _():
            send(range(KEEPERS - 1, -1, -1))

        @pl.when(v >= n // 2)
        def _():
            send(range(KEEPERS))

        @pl.when((mine >= 0) & (mine < KEEPERS))
        def _():
            landed[v] = parts[mine]

    def column_sums():
        for k in range(2):
            pair_copy(k).wait_recv()
            both = parts[2 * half + k].astype(F32) + paired[k].astype(F32)
            middle[k] = both.astype(BF)

            @pl.when(row != first_owner + k)
            def _(k=k):
                sum_copy(k, row, first_owner + k).start()

            @pl.when(row == first_owner + k)
            def _(k=k):
                arrived[row] = middle[k]

    @pl.when(s == 0)
    def _():
        inner = range(1, depth + 1)
        take_cols(inner, 3, 3)
        straight_sums()
        send_gz()
        take_cols(inner, 0, 3)
        take_cols(inner, 6, 3)
        take_cols((0, depth + 1), 0, 9)
        take_out()

    outgoing = step_copies(out, 1, s - 1)

    @pl.when(last)
    def _():
        copies = step_copies(seed, 0, s)
        on_left(wait_send, copies[1], copies[3])
        on_right(wait_send, copies[2], copies[4])

    @pl.when(s > 0)
    def _():
        take_cols(range(depth + 2), 0, 9)
        take_out()
        outgoing[6].start()
        pool_out[1] = pool_of(out)
        on_left(start, outgoing[1])
        on_right(start, outgoing[2])
        outgoing[0].start()
        on_left(start, outgoing[3])
        on_right(start, outgoing[4])
        outgoing[7].start()

    @pl.when(last)
    def _():
        pl.semaphore_wait(go, 1)

    @pl.when(late)
    def _():
        on_left(start, x_left)
        on_right(start, x_right)
        send_rows(1)

    @pl.when(late)
    def _():
        take_pooled()
        on_left(wait_recv, x_right)
        on_right(wait_recv, x_left)
        take_fine_x()

    @pl.when(late)
    def _():
        send_gz()

    @pl.when(s > 0)
    def _():
        @pl.when(paced)
        def _():
            fine_sums()
            pair_sends()

        @pl.when(direct)
        def _():
            straight_sums()

    grad_store = pltpu.make_async_copy(grad_out, grad_o, load_sem.at[0])
    coarse_store = pltpu.make_async_copy(coarse_out, coarse_o, load_sem.at[1])

    def fine_store(rows):
        return pltpu.make_async_copy(
            fine_out.at[:, rows], fine_o.at[:, rows], load_sem.at[2]
        )

    grad_out[...] = jnp.swapaxes(out[...], 0, 1)
    grad_store.start()

    def coarse_sums():
        total = jnp.zeros((3 * channels, 9 * channels), F32)
        edge = jnp.zeros((channels, cw), BF)
        for g in range(groups):
            xs = jnp.concatenate(
                [
                    pool_all[g - 1][:, group - cw:] if g else edge,
                    pool_all[g],
                    pool_all[g + 1][:, :cw] if g < groups - 1 else edge,
                ],
                axis=1,
            )
            tall = jnp.concatenate([xs[:, o * cw:o * cw + group] for o in range(3)], axis=0)
            slabs = group // slab
            flat = jnp.concatenate([gz_all[g * slabs + u] for u in range(slabs)], axis=1)
            for r, (row_step, col_step) in enumerate(STEPS):
                mask = tap_mask(group, cw, HX, row_step, col_step)
                full_cols[r * channels:(r + 1) * channels, :] = (
                    rolled(flat, row_step * HX + col_step) * mask
                )
            total = total + matmul_nt(tall, full_cols[...])
        return total * scales[1]

    def place(ref, first_row, value):
        rows = value.shape[0]
        at = first_row
        while at < first_row + rows:
            outer, inner = divmod(at, channels)
            count = min(channels - inner, first_row + rows - at)
            for r in range(9):
                ref[outer * 9 + r, inner:inner + count, :] = value[
                    at - first_row:at - first_row + count, r * channels:(r + 1) * channels
                ]
            at += count

    @pl.when(paced)
    def _():
        column_sums()

    def hand_copy(piece, row_to):
        return put(
            collected.at[piece], collected.at[piece],
            load_sem.at[5], all_recv.at[piece], s, 2 * row_to + half,
        )

    def pass_copy(k, piece):
        return put(
            collected.at[piece], collected.at[piece],
            load_sem.at[6 + k], all_recv.at[piece], s, partner,
        )

    def other_rows(act):
        def body(off, carry):
            act(lax.rem(row + off, columns))
            return carry

        lax.fori_loop(1, columns, body, 0)

    sums_arrived = put(
        arrived.at[pl.ds(0, columns - 1)], arrived.at[pl.ds(0, columns - 1)],
        sum_send.at[0], sum_recv.at[0], s, partner,
    )

    for k in range(2):
        @pl.when((row == first_owner + k) & paced)
        def _(k=k):
            piece = 2 * half + k
            sums_arrived.wait_recv()
            whole = arrived[0].astype(F32)
            for u in range(1, columns):
                whole = whole + arrived[u].astype(F32)
            collected[piece] = whole.astype(BF)
            other_rows(lambda u: hand_copy(piece, u).start())
            pass_copy(k, piece).start()

    def spread_copy(j, part, vol_to):
        block = collected.at[j, :, lanes_of(part)]
        return put(block, block, load_sem.at[5], all_recv.at[j], s, vol_to)

    def whole_share(j):
        return put(
            collected.at[j], collected.at[j], load_sem.at[5], all_recv.at[j], s, partner
        )

    @pl.when(keeper & direct)
    def _():
        for part in range(PARTS):
            straight_landed(part).wait_recv()
            at = lanes_of(part)
            whole = landed[0, :, at].astype(F32)
            for u in range(1, n):
                whole = whole + landed[u, :, at].astype(F32)
            collected[mine, :, at] = whole.astype(BF)
            in_order(lambda u, part=part: spread_copy(mine, part, u).start())

    wait_rows(2)
    place(coarse_out, 0, coarse_sums())
    coarse_store.start()

    for which in range(3):
        all_rows(which).wait_send()

    @pl.when(paced)
    def _():
        for k in range(2):
            pair_copy(k).wait_send()

            @pl.when(row != first_owner + k)
            def _(k=k):
                sum_copy(k, row, first_owner + k).wait_send()

    @pl.when(direct)
    def _():
        @pl.when(keeper)
        def _():
            block = parts.at[pl.ds(0, KEEPERS - 1)]
            put(block, block, load_sem.at[3], straight_recv.at[0], s, partner).wait_send()

        @pl.when(jnp.logical_not(keeper))
        def _():
            put(parts, parts, load_sem.at[3], straight_recv.at[0], s, partner).wait_send()

    on_left(wait_send, pre_left, x_left)
    on_right(wait_send, pre_right, x_right)

    @pl.when(s > 0)
    def _():
        on_left(wait_send, outgoing[1], outgoing[3])
        on_right(wait_send, outgoing[2], outgoing[4])
        wait_send(outgoing[0])
        wait_send(outgoing[5])

    @pl.when(paced)
    def _():
        for k in range(2):
            @pl.when(row != first_owner + k)
            def _(k=k):
                hand_copy(2 * half + k, row).wait_recv()
                pass_copy(k, 2 * half + k).start()

        for k in range(2):
            pass_copy(k, 2 * other + k).wait_recv()

    for j in range(KEEPERS):
        @pl.when(direct & (v != first_keeper + j))
        def _(j=j):
            whole_share(j).wait_recv()

        value = collected[j].astype(F32) * scales[0]
        rows = slice(j * share, (j + 1) * share)
        for k in range(TAPS):
            fine_out[k, rows, :] = value[:, k * channels:(k + 1) * channels]
        fine_store(rows).start()

    @pl.when(paced)
    def _():
        for k in range(2):
            pass_copy(k, 2 * half + k).wait_send()

            @pl.when(row == first_owner + k)
            def _(k=k):
                other_rows(lambda u: hand_copy(2 * half + k, u).wait_send())

    @pl.when(keeper & direct)
    def _():
        others(lambda u: whole_share(mine).wait_send())

    grad_store.wait()
    coarse_store.wait()
    pltpu.make_async_copy(fine_out, fine_o, load_sem.at[2]).wait()


def finish(grad, fine, coarse, grad_out, fine_out, coarse_out, sem):
    copies = [
        pltpu.make_async_copy(src, dst, sem.at[index])
        for index, (src, dst) in enumerate(
            ((fine, fine_out), (coarse, coarse_out), (grad, grad_out))
        )
    ]
    for copy in copies:
        copy.start()
    for copy in copies:
        copy.wait()


def on_device(
    cotangent, labels, class_weight, inputs, fine_pre, pooled, coarse_pre,
    fine_filters, coarse_filters,
):
    segments = lax.axis_size("segment")
    n = lax.axis_size("vol")
    channels, depth, plane = inputs.shape[1:]
    own = depth * plane
    cw = plane // 4
    cdepth = depth // 2
    slab = cdepth * cw
    reach = cdepth + 4
    row_len = pooled.shape[2] * pooled.shape[3]
    cells = own * n
    scales = (1.0 / math.sqrt(cells), 1.0 / math.sqrt(cells // 8))
    sizes = (segments, n, channels, depth, plane)
    group = min(GROUP_LANES, n * slab)
    groups = n * slab // group
    share = (channels // KEEPERS, -(-TAPS * channels // 128) * 128)
    pick_shape = (n * 64, reach * cw)
    compact_shape = (channels // 2, 128)
    if math.prod(pick_shape) * 2 > PICK_BYTES or reach * HX > 64:
        pick_shape = (1, 128)
        compact_shape = (channels, row_len)
    spaces = pl.BlockSpec(memory_space=pl.ANY)
    limit = min(60 * MIB, 16 * MIB + 6 * 2 * 9 * channels * (own + 2 * plane))
    hbm = pl.BlockSpec(memory_space=pltpu.HBM)
    dma = pltpu.SemaphoreType.DMA
    tap_shape = jax.ShapeDtypeStruct((TAPS, channels, channels), F32)
    grad_shape = jax.ShapeDtypeStruct((channels, depth, plane), BF)
    outs = pl.pallas_call(
        functools.partial(kernel, sizes, scales),
        out_shape=(grad_shape, tap_shape, tap_shape),
        in_specs=[hbm] * 9,
        out_specs=(spaces, spaces, spaces),
        scratch_shapes=[
            pltpu.VMEM((channels, depth, plane), BF),
            pltpu.VMEM((TAPS, channels, channels), F32),
            pltpu.VMEM((TAPS, channels, channels), F32),
            pltpu.SMEM(class_weight.shape, F32),
            pltpu.VMEM(cotangent.shape, BF),
            pltpu.VMEM(labels.shape, jnp.int32),
            pltpu.VMEM((channels, depth, plane), BF),
            pltpu.VMEM((channels, depth, plane), BF),
            pltpu.VMEM((2, TAPS, channels, channels), BF),
            pltpu.VMEM((depth, channels, plane), BF),
            pltpu.VMEM((depth, channels, plane), BF),
            pltpu.VMEM((3 * channels, 9 * channels), BF),
            pltpu.VMEM((3 * channels, 9 * channels), BF),
            pltpu.VMEM((channels, row_len), BF),
            pltpu.VMEM((n, channels // 2, 128), BF),
            pltpu.VMEM((n, *compact_shape), BF),
            pltpu.VMEM((n, channels, row_len), BF),
            pltpu.VMEM((depth + 2, channels, plane), BF),
            pltpu.VMEM((depth + 2, channels, plane), BF),
            pltpu.VMEM((depth + 2, channels, plane), BF),
            pltpu.VMEM((3, channels, slab), BF),
            pltpu.VMEM((2, channels, slab), BF),
            pltpu.VMEM((channels, reach * cw), BF),
            pltpu.VMEM(pick_shape, BF),
            pltpu.VMEM((own, slab), BF),
            pltpu.VMEM(((cdepth + 2) * cw, (cdepth + 2) * plane), BF),
            pltpu.VMEM((9 * channels, own), BF),
            pltpu.VMEM((groups, channels, group), BF),
            pltpu.VMEM((9 * channels, own + 2 * plane), BF),
            pltpu.VMEM((9 * channels, reach * cw), BF),
            pltpu.VMEM((9 * channels, group), BF),
            pltpu.VMEM((n, channels, slab), BF),
            pltpu.VMEM((KEEPERS, *share), BF),
            pltpu.VMEM((n, *share), BF),
            pltpu.VMEM((2, *share), BF),
            pltpu.VMEM((2, *share), BF),
            pltpu.VMEM((n // 2, *share), BF),
            pltpu.VMEM((KEEPERS, *share), BF),
            dma((8,)), dma((3,)), dma((3,)), dma((4,)), dma((4,)), dma((6,)), dma((6,)),
            dma((2,)), dma((2,)), dma((1,)), dma((KEEPERS,)), dma((PARTS,)),
            pltpu.SemaphoreType.REGULAR,
        ],
        compiler_params=pltpu.CompilerParams(
            collective_id=0, has_side_effects=True, vmem_limit_bytes=limit
        ),
    )(
        *(
            pltpu.with_memory_space_constraint(array, pltpu.HBM)
            for array in (
                class_weight,
                cotangent,
                labels,
                inputs[0],
                fine_pre[0],
                coarse_pre[0].reshape(channels, row_len),
                pooled[0].reshape(channels, row_len),
                fine_filters[0],
                coarse_filters[0],
            )
        )
    )

    grad, fine_grads, coarse_grads = pl.pallas_call(
        finish,
        out_shape=(grad_shape, tap_shape, tap_shape),
        in_specs=[spaces] * 3,
        out_specs=[hbm] * 3,
        scratch_shapes=[dma((3,))],
        compiler_params=pltpu.CompilerParams(vmem_limit_bytes=1024 * 1024),
    )(*outs)
    return (grad[None], fine_grads[None], coarse_grads[None])


def solution(mesh):
    return jax.shard_map(
        on_device,
        mesh=mesh,
        in_specs=(
            P(None, "vol", None),
            P("vol", None),
            P(),
            P("segment", None, "vol", None),
            P("segment", None, "vol", None),
            P("segment", None, "vol", None),
            P("segment", None, "vol", None),
            P("segment", None, None, None),
            P("segment", None, None, None),
        ),
        out_specs=(
            P("segment", None, "vol", None),
            P("segment", None, None, None),
            P("segment", None, None, None),
        ),
        check_vma=False,
    )
```

```python
import functools
import math

import jax
import jax.numpy as jnp
from jax import lax
from jax.experimental import pallas as pl
from jax.experimental.pallas import tpu as pltpu
from jax.sharding import PartitionSpec as P

XL = 16
HX = XL // 2
TAPS = 27
KEEPERS = 4
PARTS = 3
GROUP_LANES = 1024
MIB = 1024 * 1024
PICK_BYTES = 4 * MIB
BF = jnp.bfloat16
F32 = jnp.float32


def iota(shape, dim):
    return lax.broadcasted_iota(jnp.int32, shape, dim)


def matmul(a, b):
    return lax.dot_general(a, b, (((1,), (0,)), ((), ())), preferred_element_type=F32)


def matmul_nt(a, b):
    return lax.dot_general(a, b, (((1,), (1,)), ((), ())), preferred_element_type=F32)


def tap_mask(lanes, plane, columns, row_step, col_step):
    lane = iota((1, lanes), 1)
    column = lax.rem(lane, columns) - col_step
    row = lax.div(lax.rem(lane, plane), columns) - row_step
    rows = plane // columns
    inside = (column >= 0) & (column < columns) & (row >= 0) & (row < rows)
    return jnp.where(inside, 1.0, 0.0).astype(BF)


def rolled(value, shift):
    size = value.shape[1]
    shift = shift % size
    return value if shift == 0 else pltpu.roll(value, shift, 1)


STEPS = [(r, c) for r in (-1, 0, 1) for c in (-1, 0, 1)]


def kernel(
    sizes, scales,
    class_weight_h, cotangent_h, labels_h, saved_h, fine_pre_h, coarse_pre_h, pooled_h,
    fine_w_h, coarse_w_h,
    grad_o, fine_o, coarse_o,
    grad_out, fine_out, coarse_out, class_weight, cotangent, labels, saved, fine_pre, weights,
    out, seed, fine_cat, coarse_cat, own_rows, to_send, pre_rows, pool_rows, pre_ext, x_ext, grad_ext, pool_ext,
    pool_out, coarse_gate, pick, pool_matrix, up_matrix, fine_x, pool_all, fine_cols, coarse_cols,
    full_cols, gz_all, parts, landed, paired, middle, arrived, collected,
    load_sem, row_send, row_recv, halo_send, halo_recv, step_send, step_recv,
    pair_recv, sum_send, sum_recv, all_recv,
    straight_recv, go,
):
    segments, n, channels, depth, plane = sizes
    cw = plane // 4
    cdepth = depth // 2
    own = depth * plane
    slab = cdepth * cw
    row_len = coarse_pre_h.shape[1]
    groups = pool_all.shape[0]
    group = pool_all.shape[2]
    s = lax.axis_index("segment")
    v = lax.axis_index("vol")
    has_left, has_right = v > 0, v < n - 1
    last = s == segments - 1
    late = s >= segments - 2
    paced = (lax.rem(s, 2) == 1) & (s < segments - 1)
    direct = jnp.logical_not(paced)
    half = lax.rem(v, 2)
    other = 1 - half
    partner = v + 1 - 2 * half
    row = lax.div(v, 2)
    columns = n // 2
    first_owner = columns // 2 - 1
    share = channels // KEEPERS
    tiles = parts.shape[2] // 128
    cuts = [128 * (tiles * part // PARTS) for part in range(PARTS + 1)]
    first_keeper = n // 2 - KEEPERS // 2
    mine = v - first_keeper
    keeper = (mine >= 0) & (mine < KEEPERS)

    def put(src, dst, send, recv, segment, vol):
        return pltpu.make_async_remote_copy(
            src_ref=src, dst_ref=dst, send_sem=send, recv_sem=recv,
            device_id=(segment, vol), device_id_type=pl.DeviceIdType.MESH,
        )

    def credit(segment):
        pl.semaphore_signal(
            go, inc=1, device_id=(segment, v), device_id_type=pl.DeviceIdType.MESH
        )

    barrier = pltpu.get_barrier_semaphore()

    def greet(off, carry):
        pl.semaphore_signal(
            barrier, inc=1, device_id=(s, lax.rem(v + off, n)),
            device_id_type=pl.DeviceIdType.MESH,
        )
        return carry

    lax.fori_loop(1, n, greet, 0)
    for up in (-1, 1):
        for side in (-1, 0, 1):
            there = (s + up >= 0) & (s + up < segments) & (v + side >= 0) & (v + side < n)

            @pl.when(there)
            def _(up=up, side=side):
                pl.semaphore_signal(
                    barrier, inc=1, device_id=(s + up, v + side),
                    device_id_type=pl.DeviceIdType.MESH,
                )

    def load(src, dst, index):
        return pltpu.make_async_copy(src, dst, load_sem.at[index])

    compact = pick.shape[0] > 1
    rows_load = load(coarse_pre_h, own_rows if compact else pre_rows.at[v], 0)
    pre_load = load(fine_pre_h, fine_pre, 1)
    seed_loads = (
        load(class_weight_h, class_weight, 2),
        load(cotangent_h, cotangent, 3),
        load(labels_h, labels, 4),
    )
    coarse_w_load = load(coarse_w_h, weights.at[0], 5)
    fine_w_load = load(fine_w_h, weights.at[1], 5)
    both_w_load = load(weights, weights, 5)
    saved_load = load(saved_h, saved, 6)
    pooled_load = load(pooled_h, pool_rows.at[v], 7)

    rows_load.start()

    @pl.when(last)
    def _():
        for copy in seed_loads:
            copy.start()

    for copy in (pre_load, coarse_w_load, fine_w_load, saved_load, pooled_load):
        copy.start()

    reach = cdepth + 4
    reach_lane = iota((1, reach * cw), 1)
    reach_depth = v * cdepth - 2 + lax.div(reach_lane, cw)
    reach_cell = reach_depth * HX + lax.rem(reach_lane, HX)
    reach_cell = jnp.where(
        (reach_depth >= 0) & (reach_depth < n * cdepth), reach_cell, -1
    )
    reach_inline = lax.div(lax.rem(reach_lane, cw), HX)

    def picked(rows, u, cell, inline, lanes):
        chosen = iota((row_len, lanes), 0) == jnp.where(inline == u, cell, -1)
        return matmul(rows[u], jnp.where(chosen, 1.0, 0.0).astype(BF))

    small = channels // 2
    if compact:
        to_lane = iota((1, n * 128), 1)
        to_cell = lax.rem(to_lane, 128 // 2)
        to_depth = lax.div(to_lane, 128) * cdepth - 2 + lax.div(to_cell, HX)
        to_row = (
            lax.div(lax.rem(to_lane, 128), 128 // 2) * row_len
            + to_depth * HX + lax.rem(to_cell, HX)
        )
        inside = (to_depth >= 0) & (to_depth < n * cdepth) & (to_cell < reach * HX)
        to_row = jnp.where(inside, to_row, -1)
        split = jnp.where(iota((2 * row_len, n * 128), 0) == to_row, 1.0, 0.0).astype(BF)

    def step_copies(src, turn, segment):
        def step(which, a, b, vol):
            return put(a, b, step_send.at[which], step_recv.at[which], segment, vol)

        block = pool_out.at[turn]
        return (
            step(0, block, pool_ext.at[1], v),
            step(1, block, pool_ext.at[2], v - 1),
            step(2, block, pool_ext.at[0], v + 1),
            step(3, src.at[0], grad_ext.at[depth + 1], v - 1),
            step(4, src.at[depth - 1], grad_ext.at[0], v + 1),
            step(5, src, grad_ext.at[1:depth + 1], v),
            step(5, src.at[0], grad_ext.at[1], v),
            step(5, src.at[1:depth], grad_ext.at[2:depth + 1], v),
        )

    def on_left(act, *copies):
        @pl.when(has_left)
        def _():
            for copy in copies:
                act(copy)

    def on_right(act, *copies):
        @pl.when(has_right)
        def _():
            for copy in copies:
                act(copy)

    def start(copy):
        copy.start()

    def wait_send(copy):
        copy.wait_send()

    def wait_recv(copy):
        copy.wait_recv()

    def pool_of(ref):
        flat = jnp.concatenate([ref[p] for p in range(depth)], axis=1)
        return matmul(flat, pool_matrix[...]).astype(BF)

    def prepare():
        fine_lane = iota((own, 1), 0)
        pool_target = (
            lax.div(fine_lane, 2 * plane) * cw
            + lax.div(lax.rem(fine_lane, plane), 2 * XL) * HX
            + lax.div(lax.rem(fine_lane, XL), 2)
        )
        pool_matrix[...] = jnp.where(iota((own, slab), 1) == pool_target, 1.0, 0.0).astype(BF)

        @pl.when(last)
        def _():
            for copy in seed_loads:
                copy.wait()
            planes = jnp.swapaxes(cotangent[...], 0, 1)
            for p in range(depth):
                label = labels[p:p + 1, :]
                weight = jnp.zeros(label.shape, F32)
                for index in range(class_weight.shape[0]):
                    weight = weight + jnp.where(label == index, class_weight[index], 0.0)
                block = (planes[p].astype(F32) * weight).astype(BF)
                seed[p] = block
                grad_ext[p + 1] = block
            pool_out[0] = pool_of(seed)
            pool_ext[1] = pool_out[0]

        pre_load.wait()
        pre_ext[1:depth + 1] = jnp.swapaxes(fine_pre[...], 0, 1)
        both_w_load.wait()
        for k in range(TAPS):
            rows = slice(k // 9 * channels, (k // 9 + 1) * channels)
            lanes = slice(k % 9 * channels, (k % 9 + 1) * channels)
            coarse_cat[rows, lanes] = weights[0, k]
            fine_cat[rows, lanes] = weights[1, k]
        saved_load.wait()
        x_ext[1:depth + 1] = jnp.swapaxes(saved[...], 0, 1)

        @pl.when(v == 0)
        def _():
            pre_ext[0] = jnp.zeros((channels, plane), BF)
            x_ext[0] = jnp.zeros((channels, plane), BF)
            grad_ext[0] = jnp.zeros((channels, plane), BF)
            pool_ext[0] = jnp.zeros(pool_ext.shape[1:], BF)

        @pl.when(v == n - 1)
        def _():
            pre_ext[depth + 1] = jnp.zeros((channels, plane), BF)
            x_ext[depth + 1] = jnp.zeros((channels, plane), BF)
            grad_ext[depth + 1] = jnp.zeros((channels, plane), BF)
            pool_ext[2] = jnp.zeros(pool_ext.shape[1:], BF)

        pooled_load.wait()

    pl.when(v < n // 2)(prepare)

    rows_load.wait()
    if compact:
        halves = jnp.concatenate([own_rows[:small, :], own_rows[small:, :]], axis=1)
        blocks = matmul(halves, split).astype(BF)
        for u in range(n):
            to_send[u] = blocks[:, u * 128:(u + 1) * 128]
        pre_rows[v] = to_send[v]

    ups = jnp.where(s > 0, 1, 0) + jnp.where(last, 0, 1)
    sides = 1 + jnp.where(has_left, 1, 0) + jnp.where(has_right, 1, 0)
    pl.semaphore_wait(barrier, n - 1 + ups * sides)

    def halo(ref, index):
        return (
            put(ref.at[1], ref.at[depth + 1], halo_send.at[index], halo_recv.at[index], s, v - 1),
            put(
                ref.at[depth], ref.at[0],
                halo_send.at[index + 1], halo_recv.at[index + 1], s, v + 1,
            ),
        )

    pre_left, pre_right = halo(pre_ext, 0)
    x_left, x_right = halo(x_ext, 2)

    def far_first(act):
        def body(step, carry):
            for u in (v + n - step, v - n + step):
                @pl.when((u >= 0) & (u < n))
                def _(u=u):
                    act(u)

            return carry

        lax.fori_loop(1, n, body, 0)

    def in_order(act):
        def body(u, carry):
            @pl.when(u != v)
            def _():
                act(u)

            return carry

        lax.fori_loop(0, n, body, 0)

    def others(act):
        def body(off, carry):
            act(lax.rem(v + off, n))
            return carry

        lax.fori_loop(1, n, body, 0)

    def row_copy(which, source, target):
        ref = (pre_rows, pool_rows, gz_all)[which]
        compacted = compact and which == 0
        return put(
            to_send.at[target] if compacted else ref.at[source], ref.at[source],
            row_send.at[which], row_recv.at[which], s, target,
        )

    def all_rows(which):
        ref = (pre_rows, pool_rows, gz_all)[which].at[pl.ds(0, n - 1)]
        return put(ref, ref, row_send.at[which], row_recv.at[which], s, partner)

    def send_rows(which):
        far_first(lambda u: row_copy(which, v, u).start())

    def gz_copy(source, recv, target):
        block = gz_all.at[source]
        return put(block, block, row_send.at[2], row_recv.at[recv], s, target)

    def send_gz():
        @pl.when(direct)
        def _():
            for off in range(1, n):
                gz_copy(v, 2, lax.rem(v + off, n)).start()

        @pl.when(paced)
        def _():
            for off in range(1, columns):
                gz_copy(v, 2, 2 * lax.rem(row + off, columns) + half).start()
            gz_copy(v, 3, partner).start()

    def pass_gz():
        block = gz_all.at[pl.ds(0, columns - 1)]
        put(block, block, row_send.at[2], row_recv.at[2], s, partner).wait_recv()
        for off in range(1, columns):
            gz_copy(2 * lax.rem(row + off, columns) + half, 3, partner).start()

    def wait_gz():
        @pl.when(direct)
        def _():
            all_rows(2).wait_recv()

        @pl.when(paced)
        def _():
            block = gz_all.at[pl.ds(0, columns)]
            put(block, block, row_send.at[2], row_recv.at[3], s, partner).wait_recv()

    def wait_rows(which):
        all_rows(which).wait_recv()

    @pl.when(last)
    def _():
        send_rows(0)

    pl.when(v >= n // 2)(prepare)

    @pl.when(last)
    def _():
        copies = step_copies(seed, 0, s)
        on_left(start, copies[1])
        on_right(start, copies[2])
        on_left(start, copies[3], pre_left)
        on_right(start, copies[4], pre_right)

    @pl.when(jnp.logical_not(last))
    def _():
        @pl.when(s == segments - 2)
        def _():
            pl.semaphore_wait(go, 1)

        send_rows(0)
        on_left(start, pre_left)
        on_right(start, pre_right)

    @pl.when(jnp.logical_not(late))
    def _():
        on_left(start, x_left)
        on_right(start, x_right)

    up_wide = (cdepth + 2) * plane
    up_lane = iota((1, up_wide), 1)
    up_target = (
        lax.div(up_lane, plane) * cw
        + lax.div(lax.rem(up_lane, plane), 2 * XL) * HX
        + lax.div(lax.rem(up_lane, XL), 2)
    )
    up_matrix[...] = jnp.where(
        iota(((cdepth + 2) * cw, up_wide), 0) == up_target, 0.125, 0.0
    ).astype(BF)

    if compact:
        from_row = iota((128 // 2, reach * cw), 0)
        to_lane = iota((1, reach * cw), 1)
        wanted = lax.div(to_lane, cw) * HX + lax.rem(to_lane, HX)
        to_inline = lax.div(lax.rem(to_lane, cw), HX)
        for u in range(n):
            chosen = from_row == jnp.where(to_inline == u, wanted, -1)
            pick[u * 64:(u + 1) * 64, :] = jnp.where(chosen, 1.0, 0.0).astype(BF)

    wait_rows(0)

    @pl.when(last)
    def _():
        credit(s - 1)

    if compact:
        arrivals = [pre_rows[u] for u in range(n)]
        flat_rows = jnp.concatenate(
            [
                jnp.concatenate([rows[:, 64 * h:64 * (h + 1)] for rows in arrivals], axis=1)
                for h in range(2)
            ],
            axis=0,
        )
        coarse_gate[...] = matmul(flat_rows, pick[...]).astype(BF)
    else:
        coarse_gate[...] = lax.fori_loop(
            0, n,
            lambda u, total: total + picked(
                pre_rows, u, reach_cell, reach_inline, reach * cw
            ),
            jnp.zeros((channels, reach * cw), F32),
        ).astype(BF)

    def take_pooled():
        wait_rows(1)
        lane = iota((1, group), 1)
        inline = lax.div(lax.rem(lane, cw), HX)

        def body(g, carry):
            cell = (g * (group // cw) + lax.div(lane, cw)) * HX + lax.rem(lane, HX)
            pool_all[g] = lax.fori_loop(
                0, n,
                lambda u, total: total + picked(pool_rows, u, cell, inline, group),
                jnp.zeros((channels, group), F32),
            ).astype(BF)
            return carry

        lax.fori_loop(0, groups, body, 0)

    def take_fine_x():
        for block in range(9):
            outer, row_step = block // 3, 1 - block % 3
            mask = tap_mask(plane, plane, XL, row_step, 0)
            for p in range(depth):
                fine_x[block * channels:(block + 1) * channels, p * plane:(p + 1) * plane] = (
                    rolled(x_ext[p + outer], row_step * XL) * mask
                )

    @pl.when(jnp.logical_not(late))
    def _():
        send_rows(1)
        take_pooled()

    @pl.when(jnp.logical_not(late))
    def _():
        on_left(wait_recv, x_right)
        on_right(wait_recv, x_left)
        take_fine_x()

    incoming = step_copies(out, 1, s)

    on_left(wait_recv, incoming[2])
    on_right(wait_recv, incoming[1])

    @pl.when(jnp.logical_not(last))
    def _():
        incoming[0].wait_recv()

    @pl.when(s == segments - 2)
    def _():
        credit(s + 1)

    side = pool_ext.shape[2]
    near = jnp.concatenate(
        [pool_ext[0][:, side - 2 * cw:], pool_ext[1], pool_ext[2][:, :2 * cw]], axis=1
    )
    coarse_gz = jnp.where(coarse_gate[...] > 0, near, jnp.zeros_like(near))
    gz_all[v] = coarse_gz[:, 2 * cw:2 * cw + slab]
    for r, (row_step, col_step) in enumerate(STEPS):
        mask = tap_mask(reach * cw, cw, HX, row_step, col_step)
        coarse_cols[r * channels:(r + 1) * channels, :] = (
            rolled(coarse_gz, row_step * HX + col_step) * mask
        )

    terms = matmul(coarse_cat[...], coarse_cols[...])
    width = (cdepth + 2) * cw
    coarse_back = sum(
        terms[outer * channels:(outer + 1) * channels, (2 - outer) * cw:(2 - outer) * cw + width]
        for outer in range(3)
    ).astype(BF)

    spread = matmul(coarse_back, up_matrix[...])
    pieces = [
        spread[:, (p + 1) // 2 * plane:((p + 1) // 2 + 1) * plane] for p in range(depth + 2)
    ]

    on_left(wait_recv, pre_right, incoming[4])
    on_right(wait_recv, pre_left, incoming[3])

    @pl.when(jnp.logical_not(last))
    def _():
        incoming[5].wait_recv()

    @pl.when(jnp.logical_not(late) & (s > 0))
    def _():
        send_gz()

    def take_cols(planes, first, count):
        for p in planes:
            grad = grad_ext[p].astype(F32) + pieces[p]
            gz = jnp.where(pre_ext[p].astype(F32) > 0, grad, 0.0).astype(BF)
            for r in range(first, first + count):
                row_step, col_step = STEPS[r]
                mask = tap_mask(plane, plane, XL, row_step, col_step)
                fine_cols[r * channels:(r + 1) * channels, p * plane:(p + 1) * plane] = (
                    rolled(gz, row_step * XL + col_step) * mask
                )

    def take_out():
        terms = matmul(fine_cat[...], fine_cols[...])
        for p in range(depth):
            total = grad_ext[p + 1].astype(F32)
            for outer in range(3):
                total = total + terms[
                    outer * channels:(outer + 1) * channels,
                    (p + 2 - outer) * plane:(p + 3 - outer) * plane,
                ]
            out[p] = total.astype(BF)

    def pair_copy(k):
        return put(
            parts.at[2 * other + k], paired.at[k], load_sem.at[3 + k], pair_recv.at[k], s, partner
        )

    def sum_copy(k, row_from, row_to):
        return put(
            middle.at[k], arrived.at[row_from],
            sum_send.at[k], sum_recv.at[0], s, 2 * row_to + half,
        )

    def fine_sums():
        gz = fine_cols[3 * channels:6 * channels, plane:plane + own]
        grads = matmul_nt(fine_x[...], gz)
        blocks = [grads[block * channels:(block + 1) * channels, :] for block in range(9)]
        rest = parts.shape[2] - TAPS * channels
        if rest:
            blocks.append(jnp.zeros((channels, rest), F32))
        flat = jnp.concatenate(blocks, axis=1).astype(BF)
        for j in range(KEEPERS):
            parts[j] = flat[j * share:(j + 1) * share, :]

    def pair_sends():
        for k in range(2):
            pair_copy(k).start()

    def lanes_of(part):
        return slice(cuts[part], cuts[part + 1])

    def straight_copy(j, part, vol_to):
        return put(
            parts.at[j, :, lanes_of(part)], landed.at[v, :, lanes_of(part)],
            load_sem.at[3], straight_recv.at[part], s, vol_to,
        )

    def straight_landed(part):
        block = landed.at[pl.ds(0, n - 1), :, lanes_of(part)]
        return put(block, block, load_sem.at[3], straight_recv.at[part], s, partner)

    def straight_sums():
        fine_sums()

        def send(order):
            for part in range(PARTS):
                for j in order:
                    @pl.when(v != first_keeper + j)
                    def _(j=j, part=part):
                        straight_copy(j, part, first_keeper + j).start()

        @pl.when(v < n // 2)
        def _():
            send(range(KEEPERS - 1, -1, -1))

        @pl.when(v >= n // 2)
        def _():
            send(range(KEEPERS))

        @pl.when((mine >= 0) & (mine < KEEPERS))
        def _():
            landed[v] = parts[mine]

    def column_sums():
        for k in range(2):
            pair_copy(k).wait_recv()
            both = parts[2 * half + k].astype(F32) + paired[k].astype(F32)
            middle[k] = both.astype(BF)

            @pl.when(row != first_owner + k)
            def _(k=k):
                sum_copy(k, row, first_owner + k).start()

            @pl.when(row == first_owner + k)
            def _(k=k):
                arrived[row] = middle[k]

    @pl.when(s == 0)
    def _():
        inner = range(1, depth + 1)
        take_cols(inner, 3, 3)
        straight_sums()
        send_gz()
        take_cols(inner, 0, 3)
        take_cols(inner, 6, 3)
        take_cols((0, depth + 1), 0, 9)
        take_out()

    outgoing = step_copies(out, 1, s - 1)

    @pl.when(last)
    def _():
        copies = step_copies(seed, 0, s)
        on_left(wait_send, copies[1], copies[3])
        on_right(wait_send, copies[2], copies[4])

    @pl.when(s > 0)
    def _():
        take_cols(range(depth + 2), 0, 9)
        take_out()
        outgoing[6].start()
        pool_out[1] = pool_of(out)
        on_left(start, outgoing[1])
        on_right(start, outgoing[2])
        outgoing[0].start()
        on_left(start, outgoing[3])
        on_right(start, outgoing[4])
        outgoing[7].start()

    @pl.when(last)
    def _():
        pl.semaphore_wait(go, 1)

    @pl.when(late)
    def _():
        on_left(start, x_left)
        on_right(start, x_right)
        send_rows(1)

    @pl.when(late)
    def _():
        take_pooled()
        on_left(wait_recv, x_right)
        on_right(wait_recv, x_left)
        take_fine_x()

    @pl.when(late)
    def _():
        send_gz()

    @pl.when(s > 0)
    def _():
        @pl.when(paced)
        def _():
            fine_sums()
            pair_sends()

        @pl.when(direct)
        def _():
            straight_sums()

    grad_store = pltpu.make_async_copy(grad_out, grad_o, load_sem.at[0])
    coarse_store = pltpu.make_async_copy(coarse_out, coarse_o, load_sem.at[1])

    def fine_store(rows):
        return pltpu.make_async_copy(
            fine_out.at[:, rows], fine_o.at[:, rows], load_sem.at[2]
        )

    grad_out[...] = jnp.swapaxes(out[...], 0, 1)
    grad_store.start()

    def coarse_sums():
        total = jnp.zeros((3 * channels, 9 * channels), F32)
        edge = jnp.zeros((channels, cw), BF)
        for g in range(groups):
            xs = jnp.concatenate(
                [
                    pool_all[g - 1][:, group - cw:] if g else edge,
                    pool_all[g],
                    pool_all[g + 1][:, :cw] if g < groups - 1 else edge,
                ],
                axis=1,
            )
            tall = jnp.concatenate([xs[:, o * cw:o * cw + group] for o in range(3)], axis=0)
            slabs = group // slab
            flat = jnp.concatenate([gz_all[g * slabs + u] for u in range(slabs)], axis=1)
            for r, (row_step, col_step) in enumerate(STEPS):
                mask = tap_mask(group, cw, HX, row_step, col_step)
                full_cols[r * channels:(r + 1) * channels, :] = (
                    rolled(flat, row_step * HX + col_step) * mask
                )
            total = total + matmul_nt(tall, full_cols[...])
        return total * scales[1]

    def place(ref, first_row, value):
        rows = value.shape[0]
        at = first_row
        while at < first_row + rows:
            outer, inner = divmod(at, channels)
            count = min(channels - inner, first_row + rows - at)
            for r in range(9):
                ref[outer * 9 + r, inner:inner + count, :] = value[
                    at - first_row:at - first_row + count, r * channels:(r + 1) * channels
                ]
            at += count

    @pl.when(paced)
    def _():
        pass_gz()
        column_sums()

    def hand_copy(piece, row_to):
        return put(
            collected.at[piece], collected.at[piece],
            load_sem.at[5], all_recv.at[piece], s, 2 * row_to + half,
        )

    def pass_copy(k, piece):
        return put(
            collected.at[piece], collected.at[piece],
            load_sem.at[6 + k], all_recv.at[piece], s, partner,
        )

    def other_rows(act):
        def body(off, carry):
            act(lax.rem(row + off, columns))
            return carry

        lax.fori_loop(1, columns, body, 0)

    sums_arrived = put(
        arrived.at[pl.ds(0, columns - 1)], arrived.at[pl.ds(0, columns - 1)],
        sum_send.at[0], sum_recv.at[0], s, partner,
    )

    for k in range(2):
        @pl.when((row == first_owner + k) & paced)
        def _(k=k):
            piece = 2 * half + k
            sums_arrived.wait_recv()
            whole = arrived[0].astype(F32)
            for u in range(1, columns):
                whole = whole + arrived[u].astype(F32)
            collected[piece] = whole.astype(BF)
            other_rows(lambda u: hand_copy(piece, u).start())
            pass_copy(k, piece).start()

    def spread_copy(j, part, vol_to):
        block = collected.at[j, :, lanes_of(part)]
        return put(block, block, load_sem.at[5], all_recv.at[j], s, vol_to)

    def whole_share(j):
        return put(
            collected.at[j], collected.at[j], load_sem.at[5], all_recv.at[j], s, partner
        )

    @pl.when(keeper & direct)
    def _():
        for part in range(PARTS):
            straight_landed(part).wait_recv()
            at = lanes_of(part)
            whole = landed[0, :, at].astype(F32)
            for u in range(1, n):
                whole = whole + landed[u, :, at].astype(F32)
            collected[mine, :, at] = whole.astype(BF)
            in_order(lambda u, part=part: spread_copy(mine, part, u).start())

    wait_gz()
    place(coarse_out, 0, coarse_sums())
    coarse_store.start()

    for which in range(3):
        all_rows(which).wait_send()

    @pl.when(paced)
    def _():
        for k in range(2):
            pair_copy(k).wait_send()

            @pl.when(row != first_owner + k)
            def _(k=k):
                sum_copy(k, row, first_owner + k).wait_send()

    @pl.when(direct)
    def _():
        @pl.when(keeper)
        def _():
            block = parts.at[pl.ds(0, KEEPERS - 1)]
            put(block, block, load_sem.at[3], straight_recv.at[0], s, partner).wait_send()

        @pl.when(jnp.logical_not(keeper))
        def _():
            put(parts, parts, load_sem.at[3], straight_recv.at[0], s, partner).wait_send()

    on_left(wait_send, pre_left, x_left)
    on_right(wait_send, pre_right, x_right)

    @pl.when(s > 0)
    def _():
        on_left(wait_send, outgoing[1], outgoing[3])
        on_right(wait_send, outgoing[2], outgoing[4])
        wait_send(outgoing[0])
        wait_send(outgoing[5])

    @pl.when(paced)
    def _():
        for k in range(2):
            @pl.when(row != first_owner + k)
            def _(k=k):
                hand_copy(2 * half + k, row).wait_recv()
                pass_copy(k, 2 * half + k).start()

        for k in range(2):
            pass_copy(k, 2 * other + k).wait_recv()

    for j in range(KEEPERS):
        @pl.when(direct & (v != first_keeper + j))
        def _(j=j):
            whole_share(j).wait_recv()

        value = collected[j].astype(F32) * scales[0]
        rows = slice(j * share, (j + 1) * share)
        for k in range(TAPS):
            fine_out[k, rows, :] = value[:, k * channels:(k + 1) * channels]
        fine_store(rows).start()

    @pl.when(paced)
    def _():
        for k in range(2):
            pass_copy(k, 2 * half + k).wait_send()

            @pl.when(row == first_owner + k)
            def _(k=k):
                other_rows(lambda u: hand_copy(2 * half + k, u).wait_send())

    @pl.when(keeper & direct)
    def _():
        others(lambda u: whole_share(mine).wait_send())

    grad_store.wait()
    coarse_store.wait()
    pltpu.make_async_copy(fine_out, fine_o, load_sem.at[2]).wait()


def finish(grad, fine, coarse, grad_out, fine_out, coarse_out, sem):
    copies = [
        pltpu.make_async_copy(src, dst, sem.at[index])
        for index, (src, dst) in enumerate(
            ((fine, fine_out), (coarse, coarse_out), (grad, grad_out))
        )
    ]
    for copy in copies:
        copy.start()
    for copy in copies:
        copy.wait()


def on_device(
    cotangent, labels, class_weight, inputs, fine_pre, pooled, coarse_pre,
    fine_filters, coarse_filters,
):
    segments = lax.axis_size("segment")
    n = lax.axis_size("vol")
    channels, depth, plane = inputs.shape[1:]
    own = depth * plane
    cw = plane // 4
    cdepth = depth // 2
    slab = cdepth * cw
    reach = cdepth + 4
    row_len = pooled.shape[2] * pooled.shape[3]
    cells = own * n
    scales = (1.0 / math.sqrt(cells), 1.0 / math.sqrt(cells // 8))
    sizes = (segments, n, channels, depth, plane)
    group = min(GROUP_LANES, n * slab)
    groups = n * slab // group
    share = (channels // KEEPERS, -(-TAPS * channels // 128) * 128)
    pick_shape = (n * 64, reach * cw)
    compact_shape = (channels // 2, 128)
    if math.prod(pick_shape) * 2 > PICK_BYTES or reach * HX > 64:
        pick_shape = (1, 128)
        compact_shape = (channels, row_len)
    spaces = pl.BlockSpec(memory_space=pl.ANY)
    limit = min(60 * MIB, 16 * MIB + 6 * 2 * 9 * channels * (own + 2 * plane))
    hbm = pl.BlockSpec(memory_space=pltpu.HBM)
    dma = pltpu.SemaphoreType.DMA
    tap_shape = jax.ShapeDtypeStruct((TAPS, channels, channels), F32)
    grad_shape = jax.ShapeDtypeStruct((channels, depth, plane), BF)
    outs = pl.pallas_call(
        functools.partial(kernel, sizes, scales),
        out_shape=(grad_shape, tap_shape, tap_shape),
        in_specs=[hbm] * 9,
        out_specs=(spaces, spaces, spaces),
        scratch_shapes=[
            pltpu.VMEM((channels, depth, plane), BF),
            pltpu.VMEM((TAPS, channels, channels), F32),
            pltpu.VMEM((TAPS, channels, channels), F32),
            pltpu.SMEM(class_weight.shape, F32),
            pltpu.VMEM(cotangent.shape, BF),
            pltpu.VMEM(labels.shape, jnp.int32),
            pltpu.VMEM((channels, depth, plane), BF),
            pltpu.VMEM((channels, depth, plane), BF),
            pltpu.VMEM((2, TAPS, channels, channels), BF),
            pltpu.VMEM((depth, channels, plane), BF),
            pltpu.VMEM((depth, channels, plane), BF),
            pltpu.VMEM((3 * channels, 9 * channels), BF),
            pltpu.VMEM((3 * channels, 9 * channels), BF),
            pltpu.VMEM((channels, row_len), BF),
            pltpu.VMEM((n, channels // 2, 128), BF),
            pltpu.VMEM((n, *compact_shape), BF),
            pltpu.VMEM((n, channels, row_len), BF),
            pltpu.VMEM((depth + 2, channels, plane), BF),
            pltpu.VMEM((depth + 2, channels, plane), BF),
            pltpu.VMEM((depth + 2, channels, plane), BF),
            pltpu.VMEM((3, channels, slab), BF),
            pltpu.VMEM((2, channels, slab), BF),
            pltpu.VMEM((channels, reach * cw), BF),
            pltpu.VMEM(pick_shape, BF),
            pltpu.VMEM((own, slab), BF),
            pltpu.VMEM(((cdepth + 2) * cw, (cdepth + 2) * plane), BF),
            pltpu.VMEM((9 * channels, own), BF),
            pltpu.VMEM((groups, channels, group), BF),
            pltpu.VMEM((9 * channels, own + 2 * plane), BF),
            pltpu.VMEM((9 * channels, reach * cw), BF),
            pltpu.VMEM((9 * channels, group), BF),
            pltpu.VMEM((n, channels, slab), BF),
            pltpu.VMEM((KEEPERS, *share), BF),
            pltpu.VMEM((n, *share), BF),
            pltpu.VMEM((2, *share), BF),
            pltpu.VMEM((2, *share), BF),
            pltpu.VMEM((n // 2, *share), BF),
            pltpu.VMEM((KEEPERS, *share), BF),
            dma((8,)), dma((3,)), dma((4,)), dma((4,)), dma((4,)), dma((6,)), dma((6,)),
            dma((2,)), dma((2,)), dma((1,)), dma((KEEPERS,)), dma((PARTS,)),
            pltpu.SemaphoreType.REGULAR,
        ],
        compiler_params=pltpu.CompilerParams(
            collective_id=0, has_side_effects=True, vmem_limit_bytes=limit
        ),
    )(
        *(
            pltpu.with_memory_space_constraint(array, pltpu.HBM)
            for array in (
                class_weight,
                cotangent,
                labels,
                inputs[0],
                fine_pre[0],
                coarse_pre[0].reshape(channels, row_len),
                pooled[0].reshape(channels, row_len),
                fine_filters[0],
                coarse_filters[0],
            )
        )
    )

    grad, fine_grads, coarse_grads = pl.pallas_call(
        finish,
        out_shape=(grad_shape, tap_shape, tap_shape),
        in_specs=[spaces] * 3,
        out_specs=[hbm] * 3,
        scratch_shapes=[dma((3,))],
        compiler_params=pltpu.CompilerParams(vmem_limit_bytes=1024 * 1024),
    )(*outs)
    return (grad[None], fine_grads[None], coarse_grads[None])


def solution(mesh):
    return jax.shard_map(
        on_device,
        mesh=mesh,
        in_specs=(
            P(None, "vol", None),
            P("vol", None),
            P(),
            P("segment", None, "vol", None),
            P("segment", None, "vol", None),
            P("segment", None, "vol", None),
            P("segment", None, "vol", None),
            P("segment", None, None, None),
            P("segment", None, None, None),
        ),
        out_specs=(
            P("segment", None, "vol", None),
            P("segment", None, None, None),
            P("segment", None, None, None),
        ),
        check_vma=False,
    )
```
